32 devices in a mesh: dp: 8 (over z, x), tensor: 4 (over y, core).
Axes of the slice: x: 2, y: 2, z: 4, core: 2. Of those that a mesh axis runs over, the one named last changes fastest.
Arguments:
- inputs: bfloat16 [8192, 2048], P('dp'), may hold values from -6 to 6
- first_gain: float32 [2048], replicated, may hold values from 0.25 to 1.75
- first_bias: float32 [2048], replicated, may hold values from -1.75 to 1.75
- query_weight: bfloat16 [2048, 2048], P(None, 'tensor'), may hold values from -0.125 to 0.125
- query_bias: float32 [2048], P('tensor'), may hold values from -1.75 to 1.75
- keyval_weight: bfloat16 [2048, 256], replicated, may hold values from -0.1875 to 0.1875
- value_bias: float32 [128], replicated, may hold values from -3 to 3
- output_weight: bfloat16 [2048, 2048], P('tensor'), may hold values from -1 to 1
- output_bias: float32 [2048], replicated, may hold values from -1.75 to 1.75
- second_gain: float32 [2048], replicated, may hold values from 0.25 to 1.75
- second_bias: float32 [2048], replicated, may hold values from -1.75 to 1.75
- up_weight: bfloat16 [2048, 8192], P(None, 'tensor'), may hold values from -0.125 to 0.125
- up_bias: float32 [8192], P('tensor'), may hold values from -1.75 to 1.75
- down_weight: bfloat16 [8192, 2048], P('tensor'), may hold values from -0.09375 to 0.09375
- down_bias: float32 [2048], replicated, may hold values from -1.75 to 1.75
- cotangent: bfloat16 [8192, 2048], P('dp'), may hold values from -6 to 6
Outputs:
- layer_out: bfloat16 [8192, 2048], P('dp')
- grad_inputs: float32 [8192, 2048], P('dp')
- grad_first_gain: float32 [2048], replicated
- grad_first_bias: float32 [2048], replicated
- grad_query_weight: float32 [2048, 2048], P('dp', 'tensor')
- grad_query_bias: float32 [2048], P('tensor')
- grad_keyval_weight: float32 [2048, 256], P('dp')
- grad_value_bias: float32 [128], replicated
- grad_output_weight: float32 [2048, 2048], P('tensor', 'dp')
- grad_output_bias: float32 [2048], replicated
- grad_second_gain: float32 [2048], replicated
- grad_second_bias: float32 [2048], replicated
- grad_up_weight: float32 [2048, 8192], P('dp', 'tensor')
- grad_up_bias: float32 [8192], P('tensor')
- grad_down_weight: float32 [8192, 2048], P('tensor', 'dp')
- grad_down_bias: float32 [2048], replicated
The draws below stay inside these ranges and needn't reach their ends.
All inputs are finite; a program needn't handle non-finite values.
Results may differ from the reference program's by a relative error of at most 0.024.
Values may be sent and summed in bfloat16 or wider, within the bound.
A program may use at most 320 MiB of HBM per device.

```python
import math
import jax
import jax.numpy as jnp
from jax import lax

D = 2048
HEADS = 16
HS = 128
FF = 8192
SEQ_LEN = 8192
TOKENS = 8192
SEQS = 1


def spiked(drawn, rng, source, target, blocks, factor):
    def block_of(position):
        return (jnp.arange(drawn.shape[position]) // (drawn.shape[position] // blocks)).reshape((-1,) + (1,) * (drawn.ndim - 1 - position))

    one_side = jax.random.permutation(rng, blocks)[block_of(target)]
    other_side = (block_of(target) + blocks // 2) % blocks
    return jnp.where((block_of(source) == one_side) | (block_of(source) == other_side), factor * drawn, drawn)


def level_of(key, dims, pieces, smallest, high):
    level = 1.0
    for position, shards_of in pieces:
        draws = jax.random.uniform(jax.random.fold_in(jax.random.fold_in(key, 6), position), (shards_of,), jnp.float32, smallest / len(pieces), high / len(pieces))
        level = level * jnp.repeat(jnp.exp(draws), dims[position] // shards_of).reshape((-1,) + (1,) * (len(dims) - 1 - position))
    return level


def gaussian(key, dims, spread, limit, cuts=(), kind=jnp.bfloat16):
    values = jax.random.normal(key, dims, jnp.float32) * spread
    if len(cuts) > 0:
        values = level_of(key, dims, cuts, -0.22, 0.18) * values
    return jnp.clip(values, min=-limit, max=limit).astype(kind)


def gaussian_with(stream_key, shape, width, reach, split, heavy, held_as=jnp.bfloat16):
    entries = width * jax.random.normal(stream_key, shape, jnp.float32)
    if split:
        entries = entries * level_of(stream_key, shape, split, -0.22, 0.18)
    return jnp.clip(spiked(entries, jax.random.fold_in(stream_key, 3), *heavy), -reach, reach).astype(held_as)


def setup_inputs(seed: int = 0) -> dict:
    key_list = jax.random.split(jax.random.key(seed), 17)
    return {
        "inputs": gaussian_with(key_list[0], (TOKENS, D), 1.0, 6.0, ((0, 8),), (0, 1, 8, 2.0)),
        "first_gain": jnp.clip(1.0 + 0.15 * jax.random.normal(key_list[1], (D,), jnp.float32), 0.25, 1.75),
        "first_bias": gaussian(key_list[2], (D,), 0.3, 1.75, (), jnp.float32),
        "query_weight": gaussian(key_list[3], (D, D), D ** -0.5, 0.125, ((1, 4),)),
        "query_bias": gaussian(key_list[4], (D,), 0.3, 1.75, ((0, 4),), jnp.float32),
        "keyval_weight": gaussian(key_list[5], (D, 2 * HS), (D // 2) ** -0.5, 0.1875),
        "value_bias": gaussian(key_list[6], (HS,), 0.5, 3.0, (), jnp.float32),
        "output_weight": gaussian(key_list[7], (D, D), (D // 64) ** -0.5, 1.0, ((0, 4),)),
        "output_bias": gaussian(key_list[8], (D,), 0.3, 1.75, (), jnp.float32),
        "second_gain": jnp.clip(1.0 + 0.15 * jax.random.normal(key_list[9], (D,), jnp.float32), 0.25, 1.75),
        "second_bias": gaussian(key_list[10], (D,), 0.3, 1.75, (), jnp.float32),
        "up_weight": gaussian(key_list[11], (D, FF), D ** -0.5, 0.125, ((1, 4),)),
        "up_bias": gaussian(key_list[12], (FF,), 0.3, 1.75, ((0, 4),), jnp.float32),
        "down_weight": gaussian(key_list[13], (FF, D), (FF // 2) ** -0.5, 0.09375, ((0, 4),)),
        "down_bias": gaussian(key_list[14], (D,), 0.3, 1.75, (), jnp.float32),
        "cotangent": gaussian_with(key_list[15], (TOKENS, D), 1.0, 6.0, ((0, 8),), (0, 1, 8, 2.0)),
    }


@jax.custom_vjp
def low(v):
    return lax.optimization_barrier(v.astype(jnp.bfloat16)).astype(jnp.float32)

@jax.custom_vjp
def low_back(v):
    return v

def low_keep(v):
    return (low(v), None)

def low_pass(kept, grad):
    return (grad,)

def back_keep(v):
    return (v, None)

def back_low(kept, grad):
    return (low(grad),)
low.defvjp(low_keep, low_pass)
low_back.defvjp(back_keep, back_low)
EPSILON = 1e-05
NEG_LARGE = -1e+30
HIGHEST = lax.Precision.HIGHEST

def layer_norm(values, norm_gain, norm_bias):
    average = lax.optimization_barrier(jnp.mean(values, axis=-1, keepdims=True))
    centred = values - average
    variance = lax.optimization_barrier(jnp.mean(centred * centred, axis=-1, keepdims=True))
    return centred * lax.rsqrt(variance + EPSILON) * norm_gain + norm_bias

def gelu_tanh(values):
    return jax.nn.gelu(values, approximate=True)

def matmul_hi(left, right):
    return jnp.dot(left, right, precision=HIGHEST)

def forward(seq_rows, params):
    first_gain, first_bias, query_weight, query_bias, keyval_weight, value_bias, output_weight, output_bias, second_gain, second_bias, up_weight, up_bias, down_weight, down_bias = params
    length = seq_rows.shape[0]
    q_block = math.gcd(length, 512)
    normed1 = low(layer_norm(seq_rows, first_gain, first_bias))
    queries = low(low_back(matmul_hi(normed1, query_weight) + query_bias) * HS ** (-0.5))
    kv_bias = jnp.concatenate([jnp.zeros((HS,), jnp.float32), value_bias])
    keyval = low(low_back(matmul_hi(normed1, keyval_weight) + kv_bias))
    key_rows = keyval[:, :HS]
    value_rows = keyval[:, HS:]
    query_blocks = queries.reshape(length // q_block, q_block, HEADS, HS)
    starts = (jnp.arange(length // q_block) * q_block).astype(jnp.int32)
    columns = jnp.arange(length).astype(jnp.int32)

    def attend(packed):
        block_queries, start = packed
        scores = low_back(jnp.einsum('qhd,kd->hqk', block_queries, key_rows, precision=HIGHEST))
        positions = start + jnp.arange(q_block).astype(jnp.int32)
        allowed = columns[None, :] <= positions[:, None]
        scores = jnp.where(allowed[None], scores, NEG_LARGE)
        attn_probs = low(jax.nn.softmax(scores, axis=-1))
        return jnp.einsum('hqk,kd->qhd', attn_probs, value_rows, precision=HIGHEST)
    context = lax.map(jax.checkpoint(attend), (query_blocks, starts)).reshape(length, D)
    context = low(low_back(context))
    middle = seq_rows + low_back(matmul_hi(context, output_weight)) + output_bias
    normed2 = low(layer_norm(middle, second_gain, second_bias))
    pre_act = low_back(matmul_hi(normed2, up_weight) + up_bias)
    activ = low(gelu_tanh(pre_act))
    return middle + low_back(matmul_hi(activ, down_weight)) + down_bias

def add_pair(first, second):
    return first + second

def reference(inputs, first_gain, first_bias, query_weight, query_bias, keyval_weight, value_bias, output_weight, output_bias, second_gain, second_bias, up_weight, up_bias, down_weight, down_bias, cotangent):
    params = tuple((item.astype(jnp.float32) for item in (first_gain, first_bias, query_weight, query_bias, keyval_weight, value_bias, output_weight, output_bias, second_gain, second_bias, up_weight, up_bias, down_weight, down_bias)))
    seq_in = inputs.astype(jnp.float32).reshape(SEQS, SEQ_LEN, D)
    seq_cot = cotangent.astype(jnp.float32).reshape(SEQS, SEQ_LEN, D)

    def one_sequence(totals, packed):
        seq_rows, seq_grad = packed
        result, pullback = jax.vjp(forward, seq_rows, params)
        grad_x, grad_params = pullback(seq_grad)
        return (jax.tree.map(add_pair, totals, grad_params), (result, grad_x))
    zeros = jax.tree.map(jnp.zeros_like, params)
    totals, (results, grads) = lax.scan(one_sequence, zeros, (seq_in, seq_cot))
    layer_out = results.reshape(TOKENS, D).astype(jnp.bfloat16)
    grad_inputs = grads.reshape(TOKENS, D)
    return (layer_out, grad_inputs, totals[0], totals[1], totals[2], totals[3], totals[4], totals[5], totals[6], totals[7], totals[8], totals[9], totals[10], totals[11], totals[12], totals[13])
```

```python
import functools

import jax
import jax.numpy as jnp
from jax import lax
from jax.experimental import pallas as pl
from jax.experimental.pallas import tpu as pltpu
from jax.sharding import PartitionSpec as P

SPAN = 8
EPSILON = 1e-05
NEG_LARGE = -1e30
MESH = pl.DeviceIdType.MESH
VMEM = pl.BlockSpec(memory_space=pltpu.VMEM)
F32 = jnp.float32
BF16 = jnp.bfloat16


def contract(left, right, left_dim, right_dim):
    return lax.dot_general(
        left, right, (((left_dim,), (right_dim,)), ((), ())), preferred_element_type=F32
    )


def remote(source, target, send_sem, recv_sem, device):
    return pltpu.make_async_remote_copy(
        src_ref=source,
        dst_ref=target,
        send_sem=send_sem,
        recv_sem=recv_sem,
        device_id=device,
        device_id_type=MESH,
    )


def greet(devices):
    barrier = pltpu.get_barrier_semaphore()
    for device in devices:
        pl.semaphore_signal(barrier, inc=1, device_id=device, device_id_type=MESH)
    pl.semaphore_wait(barrier, len(devices))


def tensor_sum_kernel(
    chunks, part_ref, out_ref, from_core, summed, from_y, core_send, core_recv, y_send, y_recv,
    back_send, back_recv,
):
    block = lax.axis_index("dp")
    lane = lax.axis_index("tensor")
    core_peer = (block, lane + 1 - 2 * lax.rem(lane, 2))
    y_peer = (block, lax.rem(lane + 2, 4))
    rows, width = part_ref.shape
    half = width // 2
    step = rows // chunks
    mine = pl.ds(pl.multiple_of(lax.rem(lane, 2) * half, half), half)
    other = pl.ds(pl.multiple_of((1 - lax.rem(lane, 2)) * half, half), half)
    greet([core_peer, y_peer])

    def span(k):
        return pl.ds(pl.multiple_of(k * step, step), step)

    def to_core(k):
        return remote(
            part_ref.at[span(k), other], from_core.at[span(k)], core_send.at[k], core_recv.at[k],
            core_peer,
        )

    def to_y(k):
        return remote(
            summed.at[span(k)], from_y.at[span(k)], y_send.at[k], y_recv.at[k], y_peer
        )

    def back(k):
        return remote(
            out_ref.at[span(k), mine], out_ref.at[span(k), mine], back_send.at[k],
            back_recv.at[k], core_peer,
        )

    @pl.loop(0, chunks)
    def _(k):
        to_core(k).start()

    @pl.loop(0, chunks)
    def _(k):
        to_core(k).wait_recv()
        summed[span(k)] = (
            part_ref[span(k), mine].astype(F32) + from_core[span(k)].astype(F32)
        ).astype(BF16)
        to_y(k).start()

    @pl.loop(0, chunks)
    def _(k):
        to_y(k).wait_recv()
        out_ref[span(k), mine] = (
            summed[span(k)].astype(F32) + from_y[span(k)].astype(F32)
        ).astype(BF16)
        back(k).start()

    @pl.loop(0, chunks)
    def _(k):
        back(k).wait_recv()
        back(k).wait_send()
        to_core(k).wait_send()
        to_y(k).wait_send()


def tensor_sum(part, chunks=8):
    rows, width = part.shape
    half = pltpu.VMEM((rows, width // 2), BF16)
    return pl.pallas_call(
        functools.partial(tensor_sum_kernel, chunks),
        out_shape=jax.ShapeDtypeStruct((rows, width), BF16),
        in_specs=[VMEM],
        out_specs=VMEM,
        scratch_shapes=[half, half, half] + [pltpu.SemaphoreType.DMA((chunks,))] * 6,
        compiler_params=pltpu.CompilerParams(
            collective_id=0, has_side_effects=True, vmem_limit_bytes=32 << 20
        ),
        name="tensor_sum",
    )(part)


def gather_kernel(own_ref, out_ref, local_sem, x_send, x_recv, z_send, z_recv, c_send, c_recv):
    block = lax.axis_index("dp")
    lane = lax.axis_index("tensor")
    place = lax.rem(block, SPAN)
    level = place // 2
    levels = SPAN // 2
    core_peer = (block, lane + 1 - 2 * lax.rem(lane, 2))
    x_peer = (block + 1 - 2 * lax.rem(place, 2), lane)
    upper = (jnp.where(level < levels - 1, block + 2, block + 2 - SPAN), lane)
    lower = (jnp.where(level > 0, block - 2, block - 2 + SPAN), lane)
    rows = own_ref.shape[0]
    half = rows // 2
    part = pl.ds(pl.multiple_of(lax.rem(lane, 2) * half, half), half)
    greet([core_peer, x_peer, upper, lower])
    keep = pltpu.make_async_copy(own_ref, out_ref.at[place], local_sem)
    keep.start()
    to_x = remote(own_ref.at[part], out_ref.at[place, part], x_send, x_recv, x_peer)
    to_x.start()
    keep.wait()
    to_x.wait_recv()
    partner = place + 1 - 2 * lax.rem(place, 2)
    share = remote(
        out_ref.at[partner, part], out_ref.at[partner, part], c_send.at[levels - 1],
        c_recv.at[levels - 1], core_peer,
    )
    share.start()

    def pair(lev):
        return pl.ds(2 * lev, 2)

    def up(s):
        return remote(
            out_ref.at[pair(level - s), part], out_ref.at[pair(level - s), part], z_send.at[s],
            z_recv.at[s], upper,
        )

    def across(s):
        return remote(
            out_ref.at[pair(level - 1 - s), part], out_ref.at[pair(level - 1 - s), part],
            c_send.at[s], c_recv.at[s], core_peer,
        )

    for s in range(levels - 1):
        @pl.when((level < levels - 1) & (level >= s))
        def _(s=s):
            up(s).start()

        @pl.when(level > s)
        def _(s=s):
            up(s).wait_recv()
            across(s).start()

    share.wait()
    to_x.wait_send()
    for s in range(levels - 1):
        @pl.when((level < levels - 1) & (level >= s))
        def _(s=s):
            up(s).wait_send()

        @pl.when(level > s)
        def _(s=s):
            across(s).wait()


def gather_keyval(keyval):
    rows, width = keyval.shape
    levels = SPAN // 2
    dma = pltpu.SemaphoreType.DMA
    hbm = pl.BlockSpec(memory_space=pl.ANY)
    out = pl.pallas_call(
        gather_kernel,
        out_shape=jax.ShapeDtypeStruct((SPAN, rows, width), BF16),
        in_specs=[hbm],
        out_specs=hbm,
        scratch_shapes=[dma, dma, dma, dma((levels,)), dma((levels,)), dma((levels,)), dma((levels,))],
        compiler_params=pltpu.CompilerParams(collective_id=1, has_side_effects=True),
        name="gather_keyval",
    )(keyval)
    return out.reshape(SPAN * rows, width)


def small_sum_kernel(count, own_ref, out_ref, slots, send, recv):
    block = lax.axis_index("dp")
    lane = lax.axis_index("tensor")
    others = [(lax.rem(block + k, count), lane) for k in range(1, count)]
    greet(others)
    copies = []
    for k in range(1, count):
        copy = remote(own_ref, slots.at[k - 1], send.at[k - 1], recv.at[k - 1], others[k - 1])
        copy.start()
        copies.append(copy)
    total = own_ref[...]
    for k in range(1, count):
        copies[k - 1].wait()
        total = total + slots[k - 1]
    out_ref[...] = total


def small_sum(values, count):
    flat = jnp.concatenate(values)
    size = flat.shape[0]
    rows = -(-size // 1024) * 8
    packed = jnp.pad(flat, (0, rows * 128 - size)).reshape(rows, 128)
    total = pl.pallas_call(
        functools.partial(small_sum_kernel, count),
        out_shape=jax.ShapeDtypeStruct((rows, 128), F32),
        in_specs=[VMEM],
        out_specs=VMEM,
        scratch_shapes=[pltpu.VMEM((count - 1, rows, 128), F32)]
        + [pltpu.SemaphoreType.DMA((count - 1,))] * 2,
        compiler_params=pltpu.CompilerParams(collective_id=2, has_side_effects=True),
        name="small_sum",
    )(packed).reshape(-1)
    pieces = []
    start = 0
    for value in values:
        pieces.append(total[start : start + value.shape[0]])
        start += value.shape[0]
    return pieces


def scatter_sum(own, other, group):
    count = lax.axis_size("dp")
    length = group // 2
    block = lax.axis_index("dp")
    level = lax.rem(block, group) // 2

    def shifted(value, sources, step):
        pairs = [
            (base + 2 * source + side, base + 2 * (source + step) + side)
            for base in range(0, count, group)
            for source in sources
            for side in range(2)
        ]
        return lax.ppermute(value, "dp", pairs)

    received = lax.ppermute(other, "dp", [(p, p ^ 1) for p in range(count)])
    total = (own.astype(F32) + received.astype(F32)).astype(BF16)

    def slot(index):
        index = jnp.clip(index, 0, length - 1)
        return lax.dynamic_index_in_dim(total, index, 0, keepdims=False)

    up, down = slot(level + length - 1), slot(level - length + 1)
    for s in range(1, length):
        up = shifted(up, range(0, s), 1)
        down = shifted(down, range(length - s, length), -1)
        kept_up = slot(level + length - 1 - s).astype(F32)
        kept_down = slot(level - length + 1 + s).astype(F32)
        if s < length - 1:
            up = (kept_up + up.astype(F32)).astype(BF16)
            down = (kept_down + down.astype(F32)).astype(BF16)
        else:
            return kept_up + up.astype(F32) + down.astype(F32)


def split_sides(part, group):
    rows = part.shape[0] // group
    side = lax.rem(lax.axis_index("dp"), 2)
    parts = part.reshape(group // 2, 2, rows, part.shape[1])
    own = lax.dynamic_index_in_dim(parts, side, 1, keepdims=False)
    other = lax.dynamic_index_in_dim(parts, 1 - side, 1, keepdims=False)
    return own, other


def attend_kernel(q_rows, k_rows, q_ref, kv_ref, ctx_ref, lse_ref, acc, peak, total):
    rows = q_ref.shape[0]
    head = kv_ref.shape[1] // 2
    heads = q_ref.shape[1] // head
    place = lax.rem(lax.axis_index("dp"), SPAN)
    for i in range(rows // q_rows):
        span = slice(i * q_rows, (i + 1) * q_rows)
        peak[...] = jnp.full_like(peak, NEG_LARGE)
        total[...] = jnp.zeros_like(total)
        acc[...] = jnp.zeros_like(acc)

        def step(j, diagonal):
            at = pl.ds(pl.multiple_of(j * k_rows, k_rows), k_rows)
            keys = kv_ref[at, 0:head]
            values = kv_ref[at, head : 2 * head]
            for h in range(heads):
                query = q_ref[span, h * head : (h + 1) * head]
                scores = contract(keys, query, 1, 1)
                if diagonal is not None:
                    key_at = lax.broadcasted_iota(jnp.int32, scores.shape, 0) + diagonal
                    query_at = lax.broadcasted_iota(jnp.int32, scores.shape, 1)
                    scores = jnp.where(key_at <= query_at, scores, NEG_LARGE)
                old = peak[h]
                new = jnp.maximum(old, jnp.max(scores, axis=0, keepdims=True))
                probs = jnp.exp(scores - new)
                fade = jnp.exp(old - new)
                total[h] = total[h] * fade + jnp.sum(probs, axis=0, keepdims=True)
                peak[h] = new
                acc[h] = acc[h] * fade + contract(values, probs.astype(BF16), 0, 0)

        full = (place * rows + i * q_rows) // k_rows

        @pl.loop(0, full)
        def _(j):
            step(j, None)

        for d in range(q_rows // k_rows):
            step(full + d, d * k_rows)
        for h in range(heads):
            context = acc[h] / total[h]
            ctx_ref[span, h * head : (h + 1) * head] = context.T.astype(BF16)
            lse_ref[h : h + 1, span] = peak[h] + jnp.log(total[h])


def attend(queries, keyval, q_rows=512, k_rows=512):
    rows, width = queries.shape
    head = keyval.shape[1] // 2
    heads = width // head
    stat = pltpu.VMEM((heads, 1, q_rows), F32)
    return pl.pallas_call(
        functools.partial(attend_kernel, q_rows, k_rows),
        out_shape=(
            jax.ShapeDtypeStruct((rows, width), BF16),
            jax.ShapeDtypeStruct((heads, rows), F32),
        ),
        in_specs=[VMEM, VMEM],
        out_specs=(VMEM, VMEM),
        scratch_shapes=[pltpu.VMEM((heads, head, q_rows), F32), stat, stat],
        compiler_params=pltpu.CompilerParams(vmem_limit_bytes=48 << 20),
        cost_estimate=pl.CostEstimate(
            flops=16 * rows * rows * width, bytes_accessed=8 << 20, transcendentals=0
        ),
        name="attend",
    )(queries, keyval)


def attend_back_kernel(
    q_rows, k_rows, q_ref, kv_ref, do_ref, ctx_ref, lse_ref, dq_ref, dkv_ref, dq_acc, dkv_acc, delta
):
    rows = q_ref.shape[0]
    head = kv_ref.shape[1] // 2
    heads = q_ref.shape[1] // head
    place = lax.rem(lax.axis_index("dp"), SPAN)
    dkv_acc[...] = jnp.zeros_like(dkv_acc)
    for i in range(rows // q_rows):
        span = slice(i * q_rows, (i + 1) * q_rows)
        for h in range(heads):
            cols = slice(h * head, (h + 1) * head)
            product = do_ref[span, cols].astype(F32) * ctx_ref[span, cols].astype(F32)
            delta[h] = jnp.sum(product.T, axis=0, keepdims=True)
        dq_acc[...] = jnp.zeros_like(dq_acc)

        def step(j, diagonal):
            at = pl.ds(pl.multiple_of(j * k_rows, k_rows), k_rows)
            keys = kv_ref[at, 0:head]
            values = kv_ref[at, head : 2 * head]
            d_keys = jnp.zeros((k_rows, head), F32)
            d_values = jnp.zeros((k_rows, head), F32)
            for h in range(heads):
                cols = slice(h * head, (h + 1) * head)
                query = q_ref[span, cols]
                d_ctx = do_ref[span, cols]
                scores = contract(keys, query, 1, 1)
                if diagonal is not None:
                    key_at = lax.broadcasted_iota(jnp.int32, scores.shape, 0) + diagonal
                    query_at = lax.broadcasted_iota(jnp.int32, scores.shape, 1)
                    scores = jnp.where(key_at <= query_at, scores, NEG_LARGE)
                probs = jnp.exp(scores - lse_ref[h : h + 1, span])
                d_probs = contract(values, d_ctx, 1, 1)
                d_scores = (probs * (d_probs - delta[h])).astype(BF16)
                d_values += contract(probs.astype(BF16), d_ctx, 1, 0)
                d_keys += contract(d_scores, query, 1, 0)
                dq_acc[h] += contract(keys, d_scores, 0, 0)
            dkv_acc[at, 0:head] += d_keys
            dkv_acc[at, head : 2 * head] += d_values

        full = (place * rows + i * q_rows) // k_rows

        @pl.loop(0, full)
        def _(j):
            step(j, None)

        for d in range(q_rows // k_rows):
            step(full + d, d * k_rows)
        for h in range(heads):
            dq_ref[span, h * head : (h + 1) * head] = (dq_acc[h] * head**-0.5).T.astype(BF16)
    dkv_ref[...] = dkv_acc[...].astype(BF16)


def attend_back(queries, keyval, d_context, context, lse, q_rows=512, k_rows=512):
    rows, width = queries.shape
    head = keyval.shape[1] // 2
    heads = width // head
    return pl.pallas_call(
        functools.partial(attend_back_kernel, q_rows, k_rows),
        out_shape=(
            jax.ShapeDtypeStruct((rows, width), BF16),
            jax.ShapeDtypeStruct(keyval.shape, BF16),
        ),
        in_specs=[VMEM] * 5,
        out_specs=(VMEM, VMEM),
        scratch_shapes=[
            pltpu.VMEM((heads, head, q_rows), F32),
            pltpu.VMEM(keyval.shape, F32),
            pltpu.VMEM((heads, 1, q_rows), F32),
        ],
        compiler_params=pltpu.CompilerParams(vmem_limit_bytes=56 << 20),
        cost_estimate=pl.CostEstimate(
            flops=40 * rows * rows * width, bytes_accessed=12 << 20, transcendentals=0
        ),
        name="attend_back",
    )(queries, keyval, d_context, context, lse)


def layer_norm(values, norm_gain, norm_bias):
    average = jnp.mean(values, axis=-1, keepdims=True)
    centred = values - average
    variance = jnp.mean(centred * centred, axis=-1, keepdims=True)
    return centred * lax.rsqrt(variance + EPSILON) * norm_gain + norm_bias


def gelu_tanh(values):
    return jax.nn.gelu(values, approximate=True)


def per_device(
    inputs,
    first_gain,
    first_bias,
    query_weight,
    query_bias,
    keyval_weight,
    value_bias,
    output_weight,
    output_bias,
    second_gain,
    second_bias,
    up_weight,
    up_bias,
    down_weight,
    down_bias,
    cotangent,
):
    count = lax.axis_size("dp")
    head_size = value_bias.shape[0]
    score_scale = head_size ** (-0.5)
    x_full = inputs.astype(F32)
    normed1_full, first_pull = jax.vjp(layer_norm, x_full, first_gain, first_bias)
    normed1 = normed1_full.astype(BF16)
    query_pre = jnp.dot(normed1, query_weight, preferred_element_type=F32) + query_bias
    queries = (query_pre * score_scale).astype(BF16)
    kv_bias = jnp.concatenate([jnp.zeros_like(value_bias), value_bias])
    keyval = (jnp.dot(normed1, keyval_weight, preferred_element_type=F32) + kv_bias).astype(BF16)
    keyval_all = gather_keyval(keyval)
    context_low, lse = attend(queries, keyval_all)
    attn_part = jnp.dot(context_low, output_weight, preferred_element_type=F32).astype(BF16)
    middle = x_full + tensor_sum(attn_part).astype(F32) + output_bias
    normed2_full, second_pull = jax.vjp(layer_norm, middle, second_gain, second_bias)
    normed2 = normed2_full.astype(BF16)
    pre_act = jnp.dot(normed2, up_weight, preferred_element_type=F32) + up_bias
    act_full, gelu_pull = jax.vjp(gelu_tanh, pre_act)
    activ = act_full.astype(BF16)
    grad_full = cotangent.astype(F32)
    d_down_bias = jnp.sum(grad_full, axis=0)
    d_pre = gelu_pull(contract(cotangent, down_weight, 1, 1))[0].astype(BF16)
    d_normed2_part = contract(d_pre, up_weight, 1, 1).astype(BF16)
    d_normed2 = tensor_sum(d_normed2_part).astype(F32)
    grad_down_part = contract(cotangent, activ, 0, 0).astype(BF16)
    sent_down = scatter_sum(*split_sides(grad_down_part, count), count)
    grad_up_part = contract(normed2, d_pre, 0, 0).astype(BF16)
    sent_up = scatter_sum(*split_sides(grad_up_part, count), count)
    d_up_bias = jnp.sum(d_pre.astype(F32), axis=0)
    mlp_part = jnp.dot(activ, down_weight, preferred_element_type=F32).astype(BF16)
    result = middle + tensor_sum(mlp_part).astype(F32) + down_bias
    layer_out = result.astype(BF16)
    d_middle_norm, d_second_gain, d_second_bias = second_pull(d_normed2)
    d_middle = grad_full + d_middle_norm
    d_output_bias = jnp.sum(d_middle, axis=0)
    d_middle_low = d_middle.astype(BF16)
    grad_out_part = contract(d_middle_low, context_low, 0, 0).astype(BF16)
    d_context = contract(d_middle_low, output_weight, 1, 1).astype(BF16)
    d_queries, d_kv_part = attend_back(queries, keyval_all, d_context, context_low, lse)
    grad_query_part = contract(normed1, d_queries, 0, 0).astype(BF16)
    d_query_bias = jnp.sum(d_queries.astype(F32), axis=0)
    d_normed1_query = contract(d_queries, query_weight, 1, 1).astype(BF16)
    d_kv_own = scatter_sum(*split_sides(d_kv_part, SPAN), SPAN)
    d_normed1_sum = tensor_sum(d_normed1_query).astype(F32)
    d_keyval = lax.psum(d_kv_own.astype(BF16), "tensor")
    grad_kv_part = contract(normed1, d_keyval, 0, 0).astype(BF16)
    d_value_bias = jnp.sum(d_keyval[:, head_size:].astype(F32), axis=0)
    d_normed1 = d_normed1_sum + contract(d_keyval, keyval_weight, 1, 1)
    d_x_norm, d_first_gain, d_first_bias = first_pull(d_normed1)
    grad_inputs = d_middle + d_x_norm
    local = query_weight.shape[1]
    rest_part = jnp.concatenate([grad_query_part, grad_out_part, grad_kv_part], axis=1)
    sent_rest = scatter_sum(*split_sides(rest_part, count), count)
    sums = small_sum(
        [
            d_first_gain,
            d_first_bias,
            d_query_bias,
            d_value_bias,
            d_output_bias,
            d_second_gain,
            d_second_bias,
            d_up_bias,
            d_down_bias,
        ],
        count,
    )
    return (
        layer_out,
        grad_inputs,
        sums[0],
        sums[1],
        sent_rest[:, :local],
        sums[2],
        sent_rest[:, 2 * local :],
        sums[3],
        sent_rest[:, local : 2 * local].T,
        sums[4],
        sums[5],
        sums[6],
        sent_up,
        sums[7],
        sent_down.T,
        sums[8],
    )


def solution(mesh):
    in_specs = (
        P("dp", None),
        P(),
        P(),
        P(None, "tensor"),
        P("tensor"),
        P(),
        P(),
        P("tensor", None),
        P(),
        P(),
        P(),
        P(None, "tensor"),
        P("tensor"),
        P("tensor", None),
        P(),
        P("dp", None),
    )
    out_specs = (
        P("dp", None),
        P("dp", None),
        P(),
        P(),
        P("dp", "tensor"),
        P("tensor"),
        P("dp", None),
        P(),
        P("tensor", "dp"),
        P(),
        P(),
        P(),
        P("dp", "tensor"),
        P("tensor"),
        P("tensor", "dp"),
        P(),
    )
    return jax.shard_map(
        per_device, mesh=mesh, in_specs=in_specs, out_specs=out_specs, check_vma=False
    )
```

```python
import functools

import jax
import jax.numpy as jnp
from jax import lax
from jax.experimental import pallas as pl
from jax.experimental.pallas import tpu as pltpu
from jax.sharding import PartitionSpec as P

SPAN = 8
EPSILON = 1e-05
NEG_LARGE = -1e30
MESH = pl.DeviceIdType.MESH
VMEM = pl.BlockSpec(memory_space=pltpu.VMEM)
F32 = jnp.float32
BF16 = jnp.bfloat16


def contract(left, right, left_dim, right_dim):
    return lax.dot_general(
        left, right, (((left_dim,), (right_dim,)), ((), ())), preferred_element_type=F32
    )


def remote(source, target, send_sem, recv_sem, device):
    return pltpu.make_async_remote_copy(
        src_ref=source,
        dst_ref=target,
        send_sem=send_sem,
        recv_sem=recv_sem,
        device_id=device,
        device_id_type=MESH,
    )


def greet(devices):
    barrier = pltpu.get_barrier_semaphore()
    for device in devices:
        pl.semaphore_signal(barrier, inc=1, device_id=device, device_id_type=MESH)
    pl.semaphore_wait(barrier, len(devices))


class TensorSum:
    def __init__(self, chunks, part, result, from_core, summed, from_y, sems):
        block = lax.axis_index("dp")
        lane = lax.axis_index("tensor")
        core = lax.rem(lane, 2)
        self.core_peer = (block, lane + 1 - 2 * core)
        self.y_peer = (block, lax.rem(lane + 2, 4))
        rows, width = part.shape
        half = width // 2
        self.step = rows // chunks
        self.mine = pl.ds(pl.multiple_of(core * half, half), half)
        self.other = pl.ds(pl.multiple_of((1 - core) * half, half), half)
        self.part, self.result = part, result
        self.from_core, self.summed, self.from_y = from_core, summed, from_y
        self.sems = sems

    def span(self, k):
        return pl.ds(pl.multiple_of(k * self.step, self.step), self.step)

    def to_core(self, k):
        at = self.span(k)
        return remote(
            self.part.at[at, self.other], self.from_core.at[at], self.sems[0].at[k],
            self.sems[1].at[k], self.core_peer,
        )

    def to_y(self, k):
        at = self.span(k)
        return remote(
            self.summed.at[at], self.from_y.at[at], self.sems[2].at[k], self.sems[3].at[k],
            self.y_peer,
        )

    def back(self, k):
        at = self.span(k)
        return remote(
            self.result.at[at, self.mine], self.result.at[at, self.mine], self.sems[4].at[k],
            self.sems[5].at[k], self.core_peer,
        )

    def first(self, k):
        self.to_core(k).start()

    def second(self, k):
        at = self.span(k)
        self.to_core(k).wait_recv()
        total = self.part[at, self.mine].astype(F32) + self.from_core[at].astype(F32)
        self.summed[at] = total.astype(BF16)
        self.to_y(k).start()

    def third(self, k):
        at = self.span(k)
        self.to_y(k).wait_recv()
        total = self.summed[at].astype(F32) + self.from_y[at].astype(F32)
        self.result[at, self.mine] = total.astype(BF16)
        self.back(k).start()

    def finish(self, chunks):
        @pl.loop(0, chunks)
        def _(k):
            self.back(k).wait_recv()
            self.back(k).wait_send()
            self.to_core(k).wait_send()
            self.to_y(k).wait_send()


def sum_scratch(chunks, rows, width):
    half = pltpu.VMEM((rows, width // 2), BF16)
    return [pltpu.VMEM((rows, width), BF16), half, half, half] + [
        pltpu.SemaphoreType.DMA((chunks,))
    ] * 6


def grad_rows(left_ref, right, target, which):
    levels, rows = target.shape[0], target.shape[1]

    @pl.loop(0, levels)
    def _(lev):
        if rows % 128 == 0:
            cols = pl.ds(pl.multiple_of((2 * lev + which) * rows, rows), rows)
            target[lev] = contract(left_ref[:, cols], right[...], 0, 0).astype(BF16)
        else:
            cols = pl.ds(pl.multiple_of(2 * lev * rows, 2 * rows), 2 * rows)
            both = contract(left_ref[:, cols], right[...], 0, 0)
            target[lev] = jnp.where(which == 0, both[:rows], both[rows:]).astype(BF16)


def project_kernel(
    chunks, ctx_ref, wo_ref, cot_ref, wd_ref, out_ref, g_ref, part, from_core, summed, from_y, *sems
):
    ts = TensorSum(chunks, part, out_ref, from_core, summed, from_y, sems)
    greet([ts.core_peer, ts.y_peer])

    @pl.loop(0, chunks)
    def _(k):
        at = ts.span(k)
        part[at, :] = jnp.dot(
            ctx_ref[at, :], wo_ref[...], preferred_element_type=F32
        ).astype(BF16)
        ts.first(k)

        @pl.when(k >= 1)
        def _():
            ts.second(k - 1)

    ts.second(chunks - 1)
    tile = g_ref.shape[1] // 8

    @pl.loop(0, 8)
    def _(j):
        cols = pl.ds(pl.multiple_of(j * tile, tile), tile)
        g_ref[:, cols] = contract(cot_ref[...], wd_ref[cols, :], 1, 1).astype(BF16)

    @pl.loop(0, chunks)
    def _(k):
        ts.third(k)

    ts.finish(chunks)


def project(context, output_weight, cotangent, down_weight, chunks=8):
    rows, width = context.shape[0], output_weight.shape[1]
    return pl.pallas_call(
        functools.partial(project_kernel, chunks),
        out_shape=(
            jax.ShapeDtypeStruct((rows, width), BF16),
            jax.ShapeDtypeStruct((rows, down_weight.shape[0]), BF16),
        ),
        in_specs=[VMEM] * 4,
        out_specs=(VMEM, VMEM),
        scratch_shapes=sum_scratch(chunks, rows, width),
        compiler_params=pltpu.CompilerParams(
            collective_id=3, has_side_effects=True, vmem_limit_bytes=56 << 20
        ),
        name="project",
    )(context, output_weight, cotangent, down_weight)


def hidden_back_kernel(
    chunks, dpre_ref, wu_ref, n2_ref, sent_ref, dn_ref, own_ref, other_ref, got_ref, x_send, x_recv,
    part, from_core, summed, from_y, *sems,
):
    ts = TensorSum(chunks, part, dn_ref, from_core, summed, from_y, sems)
    side = lax.rem(lax.axis_index("dp"), 2)
    x_peer = (lax.axis_index("dp") + 1 - 2 * side, lax.axis_index("tensor"))
    greet([ts.core_peer, ts.y_peer, x_peer])
    levels, rows = own_ref.shape[0], own_ref.shape[1]
    to_x = remote(sent_ref.at[pl.ds(0, got_ref.shape[0])], got_ref, x_send, x_recv, x_peer)
    to_x.start()

    @pl.loop(0, chunks)
    def _(k):
        at = ts.span(k)
        part[at, :] = contract(dpre_ref[at, :], wu_ref[...], 1, 1).astype(BF16)
        ts.first(k)

        @pl.when(k >= 1)
        def _():
            ts.second(k - 1)

    ts.second(chunks - 1)

    def grad(target, which):
        grad_rows(n2_ref, dpre_ref, target, which)

    grad(other_ref, 1 - side)
    grad(own_ref, side)

    @pl.loop(0, chunks)
    def _(k):
        ts.third(k)

    ts.finish(chunks)
    to_x.wait()


def hidden_back(d_pre, up_weight, normed2, sent, count, chunks=4):
    rows, width = d_pre.shape[0], up_weight.shape[0]
    half = jax.ShapeDtypeStruct((count // 2, width // count, up_weight.shape[1]), BF16)
    got = jax.ShapeDtypeStruct((sent.shape[0] * 3 // 4,) + sent.shape[1:], BF16)
    hbm = pl.BlockSpec(memory_space=pl.ANY)
    return pl.pallas_call(
        functools.partial(hidden_back_kernel, chunks),
        out_shape=(jax.ShapeDtypeStruct((rows, width), BF16), half, half, got),
        in_specs=[VMEM] * 3 + [hbm],
        out_specs=(VMEM,) * 3 + (hbm,),
        scratch_shapes=[pltpu.SemaphoreType.DMA, pltpu.SemaphoreType.DMA]
        + sum_scratch(chunks, rows, width),
        compiler_params=pltpu.CompilerParams(
            collective_id=4, has_side_effects=True, vmem_limit_bytes=58 << 20
        ),
        name="hidden_back",
    )(d_pre, up_weight, normed2, sent)


class Chain:
    def __init__(self, length, level, upper, lower, pair, bufs, sems):
        self.length, self.level = length, level
        self.peers = (upper, lower)
        self.pair = pair
        self.bufs = bufs
        self.sems = sems

    def copy(self, way, s):
        inward, outward = self.bufs[2 * way], self.bufs[2 * way + 1]
        send, recv = self.sems[2 * way], self.sems[2 * way + 1]
        return remote(
            outward.at[s - 1], inward.at[s - 1], send.at[s - 1], recv.at[s - 1], self.peers[way]
        )

    def rank(self, way):
        return self.level if way == 0 else self.length - 1 - self.level

    def start(self, s):
        for way in range(2):
            rank = self.rank(way)
            slot = rank + self.length - s
            slot = jnp.clip(slot if way == 0 else self.length - 1 - slot, 0, self.length - 1)
            inward, outward = self.bufs[2 * way], self.bufs[2 * way + 1]

            @pl.when(rank <= s - 1)
            def _(way=way, rank=rank, slot=slot, inward=inward, outward=outward):
                outward[s - 1] = self.pair[slot]
                if s > 1:
                    @pl.when(rank >= 1)
                    def _():
                        outward[s - 1] = (
                            self.pair[slot].astype(F32) + inward[s - 2].astype(F32)
                        ).astype(BF16)

                self.copy(way, s).start()

    def arrive(self, s):
        for way in range(2):
            rank = self.rank(way)

            @pl.when((rank >= 1) & (rank <= s))
            def _(way=way):
                self.copy(way, s).wait_recv()

    def result(self, target):
        last = self.length - 2
        target[...] = self.pair[self.level].astype(F32)
        for way in range(2):
            @pl.when(self.rank(way) >= 1)
            def _(way=way):
                target[...] += self.bufs[2 * way][last].astype(F32)

    def drain(self):
        for s in range(1, self.length):
            for way in range(2):
                rank = self.rank(way)

                @pl.when(rank <= s - 1)
                def _(way=way, s=s):
                    self.copy(way, s).wait_send()


def chain_scratch(length, shape):
    return [pltpu.VMEM((length - 1,) + shape, BF16)] * 4 + [
        pltpu.SemaphoreType.DMA((length - 1,))
    ] * 4


def chain_peers():
    count = lax.axis_size("dp")
    block = lax.axis_index("dp")
    lane = lax.axis_index("tensor")
    level = block // 2
    upper = (jnp.where(level < count // 2 - 1, block + 2, block + 2 - count), lane)
    lower = (jnp.where(level > 0, block - 2, block - 2 + count), lane)
    return count // 2, level, upper, lower


def query_back_kernel(
    chunks, dq_ref, wq_ref, n1_ref, dkv0, dkv1, dkv2, dkv3, dn_ref, grad_ref, tot_ref, part,
    from_core, summed, from_y, kv_core, kv_sum, kv_x, kv_pair, kv_z, kv_up, kv_y, kv_sems, own_ref,
    other_ref, got_ref, q_send, q_recv, *rest,
):
    chain_bufs, chain_sems, sems = rest[:4], rest[4:8], rest[8:]
    ts = TensorSum(chunks, part, dn_ref, from_core, summed, from_y, sems)
    block = lax.axis_index("dp")
    lane = lax.axis_index("tensor")
    place = lax.rem(block, SPAN)
    side = lax.rem(place, 2)
    level = place // 2
    levels = SPAN // 2
    x_peer = (block + 1 - 2 * side, lane)
    upper = (jnp.where(level < levels - 1, block + 2, block + 2 - SPAN), lane)
    lower = (jnp.where(level > 0, block - 2, block - 2 + SPAN), lane)
    length, chain_level, chain_upper, chain_lower = chain_peers()
    if length == levels:
        greet([ts.core_peer, ts.y_peer, x_peer, upper, lower])
    else:
        greet([ts.core_peer, ts.y_peer, x_peer, upper, lower, chain_upper, chain_lower])
    chain = Chain(length, chain_level, chain_upper, chain_lower, own_ref, chain_bufs, chain_sems)
    core = lax.rem(lane, 2)
    seq_rows = tot_ref.shape[0]
    half = seq_rows // 2
    mine = pl.ds(pl.multiple_of(core * half, half), half)
    other = pl.ds(pl.multiple_of((1 - core) * half, half), half)

    def kv_copy(source, target, index, device):
        return remote(source, target, kv_sems.at[0, index], kv_sems.at[1, index], device)

    dkv_refs = (dkv0, dkv1, dkv2, dkv3)
    to_core = [
        kv_copy(ref.at[:, other], kv_core.at[lev], 3 + levels + lev, ts.core_peer)
        for lev, ref in enumerate(dkv_refs)
    ]
    for copy in to_core:
        copy.start()
    grad_levels, rows = own_ref.shape[0], own_ref.shape[1]

    @pl.loop(0, chunks)
    def _(k):
        at = ts.span(k)
        part[at, :] = contract(dq_ref[at, :], wq_ref[...], 1, 1).astype(BF16)
        ts.first(k)

        @pl.when(k >= 1)
        def _():
            ts.second(k - 1)

    ts.second(chunks - 1)
    for lev, ref in enumerate(dkv_refs):
        to_core[lev].wait_recv()
        kv_sum[lev] = (ref[:, mine].astype(F32) + kv_core[lev].astype(F32)).astype(BF16)

    to_x = kv_copy(kv_sum.at[:, 1 - side], kv_x, 1, x_peer)
    to_x.start()

    def grad(target, which):
        grad_rows(n1_ref, dq_ref, target, which)

    grad(other_ref, 1 - side)
    q_to_x = remote(other_ref, got_ref, q_send, q_recv, x_peer)
    q_to_x.start()
    grad(own_ref, side)
    to_x.wait_recv()

    @pl.loop(0, levels)
    def _(lev):
        kv_pair[lev] = (kv_sum[lev, side].astype(F32) + kv_x[lev].astype(F32)).astype(BF16)

    def down(s):
        slot = jnp.maximum(level - levels + s, 0)
        return kv_copy(kv_up.at[s - 1], kv_z.at[s - 1], 1 + s, lower), slot

    for s in range(1, levels):
        copy, slot = down(s)

        @pl.when(level >= levels - s)
        def _(copy=copy, slot=slot, s=s):
            kv_up[s - 1] = kv_pair[slot]
            if s > 1:
                @pl.when(level < levels - 1)
                def _():
                    kv_up[s - 1] = (
                        kv_pair[slot].astype(F32) + kv_z[s - 2].astype(F32)
                    ).astype(BF16)

            copy.start()

        @pl.when((level >= levels - 1 - s) & (level < levels - 1))
        def _(copy=copy):
            copy.wait_recv()

    kv_up[levels - 1] = kv_pair[level]

    @pl.when(level < levels - 1)
    def _():
        kv_up[levels - 1] = (
            kv_pair[level].astype(F32) + kv_z[levels - 2].astype(F32)
        ).astype(BF16)

    to_y = kv_copy(kv_up.at[levels - 1], kv_y, 1 + levels, ts.y_peer)
    to_y.start()
    q_to_x.wait_recv()

    @pl.loop(0, grad_levels)
    def _(lev):
        own_ref[lev] = (own_ref[lev].astype(F32) + got_ref[lev].astype(F32)).astype(BF16)

    chain.start(1)
    to_y.wait_recv()
    tot_ref[mine] = (kv_up[levels - 1].astype(F32) + kv_y[...].astype(F32)).astype(BF16)
    back = kv_copy(tot_ref.at[mine], tot_ref.at[mine], 2 + levels, ts.core_peer)
    back.start()
    half_way = chunks // 2
    for s in range(1, length):
        if s == 2:
            @pl.loop(0, half_way)
            def _(k):
                ts.third(k)

        chain.arrive(s)
        if s + 1 < length:
            chain.start(s + 1)

    @pl.loop(half_way, chunks)
    def _(k):
        ts.third(k)

    chain.result(grad_ref)
    chain.drain()
    q_to_x.wait_send()
    back.wait()
    for copy in to_core:
        copy.wait_send()
    to_x.wait_send()
    to_y.wait_send()
    for s in range(1, levels):
        copy, _slot = down(s)

        @pl.when(level >= levels - s)
        def _(copy=copy):
            copy.wait_send()

    ts.finish(chunks)


def query_back(d_queries, query_weight, normed1, d_kv_parts, count, chunks=4):
    rows, width = d_queries.shape[0], query_weight.shape[0]
    kv_width = d_kv_parts[0].shape[1]
    levels = SPAN // 2
    parts = [part.reshape(2, rows, kv_width) for part in d_kv_parts]
    shape = (width // count, query_weight.shape[1])
    half = pltpu.VMEM((count // 2,) + shape, BF16)
    piece = (rows // 2, kv_width)
    return pl.pallas_call(
        functools.partial(query_back_kernel, chunks),
        out_shape=(
            jax.ShapeDtypeStruct((rows, width), BF16),
            jax.ShapeDtypeStruct(shape, F32),
            jax.ShapeDtypeStruct((rows, kv_width), BF16),
        ),
        in_specs=[VMEM] * (3 + levels),
        out_specs=(VMEM,) * 3,
        scratch_shapes=sum_scratch(chunks, rows, width)[:4]
        + [
            pltpu.VMEM((levels, 2) + piece, BF16),
            pltpu.VMEM((levels, 2) + piece, BF16),
            pltpu.VMEM((levels,) + piece, BF16),
            pltpu.VMEM((levels,) + piece, BF16),
            pltpu.VMEM((levels - 1,) + piece, BF16),
            pltpu.VMEM((levels,) + piece, BF16),
            pltpu.VMEM(piece, BF16),
            pltpu.SemaphoreType.DMA((2, 3 + 2 * levels)),
            half,
            half,
            half,
            pltpu.SemaphoreType.DMA,
            pltpu.SemaphoreType.DMA,
        ]
        + chain_scratch(count // 2, shape)
        + [pltpu.SemaphoreType.DMA((chunks,))] * 6,
        compiler_params=pltpu.CompilerParams(
            collective_id=5, has_side_effects=True, vmem_limit_bytes=58 << 20
        ),
        name="query_back",
    )(d_queries, query_weight, normed1, *parts)


def gather_kernel(own_ref, out_ref, local_sem, x_send, x_recv, z_send, z_recv, s_send, s_recv):
    block = lax.axis_index("dp")
    lane = lax.axis_index("tensor")
    place = lax.rem(block, SPAN)
    side = lax.rem(place, 2)
    level = place // 2
    levels = SPAN // 2
    core = lax.rem(lane, 2)
    core_lane = lane + 1 - 2 * core
    y_lane = lax.rem(lane + 2, 4)
    core_peer = (block, core_lane)
    y_peer = (block, y_lane)
    x_peer = (block + 1 - 2 * side, lane)
    upper = (jnp.where(level < levels - 1, block + 2, block + 2 - SPAN), lane)
    lower = (jnp.where(level > 0, block - 2, block - 2 + SPAN), lane)
    piece = own_ref.shape[0] // 4

    def rows(which):
        return pl.ds(pl.multiple_of(which * piece, piece), piece)

    greet([core_peer, y_peer, x_peer, upper, lower])
    keep = pltpu.make_async_copy(own_ref, out_ref.at[place], local_sem)
    keep.start()
    to_x = remote(own_ref.at[rows(lane)], out_ref.at[place, rows(lane)], x_send, x_recv, x_peer)
    to_x.start()
    keep.wait()
    to_x.wait_recv()

    def share(s, kind):
        blocks = pl.ds(place + 1 - 2 * side, 1) if s == 0 else pl.ds(2 * (level - s), 2)
        at = rows(y_lane if kind == 2 else lane)
        ref = out_ref.at[blocks, at]
        return remote(
            ref, ref, s_send.at[s, kind], s_recv.at[s, kind], y_peer if kind == 0 else core_peer
        )

    def up(s):
        ref = out_ref.at[pl.ds(2 * (level - s), 2), rows(lane)]
        return remote(ref, ref, z_send.at[s], z_recv.at[s], upper)

    def from_below(s):
        ref = out_ref.at[pl.ds(2 * (level - 1 - s), 2), rows(lane)]
        return remote(ref, ref, z_send.at[s], z_recv.at[s], upper)

    for s in range(levels):
        @pl.when(level >= s)
        def _(s=s):
            if s > 0:
                from_below(s - 1).wait_recv()
            if s < levels - 1:
                @pl.when(level < levels - 1)
                def _():
                    up(s).start()

            share(s, 0).start()
            share(s, 1).start()

    for s in range(levels):
        @pl.when(level >= s)
        def _(s=s):
            share(s, 0).wait_recv()
            share(s, 2).start()

    for s in range(levels):
        @pl.when(level >= s)
        def _(s=s):
            share(s, 0).wait_send()
            share(s, 1).wait()
            share(s, 2).wait()
            if s < levels - 1:
                @pl.when(level < levels - 1)
                def _():
                    up(s).wait_send()

    to_x.wait_send()


def gather_keyval(keyval):
    rows, width = keyval.shape
    levels = SPAN // 2
    dma = pltpu.SemaphoreType.DMA
    hbm = pl.BlockSpec(memory_space=pl.ANY)
    out = pl.pallas_call(
        gather_kernel,
        out_shape=jax.ShapeDtypeStruct((SPAN, rows, width), BF16),
        in_specs=[hbm],
        out_specs=hbm,
        scratch_shapes=[dma, dma, dma]
        + [dma((levels - 1,))] * 2
        + [dma((levels, 3))] * 2,
        compiler_params=pltpu.CompilerParams(collective_id=1, has_side_effects=True),
        name="gather_keyval",
    )(keyval)
    return out.reshape(SPAN * rows, width)


def last_sums_kernel(
    n1_ref, dkv_ref, own_vec, grad_ref, vec_ref, own_ref, other_ref, got_ref, x_send, x_recv, slots,
    send, recv, *chain_refs,
):
    block = lax.axis_index("dp")
    lane = lax.axis_index("tensor")
    count = lax.axis_size("dp")
    side = lax.rem(block, 2)
    others = [(lax.rem(block + k, count), lane) for k in range(1, count)]
    x_peer = (block + 1 - 2 * side, lane)
    greet(others)
    copies = []
    for k in range(1, count):
        copy = remote(own_vec, slots.at[k - 1], send.at[k - 1], recv.at[k - 1], others[k - 1])
        copy.start()
        copies.append(copy)
    levels, rows = own_ref.shape[0], own_ref.shape[1]

    def grad(target, which):
        grad_rows(n1_ref, dkv_ref, target, which)

    grad(other_ref, 1 - side)
    to_x = remote(other_ref, got_ref, x_send, x_recv, x_peer)
    to_x.start()
    grad(own_ref, side)
    length, level, upper, lower = chain_peers()
    chain = Chain(length, level, upper, lower, own_ref, chain_refs[:4], chain_refs[4:8])
    to_x.wait_recv()
    own_ref[...] = (own_ref[...].astype(F32) + got_ref[...].astype(F32)).astype(BF16)
    chain.start(1)
    for s in range(1, length):
        chain.arrive(s)
        if s + 1 < length:
            chain.start(s + 1)
    chain.result(grad_ref)
    total = own_vec[...]
    for k in range(1, count):
        copies[k - 1].wait()
        total = total + slots[k - 1]
    vec_ref[...] = total
    chain.drain()
    to_x.wait_send()


def last_sums(normed1, d_keyval, values, count):
    flat = jnp.concatenate(values)
    size = flat.shape[0]
    rows = -(-size // 1024) * 8
    packed = jnp.pad(flat, (0, rows * 128 - size)).reshape(rows, 128)
    shape = (normed1.shape[1] // count, d_keyval.shape[1])
    half = pltpu.VMEM((count // 2,) + shape, BF16)
    dma = pltpu.SemaphoreType.DMA
    grad, total = pl.pallas_call(
        last_sums_kernel,
        out_shape=(jax.ShapeDtypeStruct(shape, F32), jax.ShapeDtypeStruct((rows, 128), F32)),
        in_specs=[VMEM] * 3,
        out_specs=(VMEM, VMEM),
        scratch_shapes=[
            half,
            half,
            half,
            dma,
            dma,
            pltpu.VMEM((count - 1, rows, 128), F32),
            dma((count - 1,)),
            dma((count - 1,)),
        ]
        + chain_scratch(count // 2, shape),
        compiler_params=pltpu.CompilerParams(
            collective_id=2, has_side_effects=True, vmem_limit_bytes=32 << 20
        ),
        name="last_sums",
    )(normed1, d_keyval, packed)
    total = total.reshape(-1)
    pieces = []
    start = 0
    for value in values:
        pieces.append(total[start : start + value.shape[0]])
        start += value.shape[0]
    return grad, pieces


def layer_sum(part):
    lane = lax.axis_index("tensor")
    core = lax.rem(lane, 2)
    half = part.shape[1] // 2
    mine = lax.dynamic_slice_in_dim(part, core * half, half, 1)
    other = lax.dynamic_slice_in_dim(part, (1 - core) * half, half, 1)
    core_pairs = [(0, 1), (1, 0), (2, 3), (3, 2)]
    y_pairs = [(0, 2), (2, 0), (1, 3), (3, 1)]
    got = lax.ppermute(other, "tensor", core_pairs)
    summed = (mine.astype(F32) + got.astype(F32)).astype(BF16)
    return summed, lax.ppermute(summed, "tensor", y_pairs)


def layer_join(summed, got):
    core = lax.rem(lax.axis_index("tensor"), 2)
    total = (summed.astype(F32) + got.astype(F32)).astype(BF16)
    peer = lax.ppermute(total, "tensor", [(0, 1), (1, 0), (2, 3), (3, 2)])
    return jnp.concatenate(
        [jnp.where(core == 0, total, peer), jnp.where(core == 0, peer, total)], axis=1
    )


def together(*values):
    return lax.optimization_barrier(values)


class ScatterSum:
    def __init__(self, own, other, arrived=None):
        self.count = lax.axis_size("dp")
        self.length = self.count // 2
        self.level = lax.axis_index("dp") // 2
        self.own = own
        if arrived is not None:
            other = other[arrived.shape[0] :]
        got = lax.ppermute(other, "dp", [(p, p ^ 1) for p in range(self.count)])
        if arrived is not None:
            got = jnp.concatenate([arrived, got], axis=0)
        self.flying = (got,)
        self.s = 0

    def shifted(self, value, sources, step):
        pairs = [
            (2 * source + side, 2 * (source + step) + side)
            for source in sources
            for side in range(2)
        ]
        return lax.ppermute(value, "dp", pairs)

    def slot(self, index):
        index = jnp.clip(index, 0, self.length - 1)
        return lax.dynamic_index_in_dim(self.total, index, 0, keepdims=False)

    def step(self, *values):
        length, level = self.length, self.level
        self.s += 1
        s = self.s
        if s == 1:
            self.total = (self.own.astype(F32) + self.flying[0].astype(F32)).astype(BF16)
            up, down = self.slot(level + length - 1), self.slot(level - length + 1)
        else:
            up, down = self.flying
            up = self.slot(level + length - s).astype(F32) + up.astype(F32)
            if s == length:
                self.result = up + down.astype(F32)
                return values
            down = self.slot(level - length + s).astype(F32) + down.astype(F32)
            up, down = up.astype(BF16), down.astype(BF16)
        up, down, *values = together(up, down, *values)
        self.flying = (
            self.shifted(up, range(0, s), 1),
            self.shifted(down, range(length - s, length), -1),
        )
        return values

    def finish(self):
        while self.s < self.length:
            self.step()
        return self.result


def weight_grad_kernel(left_ref, right_ref, own_ref, other_ref):
    side = lax.rem(lax.axis_index("dp"), 2)
    grad_rows(left_ref, right_ref, other_ref, 1 - side)
    grad_rows(left_ref, right_ref, own_ref, side)


def weight_grad(left, right, count):
    half = jax.ShapeDtypeStruct((count // 2, left.shape[1] // count, right.shape[1]), BF16)
    return pl.pallas_call(
        weight_grad_kernel,
        out_shape=(half, half),
        in_specs=[VMEM] * 2,
        out_specs=(VMEM,) * 2,
        compiler_params=pltpu.CompilerParams(vmem_limit_bytes=40 << 20),
        cost_estimate=pl.CostEstimate(
            flops=2 * left.shape[0] * left.shape[1] * right.shape[1],
            bytes_accessed=16 << 20,
            transcendentals=0,
        ),
        name="weight_grad",
    )(left, right)


def attend_kernel(q_rows, k_rows, q_ref, kv_ref, ctx_ref, lse_ref, acc, peak, total):
    rows = q_ref.shape[0]
    head = kv_ref.shape[1] // 2
    heads = q_ref.shape[1] // head
    place = lax.rem(lax.axis_index("dp"), SPAN)
    for i in range(rows // q_rows):
        span = slice(i * q_rows, (i + 1) * q_rows)
        peak[...] = jnp.full_like(peak, NEG_LARGE)
        total[...] = jnp.zeros_like(total)
        acc[...] = jnp.zeros_like(acc)

        def step(j, diagonal):
            at = pl.ds(pl.multiple_of(j * k_rows, k_rows), k_rows)
            keys = kv_ref[at, 0:head]
            values = kv_ref[at, head : 2 * head]
            for h in range(heads):
                query = q_ref[span, h * head : (h + 1) * head]
                scores = contract(keys, query, 1, 1)
                if diagonal is not None:
                    key_at = lax.broadcasted_iota(jnp.int32, scores.shape, 0) + diagonal
                    query_at = lax.broadcasted_iota(jnp.int32, scores.shape, 1)
                    scores = jnp.where(key_at <= query_at, scores, NEG_LARGE)
                old = peak[h]
                new = jnp.maximum(old, jnp.max(scores, axis=0, keepdims=True))
                probs = jnp.exp(scores - new)
                fade = jnp.exp(old - new)
                total[h] = total[h] * fade + jnp.sum(probs, axis=0, keepdims=True)
                peak[h] = new
                acc[h] = acc[h] * fade + contract(values, probs.astype(BF16), 0, 0)

        full = (place * rows + i * q_rows) // k_rows

        @pl.loop(0, full)
        def _(j):
            step(j, None)

        for d in range(q_rows // k_rows):
            step(full + d, d * k_rows)
        for h in range(heads):
            context = acc[h] / total[h]
            ctx_ref[span, h * head : (h + 1) * head] = context.T.astype(BF16)
            lse_ref[h : h + 1, span] = peak[h] + jnp.log(total[h])


def attend(queries, keyval, q_rows=512, k_rows=512):
    rows, width = queries.shape
    head = keyval.shape[1] // 2
    heads = width // head
    stat = pltpu.VMEM((heads, 1, q_rows), F32)
    return pl.pallas_call(
        functools.partial(attend_kernel, q_rows, k_rows),
        out_shape=(
            jax.ShapeDtypeStruct((rows, width), BF16),
            jax.ShapeDtypeStruct((heads, rows), F32),
        ),
        in_specs=[VMEM, VMEM],
        out_specs=(VMEM, VMEM),
        scratch_shapes=[pltpu.VMEM((heads, head, q_rows), F32), stat, stat],
        compiler_params=pltpu.CompilerParams(vmem_limit_bytes=48 << 20),
        cost_estimate=pl.CostEstimate(
            flops=16 * rows * rows * width, bytes_accessed=8 << 20, transcendentals=0
        ),
        name="attend",
    )(queries, keyval)


def attend_back_kernel(
    target, q_rows, k_rows, first, last, q_ref, kv_ref, do_ref, lse_ref, *refs
):
    refs = list(refs)
    if first:
        ctx_ref = refs.pop(0)
    else:
        delta, dq_in = refs.pop(0), refs.pop(0)
    dkv_ref = refs.pop(0)
    if first:
        delta = refs.pop(0)
    if last:
        dq_ref = refs.pop(0)
    else:
        dq_out = refs.pop(0)
    dq_acc, dkv_acc = refs
    rows = q_ref.shape[0]
    head = kv_ref.shape[1] // 2
    heads = q_ref.shape[1] // head
    place = lax.rem(lax.axis_index("dp"), SPAN)
    dkv_acc[...] = jnp.zeros_like(dkv_acc)
    for i in range(rows // q_rows):
        span = slice(i * q_rows, (i + 1) * q_rows)
        if first:
            for h in range(heads):
                cols = slice(h * head, (h + 1) * head)
                product = do_ref[span, cols].astype(F32) * ctx_ref[span, cols].astype(F32)
                delta[h : h + 1, span] = jnp.sum(product.T, axis=0, keepdims=True)
            dq_acc[...] = jnp.zeros_like(dq_acc)
        else:
            dq_acc[...] = dq_in[i]

        def step(j, diagonal):
            at = pl.ds(pl.multiple_of(j * k_rows, k_rows), k_rows)
            keys = kv_ref[at, 0:head]
            values = kv_ref[at, head : 2 * head]
            d_keys = jnp.zeros((k_rows, head), F32)
            d_values = jnp.zeros((k_rows, head), F32)
            for h in range(heads):
                cols = slice(h * head, (h + 1) * head)
                query = q_ref[span, cols]
                d_ctx = do_ref[span, cols]
                scores = contract(keys, query, 1, 1)
                if diagonal:
                    key_at = lax.broadcasted_iota(jnp.int32, scores.shape, 0)
                    query_at = lax.broadcasted_iota(jnp.int32, scores.shape, 1)
                    scores = jnp.where(key_at <= query_at, scores, NEG_LARGE)
                probs = jnp.exp(scores - lse_ref[h : h + 1, span])
                d_probs = contract(values, d_ctx, 1, 1)
                d_scores = (probs * (d_probs - delta[h : h + 1, span])).astype(BF16)
                d_values += contract(probs.astype(BF16), d_ctx, 1, 0)
                d_keys += contract(d_scores, query, 1, 0)
                dq_acc[h] += contract(keys, d_scores, 0, 0)
            dkv_acc[at, 0:head] += d_keys
            dkv_acc[at, head : 2 * head] += d_values

        parts = kv_ref.shape[0] // k_rows
        full = (place * rows + i * q_rows) // k_rows - target * parts

        @pl.loop(0, jnp.clip(full, 0, parts))
        def _(j):
            step(j, False)

        @pl.when((full >= 0) & (full < parts))
        def _():
            step(full, True)

        if last:
            for h in range(heads):
                dq_ref[span, h * head : (h + 1) * head] = (
                    (dq_acc[h] * head**-0.5).T.astype(BF16)
                )
        else:
            dq_out[i] = dq_acc[...]
    dkv_ref[...] = dkv_acc[...].astype(BF16)


def attend_back(target, queries, keyval, d_context, lse, context, carried, block=512):
    rows, width = queries.shape
    head = keyval.shape[1] // 2
    heads = width // head
    first, last = target == 0, target == SPAN // 2 - 1
    span = 2 * rows
    kv_spec = pl.BlockSpec((span, 2 * head), lambda i: (target, 0))
    dq_shape = (rows // block, heads, head, block)
    whole = lambda shape: pl.BlockSpec(shape, lambda i: (0,) * len(shape))
    outs = [jax.ShapeDtypeStruct((span, 2 * head), BF16)]
    args = [queries, keyval, d_context, lse]
    if first:
        args.append(context)
        outs.append(jax.ShapeDtypeStruct((heads, rows), F32))
    else:
        args += carried
    if last:
        outs.append(jax.ShapeDtypeStruct((rows, width), BF16))
    else:
        outs.append(jax.ShapeDtypeStruct(dq_shape, F32))
    specs = [whole(a.shape) for a in args]
    specs[1] = kv_spec
    return pl.pallas_call(
        functools.partial(attend_back_kernel, target, block, block, first, last),
        grid=(1,),
        out_shape=tuple(outs),
        in_specs=specs,
        out_specs=tuple(whole(o.shape) for o in outs),
        scratch_shapes=[pltpu.VMEM(dq_shape[1:], F32), pltpu.VMEM((span, 2 * head), F32)],
        compiler_params=pltpu.CompilerParams(vmem_limit_bytes=48 << 20),
        cost_estimate=pl.CostEstimate(
            flops=20 * rows * rows * width, bytes_accessed=12 << 20, transcendentals=0
        ),
        name=f"attend_back{target}",
    )(*args)


def layer_norm(values, norm_gain, norm_bias):
    average = jnp.mean(values, axis=-1, keepdims=True)
    centred = values - average
    variance = jnp.mean(centred * centred, axis=-1, keepdims=True)
    return centred * lax.rsqrt(variance + EPSILON) * norm_gain + norm_bias


def gelu_tanh(values):
    return jax.nn.gelu(values, approximate=True)


def per_device(
    inputs,
    first_gain,
    first_bias,
    query_weight,
    query_bias,
    keyval_weight,
    value_bias,
    output_weight,
    output_bias,
    second_gain,
    second_bias,
    up_weight,
    up_bias,
    down_weight,
    down_bias,
    cotangent,
):
    count = lax.axis_size("dp")
    head_size = value_bias.shape[0]
    score_scale = head_size ** (-0.5)
    x_full = inputs.astype(F32)
    normed1_full, first_pull = jax.vjp(layer_norm, x_full, first_gain, first_bias)
    normed1 = normed1_full.astype(BF16)
    query_pre = jnp.dot(normed1, query_weight, preferred_element_type=F32) + query_bias
    queries = (query_pre * score_scale).astype(BF16)
    kv_bias = jnp.concatenate([jnp.zeros_like(value_bias), value_bias])
    keyval = (jnp.dot(normed1, keyval_weight, preferred_element_type=F32) + kv_bias).astype(BF16)
    keyval_all = gather_keyval(keyval)
    context_low, lse = attend(queries, keyval_all)
    attn_sum, d_activ = project(context_low, output_weight, cotangent, down_weight)
    middle = x_full + attn_sum.astype(F32) + output_bias
    normed2_full, second_pull = jax.vjp(layer_norm, middle, second_gain, second_bias)
    normed2 = normed2_full.astype(BF16)
    pre_act = jnp.dot(normed2, up_weight, preferred_element_type=F32) + up_bias
    act_full, gelu_pull = jax.vjp(gelu_tanh, pre_act)
    activ = act_full.astype(BF16)
    grad_full = cotangent.astype(F32)
    d_pre = gelu_pull(d_activ.astype(F32))[0].astype(BF16)
    own, other = weight_grad(cotangent, activ, count)
    d_normed2, up_own, up_other, arrived = hidden_back(d_pre, up_weight, normed2, other, count)
    scatter_down = ScatterSum(own, other, arrived)
    up_other, d_normed2 = together(up_other, d_normed2)
    scatter_up = ScatterSum(up_own, up_other)
    d_up_bias = jnp.sum(d_pre.astype(F32), axis=0)
    d_down_bias = jnp.sum(grad_full, axis=0)
    d_middle_norm, d_second_gain, d_second_bias = second_pull(d_normed2.astype(F32))
    d_middle = grad_full + d_middle_norm
    d_output_bias = jnp.sum(d_middle, axis=0)
    d_middle_low = d_middle.astype(BF16)
    d_context = contract(d_middle_low, output_weight, 1, 1).astype(BF16)
    mlp_part = jnp.dot(activ, down_weight, preferred_element_type=F32).astype(BF16)
    mlp_part, d_context = together(mlp_part, d_context)
    mlp_sum, mlp_y = layer_sum(mlp_part)
    grad_out_own, grad_out_other = weight_grad(d_middle_low, context_low, count)
    grad_out_other, d_context = together(grad_out_other, d_context)
    scatter_out = ScatterSum(grad_out_own, grad_out_other)

    d_kv_parts = []
    carried = None
    levels = SPAN // 2
    for target in range(levels):
        (d_context,) = scatter_down.step(d_context)
        if target >= 1:
            (d_context,) = scatter_out.step(d_context)
        results = attend_back(target, queries, keyval_all, d_context, lse, context_low, carried)
        if target == 0:
            d_kv, delta, dq = results
        else:
            d_kv, dq = results
        d_kv_parts.append(d_kv)
        carried = [delta, dq]
        dq, d_context = together(dq, d_context)
        carried = [delta, dq]
    d_queries = dq
    scatter_down.finish()
    scatter_out.finish()
    (d_queries,) = scatter_up.step(d_queries)
    d_query_bias = jnp.sum(d_queries.astype(F32), axis=0)
    d_normed1_sum, sent_query, d_keyval = query_back(
        d_queries, query_weight, normed1, d_kv_parts, count
    )
    (d_keyval,) = scatter_up.step(d_keyval)
    layer_out = (
        middle + layer_join(mlp_sum, mlp_y).astype(F32) + down_bias
    ).astype(BF16)
    d_value_bias = jnp.sum(d_keyval[:, head_size:].astype(F32), axis=0)
    d_normed1 = d_normed1_sum.astype(F32) + contract(d_keyval, keyval_weight, 1, 1)
    d_x_norm, d_first_gain, d_first_bias = first_pull(d_normed1)
    grad_inputs = d_middle + d_x_norm
    scatter_up.finish()
    sent_kv, sums = last_sums(
        normed1,
        d_keyval,
        [
            d_first_gain,
            d_first_bias,
            d_query_bias,
            d_value_bias,
            d_output_bias,
            d_second_gain,
            d_second_bias,
            d_up_bias,
            d_down_bias,
        ],
        count,
    )
    return (
        layer_out,
        grad_inputs,
        sums[0],
        sums[1],
        sent_query,
        sums[2],
        sent_kv,
        sums[3],
        scatter_out.result.T,
        sums[4],
        sums[5],
        sums[6],
        scatter_up.result,
        sums[7],
        scatter_down.result.T,
        sums[8],
    )


def solution(mesh):
    in_specs = (
        P("dp", None),
        P(),
        P(),
        P(None, "tensor"),
        P("tensor"),
        P(),
        P(),
        P("tensor", None),
        P(),
        P(),
        P(),
        P(None, "tensor"),
        P("tensor"),
        P("tensor", None),
        P(),
        P("dp", None),
    )
    out_specs = (
        P("dp", None),
        P("dp", None),
        P(),
        P(),
        P("dp", "tensor"),
        P("tensor"),
        P("dp", None),
        P(),
        P("tensor", "dp"),
        P(),
        P(),
        P(),
        P("dp", "tensor"),
        P("tensor"),
        P("tensor", "dp"),
        P(),
    )
    return jax.shard_map(
        per_device, mesh=mesh, in_specs=in_specs, out_specs=out_specs, check_vma=False
    )
```

```python
import functools

import jax
import jax.numpy as jnp
from jax import lax
from jax.experimental import pallas as pl
from jax.experimental.pallas import tpu as pltpu
from jax.sharding import PartitionSpec as P

SPAN = 8
EPSILON = 1e-05
NEG_LARGE = -1e30
MESH = pl.DeviceIdType.MESH
VMEM = pl.BlockSpec(memory_space=pltpu.VMEM)
F32 = jnp.float32
BF16 = jnp.bfloat16


def contract(left, right, left_dim, right_dim):
    return lax.dot_general(
        left, right, (((left_dim,), (right_dim,)), ((), ())), preferred_element_type=F32
    )


def remote(source, target, send_sem, recv_sem, device):
    return pltpu.make_async_remote_copy(
        src_ref=source,
        dst_ref=target,
        send_sem=send_sem,
        recv_sem=recv_sem,
        device_id=device,
        device_id_type=MESH,
    )


def greet(devices):
    barrier = pltpu.get_barrier_semaphore()
    for device in devices:
        pl.semaphore_signal(barrier, inc=1, device_id=device, device_id_type=MESH)
    pl.semaphore_wait(barrier, len(devices))


class TensorSum:
    def __init__(self, chunks, part, result, from_core, summed, from_y, sems):
        block = lax.axis_index("dp")
        lane = lax.axis_index("tensor")
        core = lax.rem(lane, 2)
        self.core_peer = (block, lane + 1 - 2 * core)
        self.y_peer = (block, lax.rem(lane + 2, 4))
        rows, width = part.shape
        half = width // 2
        self.step = rows // chunks
        self.mine = pl.ds(pl.multiple_of(core * half, half), half)
        self.other = pl.ds(pl.multiple_of((1 - core) * half, half), half)
        self.part, self.result = part, result
        self.from_core, self.summed, self.from_y = from_core, summed, from_y
        self.sems = sems

    def span(self, k):
        return pl.ds(pl.multiple_of(k * self.step, self.step), self.step)

    def to_core(self, k):
        at = self.span(k)
        return remote(
            self.part.at[at, self.other], self.from_core.at[at], self.sems[0].at[k],
            self.sems[1].at[k], self.core_peer,
        )

    def to_y(self, k):
        at = self.span(k)
        return remote(
            self.summed.at[at], self.from_y.at[at], self.sems[2].at[k], self.sems[3].at[k],
            self.y_peer,
        )

    def back(self, k):
        at = self.span(k)
        return remote(
            self.result.at[at, self.mine], self.result.at[at, self.mine], self.sems[4].at[k],
            self.sems[5].at[k], self.core_peer,
        )

    def first(self, k):
        self.to_core(k).start()

    def second(self, k):
        at = self.span(k)
        self.to_core(k).wait_recv()
        total = self.part[at, self.mine].astype(F32) + self.from_core[at].astype(F32)
        self.summed[at] = total.astype(BF16)
        self.to_y(k).start()

    def third(self, k):
        at = self.span(k)
        self.to_y(k).wait_recv()
        total = self.summed[at].astype(F32) + self.from_y[at].astype(F32)
        self.result[at, self.mine] = total.astype(BF16)
        self.back(k).start()

    def finish(self, chunks):
        @pl.loop(0, chunks)
        def _(k):
            self.back(k).wait_recv()
            self.back(k).wait_send()
            self.to_core(k).wait_send()
            self.to_y(k).wait_send()


def sum_scratch(chunks, rows, width):
    half = pltpu.VMEM((rows, width // 2), BF16)
    return [pltpu.VMEM((rows, width), BF16), half, half, half] + [
        pltpu.SemaphoreType.DMA((chunks,))
    ] * 6


def grad_rows(left_ref, right, target, which):
    levels, rows = target.shape[0], target.shape[1]

    @pl.loop(0, levels)
    def _(lev):
        if rows % 128 == 0:
            cols = pl.ds(pl.multiple_of((2 * lev + which) * rows, rows), rows)
            target[lev] = contract(left_ref[:, cols], right[...], 0, 0).astype(BF16)
        else:
            cols = pl.ds(pl.multiple_of(2 * lev * rows, 2 * rows), 2 * rows)
            both = contract(left_ref[:, cols], right[...], 0, 0)
            target[lev] = jnp.where(which == 0, both[:rows], both[rows:]).astype(BF16)


def hidden_back_kernel(
    chunks, dpre_ref, wu_ref, n2_ref, activ_ref, cot_ref, far_ref, dn_ref, own_ref, other_ref, down_ref, got_ref,
    activ_x, x_send, x_recv, part, from_core, summed, from_y, *sems,
):
    ts = TensorSum(chunks, part, dn_ref, from_core, summed, from_y, sems)
    side = lax.rem(lax.axis_index("dp"), 2)
    x_peer = (lax.axis_index("dp") + 1 - 2 * side, lax.axis_index("tensor"))
    greet([ts.core_peer, ts.y_peer, x_peer])
    half = activ_x.shape[1]
    mine = pl.ds(pl.multiple_of(side * half, half), half)
    theirs = pl.ds(pl.multiple_of((1 - side) * half, half), half)
    to_x = remote(activ_ref.at[:, theirs], activ_x, x_send.at[0], x_recv.at[0], x_peer)
    to_x.start()

    @pl.loop(0, chunks)
    def _(k):
        at = ts.span(k)
        part[at, :] = contract(dpre_ref[at, :], wu_ref[...], 1, 1).astype(BF16)
        ts.first(k)

        @pl.when(k >= 1)
        def _():
            ts.second(k - 1)

    ts.second(chunks - 1)
    grad_rows(n2_ref, dpre_ref, other_ref, 1 - side)
    rest = remote(
        other_ref.at[pl.ds(0, got_ref.shape[0])], got_ref, x_send.at[1], x_recv.at[1], x_peer
    )
    rest.start()
    grad_rows(n2_ref, dpre_ref, own_ref, side)
    levels, rows = down_ref.shape[0], down_ref.shape[1]

    @pl.loop(0, levels)
    def _(lev):
        cols = pl.ds(pl.multiple_of(lev * rows, rows), rows)
        down_ref[lev] = contract(cot_ref[:, cols], activ_ref[:, mine], 0, 0).astype(BF16)

    ready = chunks // 2

    @pl.loop(0, ready)
    def _(k):
        ts.third(k)

    to_x.wait_recv()

    @pl.loop(0, levels)
    def _(lev):
        cols = pl.ds(pl.multiple_of(lev * rows, rows), rows)
        far = contract(far_ref[:, cols], activ_x[...], 0, 0)
        down_ref[lev] = (down_ref[lev].astype(F32) + far).astype(BF16)

    @pl.loop(ready, chunks)
    def _(k):
        ts.third(k)

    ts.finish(chunks)
    to_x.wait_send()
    rest.wait()


def hidden_back(d_pre, up_weight, normed2, activ, cotangent, far_cotangent, count, chunks=4):
    rows, width = d_pre.shape[0], up_weight.shape[0]
    hidden = up_weight.shape[1]
    levels = count // 2
    half = jax.ShapeDtypeStruct((levels, width // count, hidden), BF16)
    got = jax.ShapeDtypeStruct((levels // 4, width // count, hidden), BF16)
    hbm = pl.BlockSpec(memory_space=pl.ANY)
    dma = pltpu.SemaphoreType.DMA
    return pl.pallas_call(
        functools.partial(hidden_back_kernel, chunks),
        out_shape=(
            jax.ShapeDtypeStruct((rows, width), BF16),
            half,
            half,
            jax.ShapeDtypeStruct((levels, width // levels, hidden // 2), BF16),
            got,
        ),
        in_specs=[VMEM] * 6,
        out_specs=(VMEM,) * 4 + (hbm,),
        scratch_shapes=[pltpu.VMEM((rows, hidden // 2), BF16), dma((2,)), dma((2,))]
        + sum_scratch(chunks, rows, width),
        compiler_params=pltpu.CompilerParams(
            collective_id=4, has_side_effects=True, vmem_limit_bytes=62 << 20
        ),
        name="hidden_back",
    )(d_pre, up_weight, normed2, activ, cotangent, far_cotangent)


class Chain:
    def __init__(self, length, level, upper, lower, pair, bufs, sems):
        self.length, self.level = length, level
        self.peers = (upper, lower)
        self.pair = pair
        self.bufs = bufs
        self.sems = sems

    def copy(self, way, s):
        inward, outward = self.bufs[2 * way], self.bufs[2 * way + 1]
        send, recv = self.sems[2 * way], self.sems[2 * way + 1]
        return remote(
            outward.at[s - 1], inward.at[s - 1], send.at[s - 1], recv.at[s - 1], self.peers[way]
        )

    def rank(self, way):
        return self.level if way == 0 else self.length - 1 - self.level

    def start(self, s):
        for way in range(2):
            rank = self.rank(way)
            slot = rank + self.length - s
            slot = jnp.clip(slot if way == 0 else self.length - 1 - slot, 0, self.length - 1)
            inward, outward = self.bufs[2 * way], self.bufs[2 * way + 1]

            @pl.when(rank <= s - 1)
            def _(way=way, rank=rank, slot=slot, inward=inward, outward=outward):
                outward[s - 1] = self.pair[slot]
                if s > 1:
                    @pl.when(rank >= 1)
                    def _():
                        outward[s - 1] = (
                            self.pair[slot].astype(F32) + inward[s - 2].astype(F32)
                        ).astype(BF16)

                self.copy(way, s).start()

    def arrive(self, s):
        for way in range(2):
            rank = self.rank(way)

            @pl.when((rank >= 1) & (rank <= s))
            def _(way=way):
                self.copy(way, s).wait_recv()

    def result(self, target):
        last = self.length - 2
        target[...] = self.pair[self.level].astype(F32)
        for way in range(2):
            @pl.when(self.rank(way) >= 1)
            def _(way=way):
                target[...] += self.bufs[2 * way][last].astype(F32)

    def drain(self, last=None):
        for s in range(1, (last or self.length - 1) + 1):
            for way in range(2):
                rank = self.rank(way)

                @pl.when(rank <= s - 1)
                def _(way=way, s=s):
                    self.copy(way, s).wait_send()


def chain_scratch(length, shape):
    return [pltpu.VMEM((length - 1,) + shape, BF16)] * 4 + [
        pltpu.SemaphoreType.DMA((length - 1,))
    ] * 4


def chain_peers():
    count = lax.axis_size("dp")
    block = lax.axis_index("dp")
    lane = lax.axis_index("tensor")
    level = block // 2
    upper = (jnp.where(level < count // 2 - 1, block + 2, block + 2 - count), lane)
    lower = (jnp.where(level > 0, block - 2, block - 2 + count), lane)
    return count // 2, level, upper, lower


def query_back_kernel(
    chunks, steps, dq_ref, wq_ref, n1_ref, dkv_ref, wide_ref, down_ref, dn_ref, grad_ref, tot_ref,
    far_up, far_down, down_out, d_send, d_recv, down_low, down_got,
    part, from_core, summed, from_y, kv_core, kv_sum, kv_x, kv_pair, kv_z, kv_up, kv_y, kv_sems, own_ref,
    other_ref, got_ref, q_send, q_recv, *rest,
):
    chain_bufs, chain_sems, sems = rest[:4], rest[4:8], rest[8:14]
    wide_bufs, wide_sems = rest[14:18], rest[18:]
    ts = TensorSum(chunks, part, dn_ref, from_core, summed, from_y, sems)
    block = lax.axis_index("dp")
    lane = lax.axis_index("tensor")
    place = lax.rem(block, SPAN)
    side = lax.rem(place, 2)
    level = place // 2
    levels = SPAN // 2
    x_peer = (block + 1 - 2 * side, lane)
    upper = (jnp.where(level < levels - 1, block + 2, block + 2 - SPAN), lane)
    lower = (jnp.where(level > 0, block - 2, block - 2 + SPAN), lane)
    length, chain_level, chain_upper, chain_lower = chain_peers()
    if length == levels:
        greet([ts.core_peer, ts.y_peer, x_peer, upper, lower])
    else:
        greet([ts.core_peer, ts.y_peer, x_peer, upper, lower, chain_upper, chain_lower])
    chain = Chain(length, chain_level, chain_upper, chain_lower, own_ref, chain_bufs, chain_sems)
    wide = Chain(length, chain_level, chain_upper, chain_lower, wide_ref, wide_bufs, wide_sems)
    core = lax.rem(lane, 2)
    seq_rows = tot_ref.shape[0]
    half = seq_rows // 2
    mine = pl.ds(pl.multiple_of(core * half, half), half)
    other = pl.ds(pl.multiple_of((1 - core) * half, half), half)

    def kv_copy(source, target, index, device):
        return remote(source, target, kv_sems.at[0, index], kv_sems.at[1, index], device)

    to_core = [
        kv_copy(
            dkv_ref.at[pl.ds(2 * lev, 2), other], kv_core.at[lev], 3 + levels + lev, ts.core_peer
        )
        for lev in range(levels)
    ]
    for copy in to_core:
        copy.start()
    grad_levels, rows = own_ref.shape[0], own_ref.shape[1]

    @pl.loop(0, chunks)
    def _(k):
        at = ts.span(k)
        part[at, :] = contract(dq_ref[at, :], wq_ref[...], 1, 1).astype(BF16)
        ts.first(k)

        @pl.when(k >= 1)
        def _():
            ts.second(k - 1)

    ts.second(chunks - 1)
    for lev in range(levels):
        to_core[lev].wait_recv()
        total = dkv_ref[pl.ds(2 * lev, 2), mine].astype(F32) + kv_core[lev].astype(F32)
        kv_sum[lev] = total.astype(BF16)

    to_x = kv_copy(kv_sum.at[:, 1 - side], kv_x, 1, x_peer)
    to_x.start()
    wide.start(1)

    def grad(target, which):
        grad_rows(n1_ref, dq_ref, target, which)

    grad(other_ref, 1 - side)
    q_to_x = remote(other_ref, got_ref, q_send, q_recv, x_peer)
    grad(own_ref, side)
    half_rows, half_cols = down_low.shape
    down_mine = pl.ds(pl.multiple_of(side * half_rows, half_rows), half_rows)
    down_theirs = pl.ds(pl.multiple_of((1 - side) * half_rows, half_rows), half_rows)
    down_low[...] = down_ref[down_theirs].astype(BF16)
    to_x.wait_recv()
    q_to_x.start()
    d_to_x = remote(down_low, down_got, d_send, d_recv, x_peer)
    d_to_x.start()

    @pl.loop(0, levels)
    def _(lev):
        kv_pair[lev] = (kv_sum[lev, side].astype(F32) + kv_x[lev].astype(F32)).astype(BF16)

    def down(s):
        slot = jnp.maximum(level - levels + s, 0)
        return kv_copy(kv_up.at[s - 1], kv_z.at[s - 1], 1 + s, lower), slot

    for s in range(1, levels):
        copy, slot = down(s)

        @pl.when(level >= levels - s)
        def _(copy=copy, slot=slot, s=s):
            kv_up[s - 1] = kv_pair[slot]
            if s > 1:
                @pl.when(level < levels - 1)
                def _():
                    kv_up[s - 1] = (
                        kv_pair[slot].astype(F32) + kv_z[s - 2].astype(F32)
                    ).astype(BF16)

            copy.start()

        @pl.when((level >= levels - 1 - s) & (level < levels - 1))
        def _(copy=copy):
            copy.wait_recv()

    kv_up[levels - 1] = kv_pair[level]

    @pl.when(level < levels - 1)
    def _():
        kv_up[levels - 1] = (
            kv_pair[level].astype(F32) + kv_z[levels - 2].astype(F32)
        ).astype(BF16)

    to_y = kv_copy(kv_up.at[levels - 1], kv_y, 1 + levels, ts.y_peer)
    to_y.start()
    for s in range(1, steps):
        wide.arrive(s)
        wide.start(s + 1)
    q_to_x.wait_recv()

    @pl.loop(0, grad_levels)
    def _(lev):
        own_ref[lev] = (own_ref[lev].astype(F32) + got_ref[lev].astype(F32)).astype(BF16)

    chain.start(1)
    to_y.wait_recv()
    tot_ref[mine] = (kv_up[levels - 1].astype(F32) + kv_y[...].astype(F32)).astype(BF16)
    back = kv_copy(tot_ref.at[mine], tot_ref.at[mine], 2 + levels, ts.core_peer)
    back.start()
    half_way = chunks // 2
    for s in range(1, length):
        if s == 2:
            @pl.loop(0, half_way)
            def _(k):
                ts.third(k)

        chain.arrive(s)
        if s + 1 < length:
            chain.start(s + 1)

    @pl.loop(half_way, chunks)
    def _(k):
        ts.third(k)

    chain.result(grad_ref)
    d_to_x.wait()
    first = pl.ds(pl.multiple_of(side * half_cols, half_cols), half_cols)
    second = pl.ds(pl.multiple_of((1 - side) * half_cols, half_cols), half_cols)
    down_out[:, first] = down_ref[down_mine]
    down_out[:, second] = down_got[...].astype(F32)
    wide.arrive(steps)
    far_up[...] = wide.bufs[0][steps - 1]
    far_down[...] = wide.bufs[2][steps - 1]
    chain.drain()
    wide.drain(steps)
    q_to_x.wait_send()
    back.wait()
    for copy in to_core:
        copy.wait_send()
    to_x.wait_send()
    to_y.wait_send()
    for s in range(1, levels):
        copy, _slot = down(s)

        @pl.when(level >= levels - s)
        def _(copy=copy):
            copy.wait_send()

    ts.finish(chunks)


def query_back(d_queries, query_weight, normed1, parts, wide, down, count, chunks=4):
    rows, width = d_queries.shape[0], query_weight.shape[0]
    kv_width = parts.shape[2]
    steps = count // 2 - 2
    levels = SPAN // 2
    shape = (width // count, query_weight.shape[1])
    half = pltpu.VMEM((count // 2,) + shape, BF16)
    piece = (rows // 2, kv_width)
    return pl.pallas_call(
        functools.partial(query_back_kernel, chunks, steps),
        out_shape=(
            jax.ShapeDtypeStruct((rows, width), BF16),
            jax.ShapeDtypeStruct(shape, F32),
            jax.ShapeDtypeStruct((rows, kv_width), BF16),
            jax.ShapeDtypeStruct(wide.shape[1:], BF16),
            jax.ShapeDtypeStruct(wide.shape[1:], BF16),
            jax.ShapeDtypeStruct((down.shape[0] // 2, 2 * down.shape[1]), F32),
        ),
        in_specs=[VMEM] * 6,
        out_specs=(VMEM,) * 6,
        scratch_shapes=[
            pltpu.SemaphoreType.DMA,
            pltpu.SemaphoreType.DMA,
            pltpu.VMEM((down.shape[0] // 2, down.shape[1]), BF16),
            pltpu.VMEM((down.shape[0] // 2, down.shape[1]), BF16),
        ]
        + sum_scratch(chunks, rows, width)[:4]
        + [
            pltpu.VMEM((levels, 2) + piece, BF16),
            pltpu.VMEM((levels, 2) + piece, BF16),
            pltpu.VMEM((levels,) + piece, BF16),
            pltpu.VMEM((levels,) + piece, BF16),
            pltpu.VMEM((levels - 1,) + piece, BF16),
            pltpu.VMEM((levels,) + piece, BF16),
            pltpu.VMEM(piece, BF16),
            pltpu.SemaphoreType.DMA((2, 3 + 2 * levels)),
            half,
            half,
            half,
            pltpu.SemaphoreType.DMA,
            pltpu.SemaphoreType.DMA,
        ]
        + chain_scratch(count // 2, shape)
        + [pltpu.SemaphoreType.DMA((chunks,))] * 6
        + chain_scratch(steps + 1, wide.shape[1:]),
        compiler_params=pltpu.CompilerParams(
            collective_id=5, has_side_effects=True, vmem_limit_bytes=63 << 20
        ),
        name="query_back",
    )(d_queries, query_weight, normed1, parts, wide, down)


def finish_kernel(
    chunk, n1_ref, dkv_ref, wkv_ref, dn_ref, x_ref, dm_ref, gain_ref, vec_in, ends_ref, far_up, far_down,
    grad_x, grad_ref, vec_ref, up_ref, up_out, up_in, up_send, up_recv, own_ref, other_ref, got_ref,
    x_send, x_recv, own_vec, low_vec, slots, send, recv, acc, *chain_refs,
):
    block = lax.axis_index("dp")
    lane = lax.axis_index("tensor")
    count = lax.axis_size("dp")
    side = lax.rem(block, 2)
    pairs = count // 2
    others = [(lax.rem(block + 2 * k, count), lane) for k in range(1, pairs)]
    x_peer = (block + 1 - 2 * side, lane)
    greet([x_peer] + others)
    length, level, upper, lower = chain_peers()

    def last(way):
        return remote(
            up_out.at[way], up_in.at[way], up_send.at[way], up_recv.at[way], (upper, lower)[way]
        )

    ranks = (level, length - 1 - level)
    grad_rows(n1_ref, dkv_ref, other_ref, 1 - side)
    to_x = remote(other_ref, got_ref, x_send, x_recv, x_peer)
    to_x.start()
    for way, far in enumerate((far_up, far_down)):
        @pl.when(ranks[way] < length - 1)
        def _(way=way, far=far):
            up_out[way] = ends_ref[1 + way]

            @pl.when(ranks[way] >= 1)
            def _():
                up_out[way] = (ends_ref[1 + way].astype(F32) + far[...].astype(F32)).astype(BF16)

            last(way).start()

    grad_rows(n1_ref, dkv_ref, own_ref, side)
    rows, width = x_ref.shape
    acc[...] = jnp.zeros_like(acc)

    def norm_back(k):
        at = pl.ds(pl.multiple_of(k * chunk, chunk), chunk)
        values = x_ref[at, :].astype(F32)
        centred = values - jnp.mean(values, axis=-1, keepdims=True)
        scale = lax.rsqrt(jnp.mean(centred * centred, axis=-1, keepdims=True) + EPSILON)
        hat = centred * scale
        grad = dn_ref[at, :].astype(F32) + contract(dkv_ref[at, :], wkv_ref[...], 1, 1)
        acc[0] += jnp.sum((grad * hat).reshape(chunk // 8, 8, width), axis=0)
        acc[1] += jnp.sum(grad.reshape(chunk // 8, 8, width), axis=0)
        scaled = grad * gain_ref[...]
        first = jnp.mean(scaled, axis=-1, keepdims=True)
        second = jnp.mean(scaled * hat, axis=-1, keepdims=True)
        grad_x[at, :] = dm_ref[at, :].astype(F32) + scale * (scaled - first - hat * second)

    chain = Chain(length, level, upper, lower, own_ref, chain_refs[:4], chain_refs[4:8])
    chunks = rows // chunk
    half = chunks // 2

    @pl.loop(0, half)
    def _(k):
        norm_back(k)

    to_x.wait_recv()
    own_ref[...] = (own_ref[...].astype(F32) + got_ref[...].astype(F32)).astype(BF16)
    chain.start(1)

    @pl.loop(half, chunks)
    def _(k):
        norm_back(k)

    own_vec[...] = vec_in[...]
    own_vec[0:1, :] = jnp.sum(acc[0], axis=0, keepdims=True)
    own_vec[1:2, :] = jnp.sum(acc[1], axis=0, keepdims=True)
    head = dkv_ref.shape[1] // 2
    own_vec[2:3, 0:head] = jnp.sum(dkv_ref[:, head:].astype(F32), axis=0, keepdims=True)
    low_vec[0] = own_vec[...].astype(BF16)
    to_pair = remote(low_vec.at[0], slots.at[0], send.at[0], recv.at[0], x_peer)
    to_pair.start()
    chain.arrive(1)
    if length > 2:
        chain.start(2)
    to_pair.wait()
    own_vec[...] += slots[0].astype(F32)
    low_vec[1] = own_vec[...].astype(BF16)
    copies = []
    for k in range(1, pairs):
        copy = remote(low_vec.at[1], slots.at[k], send.at[k], recv.at[k], others[k - 1])
        copy.start()
        copies.append(copy)
    for s in range(2, length):
        chain.arrive(s)
        if s + 1 < length:
            chain.start(s + 1)
    chain.result(grad_ref)
    total = own_vec[...]
    for k in range(1, pairs):
        copies[k - 1].wait()
        total = total + slots[k].astype(F32)
    vec_ref[...] = total
    up_ref[...] = ends_ref[0].astype(F32)
    for way in range(2):
        @pl.when(ranks[way] >= 1)
        def _(way=way):
            last(way).wait_recv()
            up_ref[...] += up_in[way].astype(F32)

        @pl.when(ranks[way] < length - 1)
        def _(way=way):
            last(way).wait_send()

    chain.drain()
    to_x.wait_send()


def finish(
    normed1, d_keyval, keyval_weight, d_normed1, inputs, d_middle, gain, values, ends, far_up, far_down, count,
    chunk=128,
):
    rows, width = inputs.shape
    flat = jnp.concatenate(values)
    lines = -(-flat.shape[0] // width)
    height = -(-(3 + lines) // 8) * 8
    packed = jnp.pad(flat, (3 * width, (height - 3) * width - flat.shape[0])).reshape(height, width)
    shape = (width // count, d_keyval.shape[1])
    half = pltpu.VMEM((count // 2,) + shape, BF16)
    dma = pltpu.SemaphoreType.DMA
    two = pltpu.VMEM((2,) + far_up.shape, BF16)
    grad_x, grad, total, wide = pl.pallas_call(
        functools.partial(finish_kernel, chunk),
        out_shape=(
            jax.ShapeDtypeStruct((rows, width), F32),
            jax.ShapeDtypeStruct(shape, F32),
            jax.ShapeDtypeStruct((height, width), F32),
            jax.ShapeDtypeStruct(far_up.shape, F32),
        ),
        in_specs=[VMEM] * 11,
        out_specs=(VMEM,) * 4,
        scratch_shapes=[two, two, dma((2,)), dma((2,)), half, half, half, dma, dma]
        + [
            pltpu.VMEM((height, width), F32),
            pltpu.VMEM((2, height, width), BF16),
            pltpu.VMEM((count // 2, height, width), BF16),
            dma((count // 2,)),
            dma((count // 2,)),
            pltpu.VMEM((2, 8, width), F32),
        ]
        + chain_scratch(count // 2, shape),
        compiler_params=pltpu.CompilerParams(
            collective_id=2, has_side_effects=True, vmem_limit_bytes=56 << 20
        ),
        name="finish",
    )(
        normed1, d_keyval, keyval_weight, d_normed1, inputs, d_middle, gain.reshape(1, width), packed, ends,
        far_up, far_down,
    )
    flat = total[3:].reshape(-1)
    pieces = []
    start = 0
    for value in values:
        pieces.append(flat[start : start + value.shape[0]])
        start += value.shape[0]
    head = d_keyval.shape[1] // 2
    return grad_x, grad, total[0], total[1], total[2, :head], pieces, wide


def together(*values):
    return lax.optimization_barrier(values)


class ScatterSum:
    def __init__(self, own, other, arrived=None):
        self.count = lax.axis_size("dp")
        self.length = self.count // 2
        self.level = lax.axis_index("dp") // 2
        self.own = own
        if arrived is not None:
            other = other[arrived.shape[0] :]
        got = lax.ppermute(other, "dp", [(p, p ^ 1) for p in range(self.count)])
        if arrived is not None:
            got = jnp.concatenate([arrived, got], axis=0)
        self.flying = (got,)
        self.s = 0

    def shifted(self, value, sources, step):
        pairs = [
            (2 * source + side, 2 * (source + step) + side)
            for source in sources
            for side in range(2)
        ]
        return lax.ppermute(value, "dp", pairs)

    def slot(self, index):
        index = jnp.clip(index, 0, self.length - 1)
        return lax.dynamic_index_in_dim(self.total, index, 0, keepdims=False)

    def step(self, *values):
        length, level = self.length, self.level
        self.s += 1
        s = self.s
        if s == 1:
            self.total = (self.own.astype(F32) + self.flying[0].astype(F32)).astype(BF16)
            up, down = self.slot(level + length - 1), self.slot(level - length + 1)
        else:
            up, down = self.flying
            up = self.slot(level + length - s).astype(F32) + up.astype(F32)
            if s == length:
                self.result = up + down.astype(F32)
                return values
            down = self.slot(level - length + s).astype(F32) + down.astype(F32)
            up, down = up.astype(BF16), down.astype(BF16)
        up, down, *values = together(up, down, *values)
        self.flying = (
            self.shifted(up, range(0, s), 1),
            self.shifted(down, range(length - s, length), -1),
        )
        return values

    def finish(self):
        while self.s < self.length:
            self.step()
        return self.result


def weight_grad_kernel(left_ref, right_ref, own_ref, other_ref):
    side = lax.rem(lax.axis_index("dp"), 2)
    grad_rows(left_ref, right_ref, other_ref, 1 - side)
    grad_rows(left_ref, right_ref, own_ref, side)


def weight_grad(left, right, count):
    half = jax.ShapeDtypeStruct((count // 2, left.shape[1] // count, right.shape[1]), BF16)
    return pl.pallas_call(
        weight_grad_kernel,
        out_shape=(half, half),
        in_specs=[VMEM] * 2,
        out_specs=(VMEM,) * 2,
        compiler_params=pltpu.CompilerParams(vmem_limit_bytes=40 << 20),
        cost_estimate=pl.CostEstimate(
            flops=2 * left.shape[0] * left.shape[1] * right.shape[1],
            bytes_accessed=16 << 20,
            transcendentals=0,
        ),
        name="weight_grad",
    )(left, right)


def front_kernel(
    block, chunks, q_ref, own_kv, cot_hbm, wo_ref, wd_hbm, kv_ref, ctx_ref, lse_ref, sum_ref, g_ref, far_ref,
    cot_ref, wd_ref, local_sem, x_send, x_recv, z_send, z_recv, s_send, s_recv, f_send, f_recv, acc, peak, total,
    part, from_core, summed, from_y, *sems,
):
    ts = TensorSum(chunks, part, sum_ref, from_core, summed, from_y, sems)
    dp = lax.axis_index("dp")
    lane = lax.axis_index("tensor")
    place = lax.rem(dp, SPAN)
    side = lax.rem(place, 2)
    level = place // 2
    levels = SPAN // 2
    core = lax.rem(lane, 2)
    y_lane = lax.rem(lane + 2, 4)
    core_peer, y_peer = ts.core_peer, ts.y_peer
    x_peer = (dp + 1 - 2 * side, lane)
    upper = (jnp.where(level < levels - 1, dp + 2, dp + 2 - SPAN), lane)
    lower = (jnp.where(level > 0, dp - 2, dp - 2 + SPAN), lane)
    seq_rows = own_kv.shape[0]
    piece = seq_rows // 4
    head = kv_ref.shape[2] // 2
    heads = q_ref.shape[1] // head
    parts = seq_rows // block

    def rows_of(which):
        return pl.ds(pl.multiple_of(which * piece, piece), piece)

    local = [
        pltpu.make_async_copy(own_kv, kv_ref.at[place], local_sem.at[0]),
        pltpu.make_async_copy(cot_hbm, cot_ref, local_sem.at[1]),
        pltpu.make_async_copy(wd_hbm, wd_ref, local_sem.at[2]),
    ]
    local[0].start()
    greet([core_peer, y_peer, x_peer, upper, lower])
    to_x = remote(own_kv.at[rows_of(lane)], kv_ref.at[place, rows_of(lane)], x_send, x_recv, x_peer)
    to_x.start()
    far_pieces = f_send.shape[1]
    far_step = cot_hbm.shape[0] // (2 * far_pieces)

    def far(kind, k):
        start = pl.multiple_of((core * far_pieces + k) * far_step, far_step)
        source = cot_hbm if kind == 0 else far_ref
        return remote(
            source.at[pl.ds(start, far_step)], far_ref.at[pl.ds(start, far_step)], f_send.at[kind, k],
            f_recv.at[kind, k], x_peer if kind == 0 else core_peer,
        )

    def share(s, kind):
        at = rows_of(y_lane if kind == 2 else lane)
        ref = kv_ref.at[pl.ds(2 * (level - s), 2), at]
        return remote(
            ref, ref, s_send.at[s, kind], s_recv.at[s, kind], y_peer if kind == 0 else core_peer
        )

    def share_pair(kind):
        ref = kv_ref.at[place + 1 - 2 * side, rows_of(y_lane if kind == 2 else lane)]
        return remote(
            ref, ref, s_send.at[0, kind], s_recv.at[0, kind], y_peer if kind == 0 else core_peer
        )

    def up(s):
        ref = kv_ref.at[pl.ds(2 * (level - s), 2), rows_of(lane)]
        return remote(ref, ref, z_send.at[s], z_recv.at[s], upper)

    def from_below(s):
        ref = kv_ref.at[pl.ds(2 * (level - 1 - s), 2), rows_of(lane)]
        return remote(ref, ref, z_send.at[s], z_recv.at[s], upper)

    def forward(s):
        from_below(s - 1).wait_recv()

        @pl.when((s < levels - 1) & (level < levels - 1))
        def _():
            up(s).start()

        share(s, 0).start()
        share(s, 1).start()

    def score(i, h, at_block, at_row, diagonal):
        keys = kv_ref[at_block, pl.ds(at_row, block), 0:head]
        query = q_ref[i * block : (i + 1) * block, h * head : (h + 1) * head]
        scores = contract(keys, query, 1, 1)
        if diagonal:
            key_at = lax.broadcasted_iota(jnp.int32, scores.shape, 0)
            query_at = lax.broadcasted_iota(jnp.int32, scores.shape, 1)
            scores = jnp.where(key_at <= query_at, scores, NEG_LARGE)
        return scores

    def soften(i, h, scores):
        old = peak[i, h]
        new = jnp.maximum(old, jnp.max(scores, axis=0, keepdims=True))
        probs = jnp.exp(scores - new)
        fade = jnp.exp(old - new)
        total[i, h] = total[i, h] * fade + jnp.sum(probs, axis=0, keepdims=True)
        peak[i, h] = new
        return probs.astype(BF16), fade

    def weigh(i, h, at_block, at_row, probs, fade):
        values = kv_ref[at_block, pl.ds(at_row, block), head : 2 * head]
        acc[i, h] = acc[i, h] * fade + contract(values, probs, 0, 0)

    def attend(i, pieces):
        items = [(h, piece) for piece in pieces for h in range(heads)]
        scores = score(i, items[0][0], *items[0][1])
        waiting = None
        for n, (h, (at_block, at_row, _diagonal)) in enumerate(items):
            following = None
            if n + 1 < len(items):
                following = score(i, items[n + 1][0], *items[n + 1][1])
            probs, fade = soften(i, h, scores)
            if waiting is not None:
                weigh(i, *waiting)
            waiting = (h, at_block, at_row, probs, fade)
            scores = following
        weigh(i, *waiting)

    def attend_level(i, s):
        @pl.loop(0, 2)
        def _(b):
            attend(i, [(2 * (level - s) + b, n * block, False) for n in range(parts)])

    peak[...] = jnp.full_like(peak, NEG_LARGE)
    total[...] = jnp.zeros_like(total)
    acc[...] = jnp.zeros_like(acc)
    local[0].wait()
    for copy in local[1:]:
        copy.start()
    for k in range(far_pieces):
        far(0, k).start()
    to_x.wait_recv()

    @pl.when(level < levels - 1)
    def _():
        up(0).start()

    share_pair(0).start()
    share_pair(1).start()
    for i in range(parts):
        attend(i, [(place, n * block, n == i) for n in range(i + 1)])

    @pl.when(level >= 1)
    def _():
        forward(1)

    share_pair(0).wait_recv()
    share_pair(2).start()
    share_pair(1).wait_recv()
    share_pair(2).wait_recv()

    @pl.when(side == 1)
    def _():
        for i in range(parts):
            attend(i, [(place - 1, n * block, False) for n in range(parts)])

    def complete(i):
        span = slice(i * block, (i + 1) * block)
        for h in range(heads):
            context = acc[i, h] / total[i, h]
            ctx_ref[span, h * head : (h + 1) * head] = context.T.astype(BF16)
            lse_ref[h : h + 1, span] = peak[i, h] + jnp.log(total[i, h])
        each = chunks // parts
        first = i * each

        @pl.loop(first, first + each)
        def _(k):
            at = ts.span(k)
            part[at, :] = jnp.dot(
                ctx_ref[at, :], wo_ref[...], preferred_element_type=F32
            ).astype(BF16)
            ts.first(k)

        @pl.loop(first, first + each)
        def _(k):
            ts.second(k)

    @pl.loop(1, level + 1)
    def _(s):
        @pl.when(s < level)
        def _():
            forward(s + 1)

        share(s, 0).wait_recv()
        share(s, 2).start()
        share(s, 1).wait_recv()
        share(s, 2).wait_recv()
        attend_level(0, s)

    complete(0)
    for i in range(1, parts):
        @pl.loop(1, level + 1)
        def _(s, i=i):
            attend_level(i, s)

        complete(i)

    for k in range(far_pieces):
        far(0, k).wait_recv()
        far(1, k).start()
    ready = chunks - chunks // parts

    @pl.loop(0, ready)
    def _(k):
        ts.third(k)

    for copy in local[1:]:
        copy.wait()
    tile = g_ref.shape[1] // 8

    @pl.loop(0, 8)
    def _(j):
        cols = pl.ds(pl.multiple_of(j * tile, tile), tile)
        g_ref[:, cols] = contract(cot_ref[...], wd_ref[cols, :], 1, 1).astype(BF16)

    @pl.loop(ready, chunks)
    def _(k):
        ts.third(k)

    to_x.wait_send()

    @pl.when(level < levels - 1)
    def _():
        up(0).wait_send()

    for kind in range(3):
        share_pair(kind).wait_send()

    @pl.loop(1, level + 1)
    def _(s):
        for kind in range(3):
            share(s, kind).wait_send()

        @pl.when((s < levels - 1) & (level < levels - 1))
        def _():
            up(s).wait_send()

    for k in range(far_pieces):
        far(0, k).wait_send()
        far(1, k).wait()
    ts.finish(chunks)


def front(queries, keyval, cotangent, output_weight, down_weight, block=512, chunks=8):
    rows, width = queries.shape
    wide = output_weight.shape[1]
    hidden = down_weight.shape[0]
    head = keyval.shape[1] // 2
    heads = width // head
    levels = SPAN // 2
    dma = pltpu.SemaphoreType.DMA
    hbm = pl.BlockSpec(memory_space=pl.ANY)
    stat = pltpu.VMEM((rows // block, heads, 1, block), F32)
    return pl.pallas_call(
        functools.partial(front_kernel, block, chunks),
        out_shape=(
            jax.ShapeDtypeStruct((SPAN,) + keyval.shape, BF16),
            jax.ShapeDtypeStruct((rows, width), BF16),
            jax.ShapeDtypeStruct((heads, rows), F32),
            jax.ShapeDtypeStruct((rows, wide), BF16),
            jax.ShapeDtypeStruct((rows, hidden), BF16),
            jax.ShapeDtypeStruct(cotangent.shape, BF16),
        ),
        in_specs=[VMEM, VMEM, hbm, VMEM, hbm],
        out_specs=(VMEM,) * 5 + (hbm,),
        scratch_shapes=[
            pltpu.VMEM(cotangent.shape, BF16),
            pltpu.VMEM(down_weight.shape, BF16),
            dma((3,)),
            dma,
            dma,
            dma((levels - 1,)),
            dma((levels - 1,)),
            dma((levels, 3)),
            dma((levels, 3)),
            dma((2, 4)),
            dma((2, 4)),
            pltpu.VMEM((rows // block, heads, head, block), F32),
            stat,
            stat,
        ]
        + sum_scratch(chunks, rows, wide),
        compiler_params=pltpu.CompilerParams(
            collective_id=1, has_side_effects=True, vmem_limit_bytes=60 << 20
        ),
        name="front",
    )(queries, keyval, cotangent, output_weight, down_weight)


def attend_back_kernel(
    block, chunks, q_ref, kv_ref, do_ref, ctx_ref, lse_ref, pair_ref, mlp_ref, sent_ref, dq_ref, dkv_ref,
    grad_ref, out_ref, got_ref, dq_acc, dkv_acc, delta, x_send, x_recv, from_core, summed, from_y, *rest,
):
    sems, chain_refs = rest[:6], rest[6:]
    rows = q_ref.shape[0]
    head = kv_ref.shape[1] // 2
    heads = q_ref.shape[1] // head
    place = lax.rem(lax.axis_index("dp"), SPAN)
    side = lax.rem(lax.axis_index("dp"), 2)
    x_peer = (lax.axis_index("dp") + 1 - 2 * side, lax.axis_index("tensor"))
    ts = TensorSum(chunks, mlp_ref, out_ref, from_core, summed, from_y, sems)
    length, level, upper, lower = chain_peers()
    chain = Chain(length, level, upper, lower, pair_ref, chain_refs[:4], chain_refs[4:])
    greet([ts.core_peer, ts.y_peer, x_peer, upper, lower])
    left = got_ref.shape[0]
    to_x = remote(
        sent_ref.at[pl.ds(sent_ref.shape[0] - left, left)], got_ref, x_send, x_recv, x_peer
    )
    to_x.start()

    @pl.loop(0, chunks)
    def _(k):
        ts.first(k)

    chain.start(1)
    levels = SPAN // 2
    parts = 2 * rows // block
    per_slot = -(-(length - 1) // (levels - 1))
    done = 0
    for target in range(levels):
        dkv_acc[...] = jnp.zeros_like(dkv_acc)
        for i in range(rows // block):
            span = slice(i * block, (i + 1) * block)
            if target == 0:
                for h in range(heads):
                    cols = slice(h * head, (h + 1) * head)
                    product = do_ref[span, cols].astype(F32) * ctx_ref[span, cols].astype(F32)
                    delta[h : h + 1, span] = jnp.sum(product.T, axis=0, keepdims=True)
                dq_acc[i] = jnp.zeros_like(dq_acc[i])

            def step(j, diagonal, span=span, i=i):
                at = pl.ds(pl.multiple_of(j * block, block), block)
                kv_at = pl.ds(pl.multiple_of((target * parts + j) * block, block), block)
                keys = kv_ref[kv_at, 0:head]
                values = kv_ref[kv_at, head : 2 * head]
                d_keys = jnp.zeros((block, head), F32)
                d_values = jnp.zeros((block, head), F32)

                def begin(h):
                    cols = slice(h * head, (h + 1) * head)
                    scores = contract(keys, q_ref[span, cols], 1, 1)
                    if diagonal:
                        key_at = lax.broadcasted_iota(jnp.int32, scores.shape, 0)
                        query_at = lax.broadcasted_iota(jnp.int32, scores.shape, 1)
                        scores = jnp.where(key_at <= query_at, scores, NEG_LARGE)
                    return scores, contract(values, do_ref[span, cols], 1, 1)

                begun = begin(0)
                for h in range(heads):
                    cols = slice(h * head, (h + 1) * head)
                    scores, d_probs = begun
                    if h + 1 < heads:
                        begun = begin(h + 1)
                    probs = jnp.exp(scores - lse_ref[h : h + 1, span])
                    d_scores = (probs * (d_probs - delta[h : h + 1, span])).astype(BF16)
                    d_values += contract(probs.astype(BF16), do_ref[span, cols], 1, 0)
                    d_keys += contract(d_scores, q_ref[span, cols], 1, 0)
                    dq_acc[i, h] += contract(keys, d_scores, 0, 0)
                dkv_acc[at, 0:head] += d_keys
                dkv_acc[at, head : 2 * head] += d_values

            full = (place * rows + i * block) // block - target * parts

            @pl.loop(0, jnp.clip(full, 0, parts))
            def _(j):
                step(j, False)

            @pl.when((full >= 0) & (full < parts))
            def _():
                step(full, True)

            if target == 0 and i == 0:
                @pl.loop(0, chunks)
                def _(k):
                    ts.second(k)

        for b in range(2):
            dkv_ref[2 * target + b] = dkv_acc[b * rows : (b + 1) * rows].astype(BF16)
        if target < levels - 1:
            for _ in range(per_slot):
                if done < length - 1:
                    done += 1
                    chain.arrive(done)
                    if done < length - 1:
                        chain.start(done + 1)
            if done == length - 1:
                chain.result(grad_ref)
        if target == levels - 2:
            @pl.loop(0, chunks)
            def _(k):
                ts.third(k)

    for i in range(rows // block):
        span = slice(i * block, (i + 1) * block)
        for h in range(heads):
            dq_ref[span, h * head : (h + 1) * head] = (
                (dq_acc[i, h] * head**-0.5).T.astype(BF16)
            )
    chain.drain()
    ts.finish(chunks)
    to_x.wait()


def attend_back(queries, keyval, d_context, context, lse, pair, mlp_part, sent, block=512, chunks=4):
    rows, width = queries.shape
    head = keyval.shape[1] // 2
    heads = width // head
    hbm = pl.BlockSpec(memory_space=pl.ANY)
    dma = pltpu.SemaphoreType.DMA
    return pl.pallas_call(
        functools.partial(attend_back_kernel, block, chunks),
        out_shape=(
            jax.ShapeDtypeStruct((rows, width), BF16),
            jax.ShapeDtypeStruct((SPAN, rows, 2 * head), BF16),
            jax.ShapeDtypeStruct(pair.shape[1:], F32),
            jax.ShapeDtypeStruct(mlp_part.shape, BF16),
            jax.ShapeDtypeStruct((sent.shape[0] * 3 // 4,) + sent.shape[1:], BF16),
        ),
        in_specs=[VMEM] * 7 + [hbm],
        out_specs=(VMEM,) * 4 + (hbm,),
        scratch_shapes=[
            pltpu.VMEM((rows // block, heads, head, block), F32),
            pltpu.VMEM((2 * rows, 2 * head), F32),
            pltpu.VMEM((heads, rows), F32),
            dma,
            dma,
        ]
        + sum_scratch(chunks, *mlp_part.shape)[1:]
        + chain_scratch(*pair.shape[:1], pair.shape[1:]),
        compiler_params=pltpu.CompilerParams(
            collective_id=6, has_side_effects=True, vmem_limit_bytes=63 << 20
        ),
        name="attend_back",
    )(queries, keyval, d_context, context, lse, pair, mlp_part, sent)


def layer_norm(values, norm_gain, norm_bias):
    average = jnp.mean(values, axis=-1, keepdims=True)
    centred = values - average
    variance = jnp.mean(centred * centred, axis=-1, keepdims=True)
    return centred * lax.rsqrt(variance + EPSILON) * norm_gain + norm_bias


def gelu_tanh(values):
    return jax.nn.gelu(values, approximate=True)


def per_device(
    inputs,
    first_gain,
    first_bias,
    query_weight,
    query_bias,
    keyval_weight,
    value_bias,
    output_weight,
    output_bias,
    second_gain,
    second_bias,
    up_weight,
    up_bias,
    down_weight,
    down_bias,
    cotangent,
):
    count = lax.axis_size("dp")
    head_size = value_bias.shape[0]
    score_scale = head_size ** (-0.5)
    x_full = inputs.astype(F32)
    normed1 = layer_norm(x_full, first_gain, first_bias).astype(BF16)
    query_pre = jnp.dot(normed1, query_weight, preferred_element_type=F32) + query_bias
    queries = (query_pre * score_scale).astype(BF16)
    kv_bias = jnp.concatenate([jnp.zeros_like(value_bias), value_bias])
    keyval = (jnp.dot(normed1, keyval_weight, preferred_element_type=F32) + kv_bias).astype(BF16)
    keyval_all, context_low, lse, attn_sum, d_activ, far_cotangent = front(
        queries, keyval, cotangent, output_weight, down_weight
    )
    keyval_all = keyval_all.reshape(-1, keyval.shape[1])
    middle = x_full + attn_sum.astype(F32) + output_bias
    normed2_full, second_pull = jax.vjp(layer_norm, middle, second_gain, second_bias)
    normed2 = normed2_full.astype(BF16)
    pre_act = jnp.dot(normed2, up_weight, preferred_element_type=F32) + up_bias
    act_full, gelu_pull = jax.vjp(gelu_tanh, pre_act)
    activ = act_full.astype(BF16)
    grad_full = cotangent.astype(F32)
    d_pre = gelu_pull(d_activ.astype(F32))[0].astype(BF16)
    d_normed2, up_own, up_other, pair_down, arrived = hidden_back(
        d_pre, up_weight, normed2, activ, cotangent, far_cotangent, count
    )
    d_up_bias = jnp.sum(d_pre.astype(F32), axis=0)
    d_down_bias = jnp.sum(grad_full, axis=0)
    d_middle_norm, d_second_gain, d_second_bias = second_pull(d_normed2.astype(F32))
    d_middle = grad_full + d_middle_norm
    d_output_bias = jnp.sum(d_middle, axis=0)
    d_middle_low = d_middle.astype(BF16)
    d_context = contract(d_middle_low, output_weight, 1, 1).astype(BF16)
    mlp_part = jnp.dot(activ, down_weight, preferred_element_type=F32).astype(BF16)
    grad_out_own, grad_out_other = weight_grad(d_middle_low, context_low, count)
    scatter_out = ScatterSum(grad_out_own, grad_out_other)
    d_queries, d_kv_parts, half_down, mlp_sum, rest = attend_back(
        queries, keyval_all, d_context, context_low, lse, pair_down, mlp_part, up_other
    )
    arrived = jnp.concatenate([arrived, rest], axis=0)
    pair_up = (up_own.astype(F32) + arrived.astype(F32)).astype(BF16)
    scatter_out.finish()
    d_query_bias = jnp.sum(d_queries.astype(F32), axis=0)
    d_normed1_sum, sent_query, d_keyval, far_up, far_down, sent_down = query_back(
        d_queries, query_weight, normed1, d_kv_parts, pair_up, half_down, count
    )
    layer_out = (middle + mlp_sum.astype(F32) + down_bias).astype(BF16)
    level = lax.axis_index("dp") // 2
    ends = jnp.stack(
        [
            lax.dynamic_index_in_dim(pair_up, jnp.clip(level + k, 0, count // 2 - 1), 0, False)
            for k in (0, 1, -1)
        ]
    )
    grad_inputs, sent_kv, sum_gain, sum_bias, sum_value, sums, sent_up = finish(
        normed1,
        d_keyval,
        keyval_weight,
        d_normed1_sum,
        inputs,
        d_middle_low,
        first_gain,
        [d_up_bias, d_output_bias, d_second_gain, d_second_bias, d_down_bias, d_query_bias],
        ends,
        far_up,
        far_down,
        count,
    )
    return (
        layer_out,
        grad_inputs,
        sum_gain,
        sum_bias,
        sent_query,
        sums[5],
        sent_kv,
        sum_value,
        scatter_out.result.T,
        sums[1],
        sums[2],
        sums[3],
        sent_up,
        sums[0],
        sent_down.T,
        sums[4],
    )


def solution(mesh):
    in_specs = (
        P("dp", None),
        P(),
        P(),
        P(None, "tensor"),
        P("tensor"),
        P(),
        P(),
        P("tensor", None),
        P(),
        P(),
        P(),
        P(None, "tensor"),
        P("tensor"),
        P("tensor", None),
        P(),
        P("dp", None),
    )
    out_specs = (
        P("dp", None),
        P("dp", None),
        P(),
        P(),
        P("dp", "tensor"),
        P("tensor"),
        P("dp", None),
        P(),
        P("tensor", "dp"),
        P(),
        P(),
        P(),
        P("dp", "tensor"),
        P("tensor"),
        P("tensor", "dp"),
        P(),
    )
    return jax.shard_map(
        per_device, mesh=mesh, in_specs=in_specs, out_specs=out_specs, check_vma=False
    )
```

```python
import functools

import jax
import jax.numpy as jnp
from jax import lax
from jax.experimental import pallas as pl
from jax.experimental.pallas import tpu as pltpu
from jax.sharding import PartitionSpec as P

SPAN = 8
EPSILON = 1e-05
NEG_LARGE = -1e30
MESH = pl.DeviceIdType.MESH
VMEM = pl.BlockSpec(memory_space=pltpu.VMEM)
F32 = jnp.float32
BF16 = jnp.bfloat16


def contract(left, right, left_dim, right_dim):
    return lax.dot_general(
        left, right, (((left_dim,), (right_dim,)), ((), ())), preferred_element_type=F32
    )


def remote(source, target, send_sem, recv_sem, device):
    return pltpu.make_async_remote_copy(
        src_ref=source,
        dst_ref=target,
        send_sem=send_sem,
        recv_sem=recv_sem,
        device_id=device,
        device_id_type=MESH,
    )


def greet(devices):
    barrier = pltpu.get_barrier_semaphore()
    for device in devices:
        pl.semaphore_signal(barrier, inc=1, device_id=device, device_id_type=MESH)
    pl.semaphore_wait(barrier, len(devices))


class TensorSum:
    def __init__(self, chunks, part, result, from_core, summed, from_y, sems):
        block = lax.axis_index("dp")
        lane = lax.axis_index("tensor")
        core = lax.rem(lane, 2)
        self.core_peer = (block, lane + 1 - 2 * core)
        self.y_peer = (block, lax.rem(lane + 2, 4))
        rows, width = part.shape
        half = width // 2
        self.step = rows // chunks
        self.mine = pl.ds(pl.multiple_of(core * half, half), half)
        self.other = pl.ds(pl.multiple_of((1 - core) * half, half), half)
        self.part, self.result = part, result
        self.from_core, self.summed, self.from_y = from_core, summed, from_y
        self.sems = sems

    def span(self, k):
        return pl.ds(pl.multiple_of(k * self.step, self.step), self.step)

    def to_core(self, k):
        at = self.span(k)
        return remote(
            self.part.at[at, self.other], self.from_core.at[at], self.sems[0].at[k],
            self.sems[1].at[k], self.core_peer,
        )

    def to_y(self, k):
        at = self.span(k)
        return remote(
            self.summed.at[at], self.from_y.at[at], self.sems[2].at[k], self.sems[3].at[k],
            self.y_peer,
        )

    def back(self, k):
        at = self.span(k)
        return remote(
            self.result.at[at, self.mine], self.result.at[at, self.mine], self.sems[4].at[k],
            self.sems[5].at[k], self.core_peer,
        )

    def first(self, k):
        self.to_core(k).start()

    def second(self, k):
        at = self.span(k)
        self.to_core(k).wait_recv()
        total = self.part[at, self.mine].astype(F32) + self.from_core[at].astype(F32)
        self.summed[at] = total.astype(BF16)
        self.to_y(k).start()

    def third(self, k):
        at = self.span(k)
        self.to_y(k).wait_recv()
        total = self.summed[at].astype(F32) + self.from_y[at].astype(F32)
        self.result[at, self.mine] = total.astype(BF16)
        self.back(k).start()

    def finish(self, chunks):
        @pl.loop(0, chunks)
        def _(k):
            self.back(k).wait_recv()
            self.back(k).wait_send()
            self.to_core(k).wait_send()
            self.to_y(k).wait_send()


def sum_scratch(chunks, rows, width):
    half = pltpu.VMEM((rows, width // 2), BF16)
    return [pltpu.VMEM((rows, width), BF16), half, half, half] + [
        pltpu.SemaphoreType.DMA((chunks,))
    ] * 6


def grad_rows(left_ref, right, target, which):
    levels, rows = target.shape[0], target.shape[1]

    @pl.loop(0, levels)
    def _(lev):
        if rows % 128 == 0:
            cols = pl.ds(pl.multiple_of((2 * lev + which) * rows, rows), rows)
            target[lev] = contract(left_ref[:, cols], right[...], 0, 0).astype(BF16)
        else:
            cols = pl.ds(pl.multiple_of(2 * lev * rows, 2 * rows), 2 * rows)
            both = contract(left_ref[:, cols], right[...], 0, 0)
            target[lev] = jnp.where(which == 0, both[:rows], both[rows:]).astype(BF16)


def hidden_kernel(tiles, x_ref, attn_ref, g_ref, wu_ref, bias_ref, vec_ref, n2_ref, act_ref, dpre_ref, sums_ref, acc):
    step = pl.program_id(0)

    @pl.when(step == 0)
    def _():
        acc[...] = jnp.zeros_like(acc)

    rows = x_ref.shape[0]
    values = x_ref[...].astype(F32) + attn_ref[...].astype(F32) + vec_ref[0:1, :]
    centred = values - jnp.mean(values, axis=-1, keepdims=True)
    scale = lax.rsqrt(jnp.mean(centred * centred, axis=-1, keepdims=True) + EPSILON)
    n2_ref[...] = (centred * scale * vec_ref[1:2, :] + vec_ref[2:3, :]).astype(BF16)
    tile = wu_ref.shape[1] // tiles
    root = 0.7978845608028654
    for j in range(tiles):
        cols = slice(j * tile, (j + 1) * tile)
        pre = jnp.dot(n2_ref[...], wu_ref[:, cols], preferred_element_type=F32) + bias_ref[0:1, cols]
        square = pre * pre
        bend = jnp.tanh(root * pre * (1.0 + 0.044715 * square))
        half = 0.5 * (1.0 + bend)
        act_ref[:, cols] = (pre * half).astype(BF16)
        slope = half + (0.5 * root) * pre * (1.0 - bend * bend) * (1.0 + (3 * 0.044715) * square)
        d_pre = (g_ref[:, cols].astype(F32) * slope).astype(BF16)
        dpre_ref[:, cols] = d_pre
        acc[:, cols] += jnp.sum(d_pre.astype(F32).reshape(rows // 8, 8, tile), axis=0)

    @pl.when(step == pl.num_programs(0) - 1)
    def _():
        sums_ref[...] = jnp.sum(acc[...], axis=0, keepdims=True)


def hidden_stage(inputs, attn_sum, d_activ, up_weight, up_bias, output_bias, gain, bias, block=256, tiles=4):
    rows, width = inputs.shape
    wide = up_weight.shape[1]
    vec = jnp.pad(jnp.stack([output_bias, gain, bias]), ((0, 5), (0, 0)))
    row = lambda cols: pl.BlockSpec((block, cols), lambda k: (k, 0))
    fixed = lambda shape: pl.BlockSpec(shape, lambda k: (0, 0))
    return pl.pallas_call(
        functools.partial(hidden_kernel, tiles),
        grid=(rows // block,),
        out_shape=(
            jax.ShapeDtypeStruct((rows, width), BF16),
            jax.ShapeDtypeStruct((rows, wide), BF16),
            jax.ShapeDtypeStruct((rows, wide), BF16),
            jax.ShapeDtypeStruct((1, wide), F32),
        ),
        in_specs=[
            row(width),
            row(width),
            row(wide),
            pl.BlockSpec(up_weight.shape, lambda k: (0, 0), pipeline_mode=pl.Buffered(1)),
            fixed((1, wide)),
            fixed((8, width)),
        ],
        out_specs=(row(width), row(wide), row(wide), fixed((1, wide))),
        scratch_shapes=[pltpu.VMEM((8, wide), F32)],
        compiler_params=pltpu.CompilerParams(vmem_limit_bytes=60 << 20),
        name="hidden",
    )(inputs, attn_sum, d_activ, up_weight, up_bias.reshape(1, wide), vec)


def hidden_back_kernel(
    chunks, dpre_ref, wu_hbm, n2_hbm, activ_hbm, cot_hbm, far_hbm, wd_hbm, dn_ref, own_out, other_out, down_out,
    mlp_out, weight_ref, n2_ref, activ_ref, cot_ref, far_ref, own_ref, other_ref, down_ref, mlp_ref, in_sem, out_sem,
    mlp_sem, activ_x, x_send, x_recv, part,
    from_core, summed, from_y, *sems,
):
    ts = TensorSum(chunks, part, dn_ref, from_core, summed, from_y, sems)
    side = lax.rem(lax.axis_index("dp"), 2)
    x_peer = (lax.axis_index("dp") + 1 - 2 * side, lax.axis_index("tensor"))
    half = activ_x.shape[1]
    mine = pl.ds(pl.multiple_of(side * half, half), half)
    theirs = pl.ds(pl.multiple_of((1 - side) * half, half), half)
    local = [
        pltpu.make_async_copy(source, target, in_sem.at[n])
        for n, (source, target) in enumerate(
            [
                (wu_hbm, weight_ref),
                (n2_hbm, n2_ref),
                (activ_hbm, activ_ref),
                (cot_hbm, cot_ref),
                (far_hbm, far_ref),
                (wd_hbm, weight_ref),
            ]
        )
    ]
    results = [
        pltpu.make_async_copy(source, target, out_sem.at[n])
        for n, (source, target) in enumerate(
            [(other_ref, other_out), (own_ref, own_out), (down_ref, down_out)]
        )
    ]
    local[0].start()
    greet([ts.core_peer, ts.y_peer, x_peer])
    to_x = remote(activ_hbm.at[:, theirs], activ_x, x_send, x_recv, x_peer)
    to_x.start()
    for copy in local[1:5]:
        copy.start()
    local[0].wait()

    @pl.loop(0, chunks)
    def _(k):
        at = ts.span(k)
        part[at, :] = contract(dpre_ref[at, :], weight_ref[...], 1, 1).astype(BF16)
        ts.first(k)

        @pl.when(k >= 1)
        def _():
            ts.second(k - 1)

    ts.second(chunks - 1)
    local[5].start()
    local[1].wait()
    grad_rows(n2_ref, dpre_ref, other_ref, 1 - side)
    results[0].start()
    grad_rows(n2_ref, dpre_ref, own_ref, side)
    results[1].start()
    levels, rows = down_ref.shape[0], down_ref.shape[1]
    local[2].wait()
    local[3].wait()

    @pl.loop(0, levels)
    def _(lev):
        cols = pl.ds(pl.multiple_of(lev * rows, rows), rows)
        down_ref[lev] = contract(cot_ref[:, cols], activ_ref[:, mine], 0, 0).astype(BF16)

    ready = chunks // 2

    @pl.loop(0, ready)
    def _(k):
        ts.third(k)

    local[5].wait()
    tiles = 4
    tile = mlp_ref.shape[2]

    def mlp_copy(j):
        cols = pl.ds(pl.multiple_of(j * tile, tile), tile)
        slot = lax.rem(j, 2)
        return pltpu.make_async_copy(mlp_ref.at[slot], mlp_out.at[:, cols], mlp_sem.at[slot])

    @pl.loop(0, tiles)
    def _(j):
        @pl.when(j >= 2)
        def _():
            mlp_copy(j - 2).wait()

        cols = pl.ds(pl.multiple_of(j * tile, tile), tile)
        mlp_ref[lax.rem(j, 2)] = jnp.dot(
            activ_ref[...], weight_ref[:, cols], preferred_element_type=F32
        ).astype(BF16)
        mlp_copy(j).start()

    local[4].wait()
    to_x.wait_recv()

    @pl.loop(0, levels)
    def _(lev):
        cols = pl.ds(pl.multiple_of(lev * rows, rows), rows)
        far = contract(far_ref[:, cols], activ_x[...], 0, 0)
        down_ref[lev] = (down_ref[lev].astype(F32) + far).astype(BF16)

    results[2].start()

    @pl.loop(ready, chunks)
    def _(k):
        ts.third(k)

    ts.finish(chunks)
    to_x.wait_send()
    for copy in results:
        copy.wait()
    for j in (tiles - 2, tiles - 1):
        mlp_copy(j).wait()


def hidden_back(
    d_pre, up_weight, normed2, activ, cotangent, far_cotangent, down_weight, count, chunks=4
):
    rows, width = d_pre.shape[0], up_weight.shape[0]
    hidden = up_weight.shape[1]
    levels = count // 2
    half = (levels, width // count, hidden)
    down = (levels, width // levels, hidden // 2)
    dma = pltpu.SemaphoreType.DMA
    hbm = pl.BlockSpec(memory_space=pl.ANY)
    return pl.pallas_call(
        functools.partial(hidden_back_kernel, chunks),
        out_shape=(
            jax.ShapeDtypeStruct((rows, width), BF16),
            jax.ShapeDtypeStruct(half, BF16),
            jax.ShapeDtypeStruct(half, BF16),
            jax.ShapeDtypeStruct(down, BF16),
            jax.ShapeDtypeStruct((rows, width), BF16),
        ),
        in_specs=[VMEM] + [hbm] * 6,
        out_specs=(VMEM,) + (hbm,) * 4,
        scratch_shapes=[
            pltpu.VMEM(up_weight.shape, BF16),
            pltpu.VMEM((rows, width), BF16),
            pltpu.VMEM((rows, hidden), BF16),
            pltpu.VMEM((rows, width), BF16),
            pltpu.VMEM((rows, width), BF16),
            pltpu.VMEM(half, BF16),
            pltpu.VMEM(half, BF16),
            pltpu.VMEM(down, BF16),
            pltpu.VMEM((2, rows, width // 4), BF16),
            dma((6,)),
            dma((3,)),
            dma((2,)),
            pltpu.VMEM((rows, hidden // 2), BF16),
            dma,
            dma,
        ]
        + sum_scratch(chunks, rows, width),
        compiler_params=pltpu.CompilerParams(
            collective_id=4, has_side_effects=True, vmem_limit_bytes=62 << 20
        ),
        name="hidden_back",
    )(d_pre, up_weight, normed2, activ, cotangent, far_cotangent, down_weight)


class Chain:
    def __init__(self, length, level, upper, lower, pair, bufs, sems, early=None):
        self.length, self.level = length, level
        self.peers = (upper, lower)
        self.pair = pair
        self.bufs = bufs
        self.sems = sems
        self.early = early
        self.skip = 0 if early is None else 1

    def copy(self, way, s):
        at = s - 1 - self.skip
        inward, outward = self.bufs[2 * way], self.bufs[2 * way + 1]
        send, recv = self.sems[2 * way], self.sems[2 * way + 1]
        return remote(outward.at[at], inward.at[at], send.at[at], recv.at[at], self.peers[way])

    def arrived(self, way, s):
        if s == 1 and self.early is not None:
            return self.early[way][...]
        return self.bufs[2 * way][s - 1 - self.skip]

    def rank(self, way):
        return self.level if way == 0 else self.length - 1 - self.level

    def start(self, s):
        for way in range(2):
            rank = self.rank(way)
            slot = rank + self.length - s
            slot = jnp.clip(slot if way == 0 else self.length - 1 - slot, 0, self.length - 1)
            outward = self.bufs[2 * way + 1]
            at = s - 1 - self.skip

            @pl.when(rank <= s - 1)
            def _(way=way, rank=rank, slot=slot, outward=outward, at=at):
                outward[at] = self.pair[slot]
                if s > 1:
                    @pl.when(rank >= 1)
                    def _():
                        outward[at] = (
                            self.pair[slot].astype(F32) + self.arrived(way, s - 1).astype(F32)
                        ).astype(BF16)

                self.copy(way, s).start()

    def arrive(self, s):
        for way in range(2):
            rank = self.rank(way)

            @pl.when((rank >= 1) & (rank <= s))
            def _(way=way):
                self.copy(way, s).wait_recv()

    def result(self, target):
        target[...] = self.pair[self.level].astype(F32)
        for way in range(2):
            @pl.when(self.rank(way) >= 1)
            def _(way=way):
                target[...] += self.arrived(way, self.length - 1).astype(F32)

    def drain(self, last=None):
        for s in range(1 + self.skip, (last or self.length - 1) + 1):
            for way in range(2):
                rank = self.rank(way)

                @pl.when(rank <= s - 1)
                def _(way=way, s=s):
                    self.copy(way, s).wait_send()


class FirstStep:
    def __init__(self, length, level, upper, lower, sources, targets, send, recv):
        self.length, self.level = length, level
        self.copies = [
            remote(sources[way], targets[way], send.at[way], recv.at[way], (upper, lower)[way])
            for way in range(2)
        ]

    def each(self, rank, act):
        for way in range(2):
            mine = self.level if way == 0 else self.length - 1 - self.level

            @pl.when(mine == rank)
            def _(way=way):
                act(self.copies[way])

    def start(self):
        self.each(0, lambda copy: copy.start())

    def wait(self):
        self.each(1, lambda copy: copy.wait_recv())
        self.each(0, lambda copy: copy.wait_send())


def chain_scratch(length, shape):
    return [pltpu.VMEM((length - 1,) + shape, BF16)] * 4 + [
        pltpu.SemaphoreType.DMA((length - 1,))
    ] * 4


def chain_peers():
    count = lax.axis_size("dp")
    block = lax.axis_index("dp")
    lane = lax.axis_index("tensor")
    level = block // 2
    upper = (jnp.where(level < count // 2 - 1, block + 2, block + 2 - count), lane)
    lower = (jnp.where(level > 0, block - 2, block - 2 + count), lane)
    return count // 2, level, upper, lower


def middle_kernel(
    chunk, dn_ref, x_ref, attn_ref, cot_ref, vec_ref, part_ref, wo_hbm, ctx_hbm, down_hbm, own_hbm, other_hbm,
    dm_ref, dctx_ref, mlp_ref, out_own, out_other, sums_ref, edge_ref, far_up, far_down, wo_ref, ctx_ref,
    edge_own, edge_got, local_sem, x_send, x_recv, z_send, z_recv, acc,
):
    dp = lax.axis_index("dp")
    lane = lax.axis_index("tensor")
    side = lax.rem(dp, 2)
    x_peer = (dp + 1 - 2 * side, lane)
    length, level, upper, lower = chain_peers()
    edge = jnp.where(level < length // 2, length - 1, 0)
    local = [
        pltpu.make_async_copy(source, target, local_sem.at[n])
        for n, (source, target) in enumerate(
            [
                (wo_hbm, wo_ref),
                (ctx_hbm, ctx_ref),
                (own_hbm.at[edge], edge_own),
            ]
        )
    ]
    for copy in local:
        copy.start()
    greet([x_peer, upper, lower])
    to_x = remote(other_hbm.at[edge], edge_got, x_send, x_recv, x_peer)
    to_x.start()
    first_step = FirstStep(
        length, level, upper, lower, (down_hbm.at[length - 1], down_hbm.at[0]), (far_up, far_down), z_send,
        z_recv,
    )
    first_step.start()
    rows, width = x_ref.shape
    acc[...] = jnp.zeros_like(acc)
    share = 1.0 / lax.axis_size("tensor")

    def fold(values):
        return jnp.sum(values.reshape(chunk // 8, 8, width), axis=0)

    def norm_rows(k):
        at = pl.ds(pl.multiple_of(k * chunk, chunk), chunk)
        values = x_ref[at, :].astype(F32) + attn_ref[at, :].astype(F32) + vec_ref[0:1, :]
        base = share * (values + vec_ref[2:3, :])
        mlp_ref[at, :] = (part_ref[at, :].astype(F32) + base).astype(BF16)
        centred = values - jnp.mean(values, axis=-1, keepdims=True)
        scale = lax.rsqrt(jnp.mean(centred * centred, axis=-1, keepdims=True) + EPSILON)
        hat = centred * scale
        grad = dn_ref[at, :].astype(F32)
        acc[0] += fold(grad * hat)
        acc[1] += fold(grad)
        scaled = grad * vec_ref[1:2, :]
        first = jnp.mean(scaled, axis=-1, keepdims=True)
        second = jnp.mean(scaled * hat, axis=-1, keepdims=True)
        cot = cot_ref[at, :].astype(F32)
        d_middle = cot + scale * (scaled - first - hat * second)
        acc[2] += fold(d_middle)
        acc[3] += fold(cot)
        dm_ref[at, :] = d_middle.astype(BF16)

    @pl.loop(0, rows // chunk)
    def _(k):
        norm_rows(k)

    for n in range(4):
        sums_ref[n : n + 1, :] = jnp.sum(acc[n], axis=0, keepdims=True)
    sums_ref[4:8, :] = jnp.zeros((4, width), F32)
    local[0].wait()

    @pl.loop(0, 4)
    def _(k):
        at = pl.ds(pl.multiple_of(k * (rows // 4), rows // 4), rows // 4)
        dctx_ref[at, :] = contract(dm_ref[at, :], wo_ref[...], 1, 1).astype(BF16)

    local[1].wait()
    grad_rows(dm_ref, ctx_ref, out_other, 1 - side)
    grad_rows(dm_ref, ctx_ref, out_own, side)
    local[2].wait()
    to_x.wait()
    edge_ref[...] = (edge_own[...].astype(F32) + edge_got[...].astype(F32)).astype(BF16)
    first_step.wait()


def middle_stage(
    d_normed2, inputs, attn_sum, cotangent, output_bias, gain, down_bias, part, output_weight, context, down,
    up_own, up_other, count, chunk=128,
):
    rows, width = inputs.shape
    heads = context.shape[1]
    vec = jnp.stack([output_bias, gain, down_bias])
    vec = jnp.pad(vec, ((0, 5), (0, 0)))
    half = jax.ShapeDtypeStruct((count // 2, width // count, heads), BF16)
    hbm = pl.BlockSpec(memory_space=pl.ANY)
    dma = pltpu.SemaphoreType.DMA
    low = lambda shape: jax.ShapeDtypeStruct(shape, BF16)
    edge = pltpu.VMEM(up_own.shape[1:], BF16)
    return pl.pallas_call(
        functools.partial(middle_kernel, chunk),
        out_shape=(
            low((rows, width)),
            low((rows, heads)),
            low((rows, width)),
            half,
            half,
            jax.ShapeDtypeStruct((8, width), F32),
            low(up_own.shape[1:]),
            low(down.shape[1:]),
            low(down.shape[1:]),
        ),
        in_specs=[VMEM] * 6 + [hbm] * 5,
        out_specs=(VMEM,) * 7 + (hbm,) * 2,
        scratch_shapes=[
            pltpu.VMEM(output_weight.shape, BF16),
            pltpu.VMEM(context.shape, BF16),
            edge,
            edge,
            dma((3,)),
            dma,
            dma,
            dma((2,)),
            dma((2,)),
            pltpu.VMEM((4, 8, width), F32),
        ],
        compiler_params=pltpu.CompilerParams(
            collective_id=7, has_side_effects=True, vmem_limit_bytes=60 << 20
        ),
        name="middle",
    )(
        d_normed2, inputs, attn_sum, cotangent, vec, part, output_weight, context, down, up_own, up_other,
    )


def query_back_kernel(
    chunks, steps, dq_ref, wq_ref, n1_ref, dkv_ref, wide_ref, wide_up, wide_down, proj_ref, proj_x, dn_ref,
    grad_ref, proj_grad, tot_ref, far_up, far_down, kv_local, part, from_core, summed, from_y, kv_core, kv_sum, kv_x,
    kv_pair, kv_z, kv_up, kv_y, kv_sems, own_ref, other_ref, got_ref, q_send, q_recv, proj_pair, *rest,
):
    chain_bufs, chain_sems, sems = rest[:4], rest[4:8], rest[8:14]
    wide_bufs, wide_sems = rest[14:18], rest[18:22]
    proj_bufs, proj_sems = rest[22:26], rest[26:]
    ts = TensorSum(chunks, part, dn_ref, from_core, summed, from_y, sems)
    block = lax.axis_index("dp")
    lane = lax.axis_index("tensor")
    place = lax.rem(block, SPAN)
    side = lax.rem(place, 2)
    level = place // 2
    levels = SPAN // 2
    x_peer = (block + 1 - 2 * side, lane)
    upper = (jnp.where(level < levels - 1, block + 2, block + 2 - SPAN), lane)
    lower = (jnp.where(level > 0, block - 2, block - 2 + SPAN), lane)
    length, chain_level, chain_upper, chain_lower = chain_peers()
    if length == levels:
        greet([ts.core_peer, ts.y_peer, x_peer, upper, lower])
    else:
        greet([ts.core_peer, ts.y_peer, x_peer, upper, lower, chain_upper, chain_lower])
    chain = Chain(length, chain_level, chain_upper, chain_lower, own_ref, chain_bufs, chain_sems)
    early = (wide_up, wide_down)
    wide = Chain(length, chain_level, chain_upper, chain_lower, wide_ref, wide_bufs, wide_sems, early)
    proj = Chain(length, chain_level, chain_upper, chain_lower, proj_pair, proj_bufs, proj_sems)
    core = lax.rem(lane, 2)
    seq_rows = tot_ref.shape[0]
    half = seq_rows // 2
    mine = pl.ds(pl.multiple_of(core * half, half), half)
    other = pl.ds(pl.multiple_of((1 - core) * half, half), half)

    def kv_copy(source, target, index, device):
        return remote(source, target, kv_sems.at[0, index], kv_sems.at[1, index], device)

    to_core = [
        kv_copy(
            dkv_ref.at[pl.ds(2 * lev, 2), other], kv_core.at[lev], 3 + levels + lev, ts.core_peer
        )
        for lev in range(levels)
    ]
    keep = [
        pltpu.make_async_copy(dkv_ref.at[pl.ds(2 * lev, 2), mine], kv_sum.at[lev], kv_local.at[lev])
        for lev in range(levels)
    ]
    for copy in to_core + keep:
        copy.start()
    proj_pair[...] = (proj_ref[...].astype(F32) + proj_x[...].astype(F32)).astype(BF16)
    proj.start(1)
    wide.start(2)
    grad_levels, rows = own_ref.shape[0], own_ref.shape[1]
    for lev in range(levels):
        to_core[lev].wait_recv()
        keep[lev].wait()
        kv_sum[lev] = (kv_sum[lev].astype(F32) + kv_core[lev].astype(F32)).astype(BF16)

    to_x = kv_copy(kv_sum.at[:, 1 - side], kv_x, 1, x_peer)
    to_x.start()

    @pl.loop(0, chunks)
    def _(k):
        at = ts.span(k)
        part[at, :] = contract(dq_ref[at, :], wq_ref[...], 1, 1).astype(BF16)
        ts.first(k)

        @pl.when(k >= 1)
        def _():
            ts.second(k - 1)

    ts.second(chunks - 1)

    def grad(target, which):
        grad_rows(n1_ref, dq_ref, target, which)

    grad(other_ref, 1 - side)
    q_to_x = remote(other_ref, got_ref, q_send, q_recv, x_peer)
    grad(own_ref, side)
    for s in range(1, length - 1):
        proj.arrive(s)
        proj.start(s + 1)
    to_x.wait_recv()
    q_to_x.start()

    @pl.loop(0, levels)
    def _(lev):
        kv_pair[lev] = (kv_sum[lev, side].astype(F32) + kv_x[lev].astype(F32)).astype(BF16)

    def down(s):
        slot = jnp.maximum(level - levels + s, 0)
        return kv_copy(kv_up.at[s - 1], kv_z.at[s - 1], 1 + s, lower), slot

    for s in range(1, levels):
        copy, slot = down(s)

        @pl.when(level >= levels - s)
        def _(copy=copy, slot=slot, s=s):
            kv_up[s - 1] = kv_pair[slot]
            if s > 1:
                @pl.when(level < levels - 1)
                def _():
                    kv_up[s - 1] = (
                        kv_pair[slot].astype(F32) + kv_z[s - 2].astype(F32)
                    ).astype(BF16)

            copy.start()

        @pl.when((level >= levels - 1 - s) & (level < levels - 1))
        def _(copy=copy):
            copy.wait_recv()

    kv_up[levels - 1] = kv_pair[level]

    @pl.when(level < levels - 1)
    def _():
        kv_up[levels - 1] = (
            kv_pair[level].astype(F32) + kv_z[levels - 2].astype(F32)
        ).astype(BF16)

    to_y = kv_copy(kv_up.at[levels - 1], kv_y, 1 + levels, ts.y_peer)
    to_y.start()
    for s in range(2, steps):
        wide.arrive(s)
        wide.start(s + 1)
    q_to_x.wait_recv()

    @pl.loop(0, grad_levels)
    def _(lev):
        own_ref[lev] = (own_ref[lev].astype(F32) + got_ref[lev].astype(F32)).astype(BF16)

    chain.start(1)
    to_y.wait_recv()
    tot_ref[mine] = (kv_up[levels - 1].astype(F32) + kv_y[...].astype(F32)).astype(BF16)
    back = kv_copy(tot_ref.at[mine], tot_ref.at[mine], 2 + levels, ts.core_peer)
    back.start()
    half_way = chunks // 2
    for s in range(1, length):
        if s == 2:
            @pl.loop(0, half_way)
            def _(k):
                ts.third(k)

        chain.arrive(s)
        if s + 1 < length:
            chain.start(s + 1)

    @pl.loop(half_way, chunks)
    def _(k):
        ts.third(k)

    chain.result(grad_ref)
    proj.arrive(length - 1)
    proj.result(proj_grad)
    wide.arrive(steps)
    far_up[...] = wide.arrived(0, steps)
    far_down[...] = wide.arrived(1, steps)
    chain.drain()
    proj.drain()
    wide.drain(steps)
    q_to_x.wait_send()
    back.wait()
    for copy in to_core:
        copy.wait_send()
    to_x.wait_send()
    to_y.wait_send()
    for s in range(1, levels):
        copy, _slot = down(s)

        @pl.when(level >= levels - s)
        def _(copy=copy):
            copy.wait_send()

    ts.finish(chunks)


def query_back(
    d_queries, query_weight, normed1, parts, wide, wide_up, wide_down, proj, proj_x, count, chunks=4
):
    rows, width = d_queries.shape[0], query_weight.shape[0]
    kv_width = parts.shape[2]
    steps = count // 2 - 2
    levels = SPAN // 2
    shape = (width // count, query_weight.shape[1])
    half = pltpu.VMEM((count // 2,) + shape, BF16)
    piece = (rows // 2, kv_width)
    return pl.pallas_call(
        functools.partial(query_back_kernel, chunks, steps),
        out_shape=(
            jax.ShapeDtypeStruct((rows, width), BF16),
            jax.ShapeDtypeStruct(shape, F32),
            jax.ShapeDtypeStruct(proj.shape[1:], F32),
            jax.ShapeDtypeStruct((rows, kv_width), BF16),
            jax.ShapeDtypeStruct(wide.shape[1:], BF16),
            jax.ShapeDtypeStruct(wide.shape[1:], BF16),
        ),
        in_specs=[VMEM] * 3 + [pl.BlockSpec(memory_space=pl.ANY)] + [VMEM] * 5,
        out_specs=(VMEM,) * 6,
        scratch_shapes=[
            pltpu.SemaphoreType.DMA((levels,)),
        ]
        + sum_scratch(chunks, rows, width)[:4]
        + [
            pltpu.VMEM((levels, 2) + piece, BF16),
            pltpu.VMEM((levels, 2) + piece, BF16),
            pltpu.VMEM((levels,) + piece, BF16),
            pltpu.VMEM((levels,) + piece, BF16),
            pltpu.VMEM((levels - 1,) + piece, BF16),
            pltpu.VMEM((levels,) + piece, BF16),
            pltpu.VMEM(piece, BF16),
            pltpu.SemaphoreType.DMA((2, 3 + 2 * levels)),
            half,
            half,
            half,
            pltpu.SemaphoreType.DMA,
            pltpu.SemaphoreType.DMA,
            pltpu.VMEM(proj.shape, BF16),
        ]
        + chain_scratch(count // 2, shape)
        + [pltpu.SemaphoreType.DMA((chunks,))] * 6
        + chain_scratch(steps, wide.shape[1:])
        + chain_scratch(count // 2, proj.shape[1:]),
        compiler_params=pltpu.CompilerParams(
            collective_id=5, has_side_effects=True, vmem_limit_bytes=63 << 20
        ),
        name="query_back",
    )(d_queries, query_weight, normed1, parts, wide, wide_up, wide_down, proj, proj_x)


def norm_back_kernel(dkv_ref, wkv_ref, dn_ref, x_ref, dm_ref, gain_ref, grad_x, sums_ref, acc, acc_kv):
    k = pl.program_id(0)

    @pl.when(k == 0)
    def _():
        acc[...] = jnp.zeros_like(acc)
        acc_kv[...] = jnp.zeros_like(acc_kv)

    chunk, width = x_ref.shape

    def fold(values):
        return jnp.sum(values.reshape(chunk // 8, 8, values.shape[1]), axis=0)

    values = x_ref[...].astype(F32)
    centred = values - jnp.mean(values, axis=-1, keepdims=True)
    scale = lax.rsqrt(jnp.mean(centred * centred, axis=-1, keepdims=True) + EPSILON)
    hat = centred * scale
    grad = dn_ref[...].astype(F32) + contract(dkv_ref[...], wkv_ref[...], 1, 1)
    acc[0] += fold(grad * hat)
    acc[1] += fold(grad)
    acc_kv[...] += fold(dkv_ref[...].astype(F32))
    scaled = grad * gain_ref[...]
    first = jnp.mean(scaled, axis=-1, keepdims=True)
    second = jnp.mean(scaled * hat, axis=-1, keepdims=True)
    grad_x[...] = dm_ref[...].astype(F32) + scale * (scaled - first - hat * second)

    @pl.when(k == pl.num_programs(0) - 1)
    def _():
        sums_ref[...] = jnp.zeros_like(sums_ref)
        sums_ref[0:1, :] = jnp.sum(acc[0], axis=0, keepdims=True)
        sums_ref[1:2, :] = jnp.sum(acc[1], axis=0, keepdims=True)
        sums_ref[2:3, 0 : acc_kv.shape[1]] = jnp.sum(acc_kv[...], axis=0, keepdims=True)


def norm_back(d_keyval, keyval_weight, d_normed1, inputs, d_middle, gain, chunk=128):
    rows, width = inputs.shape
    kv_width = d_keyval.shape[1]
    row = lambda cols: pl.BlockSpec((chunk, cols), lambda k: (k, 0))
    fixed = lambda shape: pl.BlockSpec(shape, lambda k: (0, 0))
    return pl.pallas_call(
        norm_back_kernel,
        grid=(rows // chunk,),
        out_shape=(
            jax.ShapeDtypeStruct((rows, width), F32),
            jax.ShapeDtypeStruct((8, width), F32),
        ),
        in_specs=[
            row(kv_width),
            fixed((width, kv_width)),
            row(width),
            row(width),
            row(width),
            fixed((1, width)),
        ],
        out_specs=(row(width), fixed((8, width))),
        scratch_shapes=[pltpu.VMEM((2, 8, width), F32), pltpu.VMEM((8, kv_width), F32)],
        compiler_params=pltpu.CompilerParams(vmem_limit_bytes=62 << 20),
        name="norm_back",
    )(d_keyval, keyval_weight, d_normed1, inputs, d_middle, gain.reshape(1, width))


def finish_kernel(
    n1_ref, dkv_ref, vec_in, wide_ref, far_up, far_down, down_ref, grad_ref, vec_ref, up_ref, down_out, ends_ref,
    local_sem, d_send, d_recv, down_low, down_got, up_out, up_in, up_send, up_recv, own_ref, other_ref, got_ref, x_send, x_recv, own_vec, low_vec, slots, send, recv, *chain_refs,
):
    block = lax.axis_index("dp")
    lane = lax.axis_index("tensor")
    count = lax.axis_size("dp")
    side = lax.rem(block, 2)
    pairs = count // 2
    others = [(lax.rem(block + 2 * k, count), lane) for k in range(1, pairs)]
    x_peer = (block + 1 - 2 * side, lane)
    length, level, upper, lower = chain_peers()
    local = [
        pltpu.make_async_copy(
            wide_ref.at[jnp.clip(level + k, 0, length - 1)], ends_ref.at[n], local_sem.at[n]
        )
        for n, k in enumerate((0, 1, -1))
    ]
    for copy in local:
        copy.start()
    greet([x_peer] + others)
    low_vec[0] = vec_in[...].astype(BF16)
    to_pair = remote(low_vec.at[0], slots.at[0], send.at[0], recv.at[0], x_peer)
    to_pair.start()

    def last(way):
        return remote(
            up_out.at[way], up_in.at[way], up_send.at[way], up_recv.at[way], (upper, lower)[way]
        )

    ranks = (level, length - 1 - level)
    for copy in local:
        copy.wait()
    for way, far in enumerate((far_up, far_down)):
        @pl.when(ranks[way] < length - 1)
        def _(way=way, far=far):
            up_out[way] = ends_ref[1 + way]

            @pl.when(ranks[way] >= 1)
            def _():
                up_out[way] = (ends_ref[1 + way].astype(F32) + far[...].astype(F32)).astype(BF16)

            last(way).start()

    grad_rows(n1_ref, dkv_ref, other_ref, 1 - side)
    to_x = remote(other_ref, got_ref, x_send, x_recv, x_peer)
    to_x.start()
    half_rows, half_cols = down_low.shape
    down_mine = pl.ds(pl.multiple_of(side * half_rows, half_rows), half_rows)
    down_theirs = pl.ds(pl.multiple_of((1 - side) * half_rows, half_rows), half_rows)
    down_low[...] = down_ref[down_theirs].astype(BF16)
    d_to_x = remote(down_low, down_got, d_send, d_recv, x_peer)
    to_pair.wait()
    own_vec[...] = vec_in[...] + slots[0].astype(F32)
    low_vec[1] = own_vec[...].astype(BF16)
    copies = []
    for k in range(1, pairs):
        copy = remote(low_vec.at[1], slots.at[k], send.at[k], recv.at[k], others[k - 1])
        copy.start()
        copies.append(copy)
    grad_rows(n1_ref, dkv_ref, own_ref, side)
    chain = Chain(length, level, upper, lower, own_ref, chain_refs[:4], chain_refs[4:8])
    to_x.wait_recv()
    own_ref[...] = (own_ref[...].astype(F32) + got_ref[...].astype(F32)).astype(BF16)
    chain.start(1)
    d_to_x.start()
    for s in range(1, length):
        chain.arrive(s)
        if s + 1 < length:
            chain.start(s + 1)
    chain.result(grad_ref)
    d_to_x.wait()
    first = pl.ds(pl.multiple_of(side * half_cols, half_cols), half_cols)
    second = pl.ds(pl.multiple_of((1 - side) * half_cols, half_cols), half_cols)
    down_out[:, first] = down_ref[down_mine]
    down_out[:, second] = down_got[...].astype(F32)
    total = own_vec[...]
    for k in range(1, pairs):
        copies[k - 1].wait()
        total = total + slots[k].astype(F32)
    vec_ref[...] = total
    up_ref[...] = ends_ref[0].astype(F32)
    for way in range(2):
        @pl.when(ranks[way] >= 1)
        def _(way=way):
            last(way).wait_recv()
            up_ref[...] += up_in[way].astype(F32)

        @pl.when(ranks[way] < length - 1)
        def _(way=way):
            last(way).wait_send()

    chain.drain()
    to_x.wait_send()


def finish(normed1, d_keyval, rows_of_vectors, vectors, wide, far_up, far_down, down, count):
    width = normed1.shape[1]
    flat = jnp.concatenate(vectors)
    lines = -(-flat.shape[0] // width)
    flat = jnp.pad(flat, (0, lines * width - flat.shape[0])).reshape(lines, width)
    packed = jnp.concatenate(rows_of_vectors + [flat], axis=0)
    height = -(-packed.shape[0] // 8) * 8
    packed = jnp.pad(packed, ((0, height - packed.shape[0]), (0, 0)))
    shape = (width // count, d_keyval.shape[1])
    half = pltpu.VMEM((count // 2,) + shape, BF16)
    dma = pltpu.SemaphoreType.DMA
    two = pltpu.VMEM((2,) + far_up.shape, BF16)
    return pl.pallas_call(
        finish_kernel,
        out_shape=(
            jax.ShapeDtypeStruct(shape, F32),
            jax.ShapeDtypeStruct((height, width), F32),
            jax.ShapeDtypeStruct(far_up.shape, F32),
            jax.ShapeDtypeStruct((down.shape[0] // 2, 2 * down.shape[1]), F32),
        ),
        in_specs=[VMEM] * 3 + [pl.BlockSpec(memory_space=pl.ANY)] + [VMEM] * 3,
        out_specs=(VMEM,) * 4,
        scratch_shapes=[
            pltpu.VMEM((3,) + far_up.shape, BF16),
            dma((3,)),
            dma,
            dma,
            pltpu.VMEM((down.shape[0] // 2, down.shape[1]), BF16),
            pltpu.VMEM((down.shape[0] // 2, down.shape[1]), BF16),
        ]
        + [two, two, dma((2,)), dma((2,)), half, half, half, dma, dma]
        + [
            pltpu.VMEM((height, width), F32),
            pltpu.VMEM((2, height, width), BF16),
            pltpu.VMEM((count // 2, height, width), BF16),
            dma((count // 2,)),
            dma((count // 2,)),
        ]
        + chain_scratch(count // 2, shape),
        compiler_params=pltpu.CompilerParams(
            collective_id=2, has_side_effects=True, vmem_limit_bytes=62 << 20
        ),
        name="finish",
    )(normed1, d_keyval, packed, wide, far_up, far_down, down)


def front_kernel(
    block, chunks, q_ref, own_kv, cot_hbm, wo_ref, wd_hbm, kv_ref, ctx_ref, lse_ref, sum_ref, g_ref, far_ref,
    cot_ref, wd_ref, local_sem, x_send, x_recv, z_send, z_recv, s_send, s_recv, f_send, f_recv, acc, peak, total,
    part, from_core, summed, from_y, *sems,
):
    ts = TensorSum(chunks, part, sum_ref, from_core, summed, from_y, sems)
    dp = lax.axis_index("dp")
    lane = lax.axis_index("tensor")
    place = lax.rem(dp, SPAN)
    side = lax.rem(place, 2)
    level = place // 2
    levels = SPAN // 2
    core = lax.rem(lane, 2)
    y_lane = lax.rem(lane + 2, 4)
    core_peer, y_peer = ts.core_peer, ts.y_peer
    x_peer = (dp + 1 - 2 * side, lane)
    upper = (jnp.where(level < levels - 1, dp + 2, dp + 2 - SPAN), lane)
    lower = (jnp.where(level > 0, dp - 2, dp - 2 + SPAN), lane)
    seq_rows = own_kv.shape[0]
    piece = seq_rows // 4
    head = kv_ref.shape[2] // 2
    heads = q_ref.shape[1] // head
    parts = seq_rows // block

    def rows_of(which):
        return pl.ds(pl.multiple_of(which * piece, piece), piece)

    local = [
        pltpu.make_async_copy(own_kv, kv_ref.at[place], local_sem.at[0]),
        pltpu.make_async_copy(cot_hbm, cot_ref, local_sem.at[1]),
        pltpu.make_async_copy(wd_hbm, wd_ref, local_sem.at[2]),
    ]
    local[0].start()
    greet([core_peer, y_peer, x_peer, upper, lower])
    to_x = remote(own_kv.at[rows_of(lane)], kv_ref.at[place, rows_of(lane)], x_send, x_recv, x_peer)
    to_x.start()
    far_pieces = f_send.shape[1]
    far_step = cot_hbm.shape[0] // (2 * far_pieces)

    def far(kind, k):
        start = pl.multiple_of((core * far_pieces + k) * far_step, far_step)
        source = cot_hbm if kind == 0 else far_ref
        return remote(
            source.at[pl.ds(start, far_step)], far_ref.at[pl.ds(start, far_step)], f_send.at[kind, k],
            f_recv.at[kind, k], x_peer if kind == 0 else core_peer,
        )

    def share(s, kind):
        at = rows_of(y_lane if kind == 2 else lane)
        ref = kv_ref.at[pl.ds(2 * (level - s), 2), at]
        return remote(
            ref, ref, s_send.at[s, kind], s_recv.at[s, kind], y_peer if kind == 0 else core_peer
        )

    def share_pair(kind):
        ref = kv_ref.at[place + 1 - 2 * side, rows_of(y_lane if kind == 2 else lane)]
        return remote(
            ref, ref, s_send.at[0, kind], s_recv.at[0, kind], y_peer if kind == 0 else core_peer
        )

    def up(s):
        ref = kv_ref.at[pl.ds(2 * (level - s), 2), rows_of(lane)]
        return remote(ref, ref, z_send.at[s], z_recv.at[s], upper)

    def from_below(s):
        ref = kv_ref.at[pl.ds(2 * (level - 1 - s), 2), rows_of(lane)]
        return remote(ref, ref, z_send.at[s], z_recv.at[s], upper)

    def forward(s):
        from_below(s - 1).wait_recv()

        @pl.when((s < levels - 1) & (level < levels - 1))
        def _():
            up(s).start()

        share(s, 0).start()
        share(s, 1).start()

    def score(i, h, at_block, at_row, diagonal):
        keys = kv_ref[at_block, pl.ds(at_row, block), 0:head]
        query = q_ref[i * block : (i + 1) * block, h * head : (h + 1) * head]
        scores = contract(keys, query, 1, 1)
        if diagonal:
            key_at = lax.broadcasted_iota(jnp.int32, scores.shape, 0)
            query_at = lax.broadcasted_iota(jnp.int32, scores.shape, 1)
            scores = jnp.where(key_at <= query_at, scores, NEG_LARGE)
        return scores

    def soften(i, h, scores):
        old = peak[i, h]
        new = jnp.maximum(old, jnp.max(scores, axis=0, keepdims=True))
        probs = jnp.exp(scores - new)
        fade = jnp.exp(old - new)
        total[i, h] = total[i, h] * fade + jnp.sum(probs, axis=0, keepdims=True)
        peak[i, h] = new
        return probs.astype(BF16), fade

    def weigh(i, h, at_block, at_row, probs, fade):
        values = kv_ref[at_block, pl.ds(at_row, block), head : 2 * head]
        acc[i, h] = acc[i, h] * fade + contract(values, probs, 0, 0)

    def attend(i, pieces):
        items = [(h, piece) for piece in pieces for h in range(heads)]
        scores = score(i, items[0][0], *items[0][1])
        waiting = None
        for n, (h, (at_block, at_row, _diagonal)) in enumerate(items):
            following = None
            if n + 1 < len(items):
                following = score(i, items[n + 1][0], *items[n + 1][1])
            probs, fade = soften(i, h, scores)
            if waiting is not None:
                weigh(i, *waiting)
            waiting = (h, at_block, at_row, probs, fade)
            scores = following
        weigh(i, *waiting)

    def attend_level(i, s):
        @pl.loop(0, 2)
        def _(b):
            attend(i, [(2 * (level - s) + b, n * block, False) for n in range(parts)])

    peak[...] = jnp.full_like(peak, NEG_LARGE)
    total[...] = jnp.zeros_like(total)
    acc[...] = jnp.zeros_like(acc)
    local[0].wait()
    for copy in local[1:]:
        copy.start()
    for k in range(far_pieces):
        far(0, k).start()
    to_x.wait_recv()

    @pl.when(level < levels - 1)
    def _():
        up(0).start()

    share_pair(0).start()
    share_pair(1).start()
    for i in range(parts):
        attend(i, [(place, n * block, n == i) for n in range(i + 1)])

    @pl.when(level >= 1)
    def _():
        forward(1)

    share_pair(0).wait_recv()
    share_pair(2).start()
    share_pair(1).wait_recv()
    share_pair(2).wait_recv()

    @pl.when(side == 1)
    def _():
        for i in range(parts):
            attend(i, [(place - 1, n * block, False) for n in range(parts)])

    def complete(i):
        span = slice(i * block, (i + 1) * block)
        for h in range(heads):
            context = acc[i, h] / total[i, h]
            ctx_ref[span, h * head : (h + 1) * head] = context.T.astype(BF16)
            lse_ref[h : h + 1, span] = peak[i, h] + jnp.log(total[i, h])
        each = chunks // parts
        first = i * each

        @pl.loop(first, first + each)
        def _(k):
            at = ts.span(k)
            part[at, :] = jnp.dot(
                ctx_ref[at, :], wo_ref[...], preferred_element_type=F32
            ).astype(BF16)
            ts.first(k)

        @pl.loop(first, first + each)
        def _(k):
            ts.second(k)

    @pl.loop(1, level + 1)
    def _(s):
        @pl.when(s < level)
        def _():
            forward(s + 1)

        share(s, 0).wait_recv()
        share(s, 2).start()
        share(s, 1).wait_recv()
        share(s, 2).wait_recv()
        attend_level(0, s)

    complete(0)
    for i in range(1, parts):
        @pl.loop(1, level + 1)
        def _(s, i=i):
            attend_level(i, s)

        complete(i)

    for k in range(far_pieces):
        far(0, k).wait_recv()
        far(1, k).start()
    ready = chunks - chunks // parts

    @pl.loop(0, ready)
    def _(k):
        ts.third(k)

    for copy in local[1:]:
        copy.wait()
    tile = g_ref.shape[1] // 8

    @pl.loop(0, 8)
    def _(j):
        cols = pl.ds(pl.multiple_of(j * tile, tile), tile)
        g_ref[:, cols] = contract(cot_ref[...], wd_ref[cols, :], 1, 1).astype(BF16)

    @pl.loop(ready, chunks)
    def _(k):
        ts.third(k)

    to_x.wait_send()

    @pl.when(level < levels - 1)
    def _():
        up(0).wait_send()

    for kind in range(3):
        share_pair(kind).wait_send()

    @pl.loop(1, level + 1)
    def _(s):
        for kind in range(3):
            share(s, kind).wait_send()

        @pl.when((s < levels - 1) & (level < levels - 1))
        def _():
            up(s).wait_send()

    for k in range(far_pieces):
        far(0, k).wait_send()
        far(1, k).wait()
    ts.finish(chunks)


def front(queries, keyval, cotangent, output_weight, down_weight, block=512, chunks=8):
    rows, width = queries.shape
    wide = output_weight.shape[1]
    hidden = down_weight.shape[0]
    head = keyval.shape[1] // 2
    heads = width // head
    levels = SPAN // 2
    dma = pltpu.SemaphoreType.DMA
    hbm = pl.BlockSpec(memory_space=pl.ANY)
    stat = pltpu.VMEM((rows // block, heads, 1, block), F32)
    return pl.pallas_call(
        functools.partial(front_kernel, block, chunks),
        out_shape=(
            jax.ShapeDtypeStruct((SPAN,) + keyval.shape, BF16),
            jax.ShapeDtypeStruct((rows, width), BF16),
            jax.ShapeDtypeStruct((heads, rows), F32),
            jax.ShapeDtypeStruct((rows, wide), BF16),
            jax.ShapeDtypeStruct((rows, hidden), BF16),
            jax.ShapeDtypeStruct(cotangent.shape, BF16),
        ),
        in_specs=[VMEM, VMEM, hbm, VMEM, hbm],
        out_specs=(VMEM,) * 5 + (hbm,),
        scratch_shapes=[
            pltpu.VMEM(cotangent.shape, BF16),
            pltpu.VMEM(down_weight.shape, BF16),
            dma((3,)),
            dma,
            dma,
            dma((levels - 1,)),
            dma((levels - 1,)),
            dma((levels, 3)),
            dma((levels, 3)),
            dma((2, 4)),
            dma((2, 4)),
            pltpu.VMEM((rows // block, heads, head, block), F32),
            stat,
            stat,
        ]
        + sum_scratch(chunks, rows, wide),
        compiler_params=pltpu.CompilerParams(
            collective_id=1, has_side_effects=True, vmem_limit_bytes=60 << 20
        ),
        name="front",
    )(queries, keyval, cotangent, output_weight, down_weight)


def attend_back_kernel(
    block, chunks, q_ref, kv_ref, do_ref, ctx_ref, lse_ref, pair_ref, far_up, far_down, mlp_ref, sent_ref,
    edge_ref, proj_ref, dq_ref, dkv_ref, grad_ref, out_ref, got_ref, wide_up, wide_down, proj_got, dq_acc, dkv_acc,
    delta, x_send, x_recv, z_send, z_recv, from_core, summed, from_y, *rest,
):
    sems, chain_refs = rest[:6], rest[6:]
    rows = q_ref.shape[0]
    head = kv_ref.shape[1] // 2
    heads = q_ref.shape[1] // head
    place = lax.rem(lax.axis_index("dp"), SPAN)
    side = lax.rem(lax.axis_index("dp"), 2)
    x_peer = (lax.axis_index("dp") + 1 - 2 * side, lax.axis_index("tensor"))
    ts = TensorSum(chunks, mlp_ref, out_ref, from_core, summed, from_y, sems)
    length, level, upper, lower = chain_peers()
    early = (far_up, far_down)
    chain = Chain(length, level, upper, lower, pair_ref, chain_refs[:4], chain_refs[4:], early)
    greet([ts.core_peer, ts.y_peer, x_peer, upper, lower])
    left = pl.ds(jnp.where(level < length // 2, 0, 1), length - 1)
    proj_to_x = remote(proj_ref, proj_got, x_send.at[1], x_recv.at[1], x_peer)
    proj_to_x.start()
    to_x = remote(sent_ref.at[left], got_ref.at[left], x_send.at[0], x_recv.at[0], x_peer)
    to_x.start()

    @pl.loop(0, chunks)
    def _(k):
        ts.first(k)

    chain.start(2)
    wide_step = FirstStep(
        length, level, upper, lower, (edge_ref, edge_ref), (wide_up, wide_down), z_send, z_recv
    )
    wide_step.start()
    levels = SPAN // 2
    parts = 2 * rows // block
    per_slot = -(-(length - 2) // (levels - 1))
    done = 1
    for target in range(levels):
        dkv_acc[...] = jnp.zeros_like(dkv_acc)
        for i in range(rows // block):
            span = slice(i * block, (i + 1) * block)
            if target == 0:
                for h in range(heads):
                    cols = slice(h * head, (h + 1) * head)
                    product = do_ref[span, cols].astype(F32) * ctx_ref[span, cols].astype(F32)
                    delta[h : h + 1, span] = jnp.sum(product.T, axis=0, keepdims=True)
                dq_acc[i] = jnp.zeros_like(dq_acc[i])

            def step(j, diagonal, span=span, i=i):
                at = pl.ds(pl.multiple_of(j * block, block), block)
                kv_at = pl.ds(pl.multiple_of((target * parts + j) * block, block), block)
                keys = kv_ref[kv_at, 0:head]
                values = kv_ref[kv_at, head : 2 * head]
                d_keys = jnp.zeros((block, head), F32)
                d_values = jnp.zeros((block, head), F32)

                def begin(h):
                    cols = slice(h * head, (h + 1) * head)
                    scores = contract(keys, q_ref[span, cols], 1, 1)
                    if diagonal:
                        key_at = lax.broadcasted_iota(jnp.int32, scores.shape, 0)
                        query_at = lax.broadcasted_iota(jnp.int32, scores.shape, 1)
                        scores = jnp.where(key_at <= query_at, scores, NEG_LARGE)
                    return scores, contract(values, do_ref[span, cols], 1, 1)

                begun = begin(0)
                for h in range(heads):
                    cols = slice(h * head, (h + 1) * head)
                    scores, d_probs = begun
                    if h + 1 < heads:
                        begun = begin(h + 1)
                    probs = jnp.exp(scores - lse_ref[h : h + 1, span])
                    d_scores = (probs * (d_probs - delta[h : h + 1, span])).astype(BF16)
                    d_values += contract(probs.astype(BF16), do_ref[span, cols], 1, 0)
                    d_keys += contract(d_scores, q_ref[span, cols], 1, 0)
                    dq_acc[i, h] += contract(keys, d_scores, 0, 0)
                dkv_acc[at, 0:head] += d_keys
                dkv_acc[at, head : 2 * head] += d_values

            full = (place * rows + i * block) // block - target * parts

            @pl.loop(0, jnp.clip(full, 0, parts))
            def _(j):
                step(j, False)

            @pl.when((full >= 0) & (full < parts))
            def _():
                step(full, True)

            if target == 0 and i == 0:
                @pl.loop(0, chunks)
                def _(k):
                    ts.second(k)

        for b in range(2):
            dkv_ref[2 * target + b] = dkv_acc[b * rows : (b + 1) * rows].astype(BF16)
        if target < levels - 1:
            for _ in range(per_slot):
                if done < length - 1:
                    done += 1
                    chain.arrive(done)
                    if done < length - 1:
                        chain.start(done + 1)
                    else:
                        chain.result(grad_ref)
        if target == levels - 2:
            @pl.loop(0, chunks)
            def _(k):
                ts.third(k)

    for i in range(rows // block):
        span = slice(i * block, (i + 1) * block)
        for h in range(heads):
            dq_ref[span, h * head : (h + 1) * head] = (
                (dq_acc[i, h] * head**-0.5).T.astype(BF16)
            )
    chain.drain()
    wide_step.wait()
    ts.finish(chunks)
    to_x.wait()
    proj_to_x.wait()


def attend_back(
    queries, keyval, d_context, context, lse, pair, far_up, far_down, mlp_part, sent, edge, proj, block=512, chunks=4
):
    rows, width = queries.shape
    head = keyval.shape[1] // 2
    heads = width // head
    hbm = pl.BlockSpec(memory_space=pl.ANY)
    dma = pltpu.SemaphoreType.DMA
    low = lambda shape: jax.ShapeDtypeStruct(shape, BF16)
    return pl.pallas_call(
        functools.partial(attend_back_kernel, block, chunks),
        out_shape=(
            low((rows, width)),
            low((SPAN, rows, 2 * head)),
            jax.ShapeDtypeStruct(pair.shape[1:], F32),
            low(mlp_part.shape),
            low(sent.shape),
            low(edge.shape),
            low(edge.shape),
            low(proj.shape),
        ),
        in_specs=[VMEM] * 9 + [hbm] * 3,
        out_specs=(VMEM,) * 4 + (hbm,) * 4,
        scratch_shapes=[
            pltpu.VMEM((rows // block, heads, head, block), F32),
            pltpu.VMEM((2 * rows, 2 * head), F32),
            pltpu.VMEM((heads, rows), F32),
            dma((2,)),
            dma((2,)),
            dma((2,)),
            dma((2,)),
        ]
        + sum_scratch(chunks, *mlp_part.shape)[1:]
        + chain_scratch(pair.shape[0] - 1, pair.shape[1:]),
        compiler_params=pltpu.CompilerParams(
            collective_id=6, has_side_effects=True, vmem_limit_bytes=63 << 20
        ),
        name="attend_back",
    )(
        queries, keyval, d_context, context, lse, pair, far_up, far_down, mlp_part, sent, edge, proj
    )


def layer_norm(values, norm_gain, norm_bias):
    average = jnp.mean(values, axis=-1, keepdims=True)
    centred = values - average
    variance = jnp.mean(centred * centred, axis=-1, keepdims=True)
    return centred * lax.rsqrt(variance + EPSILON) * norm_gain + norm_bias


def per_device(
    inputs,
    first_gain,
    first_bias,
    query_weight,
    query_bias,
    keyval_weight,
    value_bias,
    output_weight,
    output_bias,
    second_gain,
    second_bias,
    up_weight,
    up_bias,
    down_weight,
    down_bias,
    cotangent,
):
    count = lax.axis_size("dp")
    head_size = value_bias.shape[0]
    score_scale = head_size ** (-0.5)
    x_full = inputs.astype(F32)
    normed1 = layer_norm(x_full, first_gain, first_bias).astype(BF16)
    query_pre = jnp.dot(normed1, query_weight, preferred_element_type=F32) + query_bias
    queries = (query_pre * score_scale).astype(BF16)
    kv_bias = jnp.concatenate([jnp.zeros_like(value_bias), value_bias])
    keyval = (jnp.dot(normed1, keyval_weight, preferred_element_type=F32) + kv_bias).astype(BF16)
    keyval_all, context_low, lse, attn_sum, d_activ, far_cotangent = front(
        queries, keyval, cotangent, output_weight, down_weight
    )
    keyval_all = keyval_all.reshape(-1, keyval.shape[1])
    normed2, activ, d_pre, d_up_bias = hidden_stage(
        inputs, attn_sum, d_activ, up_weight, up_bias, output_bias, second_gain, second_bias
    )
    d_up_bias = d_up_bias[0]
    d_normed2, up_own, up_other, pair_down, out_part = hidden_back(
        d_pre, up_weight, normed2, activ, cotangent, far_cotangent, down_weight, count
    )
    d_middle, d_context, out_part, proj_own, proj_other, row_sums, edge, far_up, far_down = middle_stage(
        d_normed2,
        inputs,
        attn_sum,
        cotangent,
        output_bias,
        second_gain,
        down_bias,
        out_part,
        output_weight,
        context_low,
        pair_down,
        up_own,
        up_other,
        count,
    )
    d_queries, d_kv_parts, half_down, layer_out, rest, wide_up, wide_down, proj_got = attend_back(
        queries,
        keyval_all,
        d_context,
        context_low,
        lse,
        pair_down,
        far_up,
        far_down,
        out_part,
        up_other,
        edge,
        proj_other,
    )
    length = count // 2
    at_edge = jnp.where(lax.axis_index("dp") // 2 < length // 2, length - 1, 0)
    pair_up = (up_own.astype(F32) + rest.astype(F32)).astype(BF16)
    pair_up = lax.dynamic_update_index_in_dim(pair_up, edge, at_edge, 0)
    d_query_bias = jnp.sum(d_queries.astype(F32), axis=0)
    d_normed1, sent_query, sent_proj, d_keyval, far_up, far_down = query_back(
        d_queries,
        query_weight,
        normed1,
        d_kv_parts,
        pair_up,
        wide_up,
        wide_down,
        proj_own,
        proj_got,
        count,
    )
    grad_inputs, first_sums = norm_back(
        d_keyval, keyval_weight, d_normed1, inputs, d_middle, first_gain
    )
    sent_kv, sums, sent_up, sent_down = finish(
        normed1,
        d_keyval,
        [first_sums[:3], row_sums[:4]],
        [d_up_bias, d_query_bias],
        pair_up,
        far_up,
        far_down,
        half_down,
        count,
    )
    local = query_weight.shape[1]
    hidden = d_up_bias.shape[0]
    flat = sums[7:].reshape(-1)
    return (
        layer_out,
        grad_inputs,
        sums[0],
        sums[1],
        sent_query,
        flat[hidden : hidden + local],
        sent_kv,
        sums[2, head_size : 2 * head_size],
        sent_proj.T,
        sums[5],
        sums[3],
        sums[4],
        sent_up,
        flat[:hidden],
        sent_down.T,
        sums[6],
    )


def solution(mesh):
    in_specs = (
        P("dp", None),
        P(),
        P(),
        P(None, "tensor"),
        P("tensor"),
        P(),
        P(),
        P("tensor", None),
        P(),
        P(),
        P(),
        P(None, "tensor"),
        P("tensor"),
        P("tensor", None),
        P(),
        P("dp", None),
    )
    out_specs = (
        P("dp", None),
        P("dp", None),
        P(),
        P(),
        P("dp", "tensor"),
        P("tensor"),
        P("dp", None),
        P(),
        P("tensor", "dp"),
        P(),
        P(),
        P(),
        P("dp", "tensor"),
        P("tensor"),
        P("tensor", "dp"),
        P(),
    )
    return jax.shard_map(
        per_device, mesh=mesh, in_specs=in_specs, out_specs=out_specs, check_vma=False
    )
```

```python
import functools

import jax
import jax.numpy as jnp
from jax import lax
from jax.experimental import pallas as pl
from jax.experimental.pallas import tpu as pltpu
from jax.sharding import PartitionSpec as P

SPAN = 8
EPSILON = 1e-05
NEG_LARGE = -1e30
MESH = pl.DeviceIdType.MESH
VMEM = pl.BlockSpec(memory_space=pltpu.VMEM)
F32 = jnp.float32
BF16 = jnp.bfloat16


def contract(left, right, left_dim, right_dim):
    return lax.dot_general(
        left, right, (((left_dim,), (right_dim,)), ((), ())), preferred_element_type=F32
    )


def remote(source, target, send_sem, recv_sem, device):
    return pltpu.make_async_remote_copy(
        src_ref=source,
        dst_ref=target,
        send_sem=send_sem,
        recv_sem=recv_sem,
        device_id=device,
        device_id_type=MESH,
    )


def greet(devices):
    barrier = pltpu.get_barrier_semaphore()
    for device in devices:
        pl.semaphore_signal(barrier, inc=1, device_id=device, device_id_type=MESH)
    pl.semaphore_wait(barrier, len(devices))


class TensorSum:
    def __init__(self, chunks, part, result, from_core, summed, from_y, sems):
        block = lax.axis_index("dp")
        lane = lax.axis_index("tensor")
        core = lax.rem(lane, 2)
        self.core_peer = (block, lane + 1 - 2 * core)
        self.y_peer = (block, lax.rem(lane + 2, 4))
        rows, width = part.shape
        half = width // 2
        self.step = rows // chunks
        self.mine = pl.ds(pl.multiple_of(core * half, half), half)
        self.other = pl.ds(pl.multiple_of((1 - core) * half, half), half)
        self.part, self.result = part, result
        self.from_core, self.summed, self.from_y = from_core, summed, from_y
        self.sems = sems

    def span(self, k):
        return pl.ds(pl.multiple_of(k * self.step, self.step), self.step)

    def to_core(self, k):
        at = self.span(k)
        return remote(
            self.part.at[at, self.other], self.from_core.at[at], self.sems[0].at[k],
            self.sems[1].at[k], self.core_peer,
        )

    def to_y(self, k):
        at = self.span(k)
        return remote(
            self.summed.at[at], self.from_y.at[at], self.sems[2].at[k], self.sems[3].at[k],
            self.y_peer,
        )

    def back(self, k):
        at = self.span(k)
        return remote(
            self.result.at[at, self.mine], self.result.at[at, self.mine], self.sems[4].at[k],
            self.sems[5].at[k], self.core_peer,
        )

    def first(self, k):
        self.to_core(k).start()

    def second(self, k):
        at = self.span(k)
        self.to_core(k).wait_recv()
        total = self.part[at, self.mine].astype(F32) + self.from_core[at].astype(F32)
        self.summed[at] = total.astype(BF16)
        self.to_y(k).start()

    def third(self, k):
        at = self.span(k)
        self.to_y(k).wait_recv()
        total = self.summed[at].astype(F32) + self.from_y[at].astype(F32)
        self.result[at, self.mine] = total.astype(BF16)
        self.back(k).start()

    def finish(self, chunks):
        @pl.loop(0, chunks)
        def _(k):
            self.back(k).wait_recv()
            self.back(k).wait_send()
            self.to_core(k).wait_send()
            self.to_y(k).wait_send()


def sum_scratch(chunks, rows, width):
    half = pltpu.VMEM((rows, width // 2), BF16)
    return [pltpu.VMEM((rows, width), BF16), half, half, half] + [
        pltpu.SemaphoreType.DMA((chunks,))
    ] * 6


def grad_rows(left_ref, right, target, which):
    levels, rows = target.shape[0], target.shape[1]

    @pl.loop(0, levels)
    def _(lev):
        if rows % 128 == 0:
            cols = pl.ds(pl.multiple_of((2 * lev + which) * rows, rows), rows)
            target[lev] = contract(left_ref[:, cols], right[...], 0, 0).astype(BF16)
        else:
            cols = pl.ds(pl.multiple_of(2 * lev * rows, 2 * rows), 2 * rows)
            both = contract(left_ref[:, cols], right[...], 0, 0)
            target[lev] = jnp.where(which == 0, both[:rows], both[rows:]).astype(BF16)


def hidden_kernel(tiles, x_ref, attn_ref, g_ref, wu_ref, bias_ref, vec_ref, n2_ref, act_ref, dpre_ref, sums_ref, acc):
    step = pl.program_id(0)

    @pl.when(step == 0)
    def _():
        acc[...] = jnp.zeros_like(acc)

    rows = x_ref.shape[0]
    values = x_ref[...].astype(F32) + attn_ref[...].astype(F32) + vec_ref[0:1, :]
    centred = values - jnp.mean(values, axis=-1, keepdims=True)
    scale = lax.rsqrt(jnp.mean(centred * centred, axis=-1, keepdims=True) + EPSILON)
    n2_ref[...] = (centred * scale * vec_ref[1:2, :] + vec_ref[2:3, :]).astype(BF16)
    tile = wu_ref.shape[1] // tiles
    root = 0.7978845608028654
    for j in range(tiles):
        cols = slice(j * tile, (j + 1) * tile)
        pre = jnp.dot(n2_ref[...], wu_ref[:, cols], preferred_element_type=F32) + bias_ref[0:1, cols]
        square = pre * pre
        bend = jnp.tanh(root * pre * (1.0 + 0.044715 * square))
        half = 0.5 * (1.0 + bend)
        act_ref[:, cols] = (pre * half).astype(BF16)
        slope = half + (0.5 * root) * pre * (1.0 - bend * bend) * (1.0 + (3 * 0.044715) * square)
        d_pre = (g_ref[:, cols].astype(F32) * slope).astype(BF16)
        dpre_ref[:, cols] = d_pre
        acc[:, cols] += jnp.sum(d_pre.astype(F32).reshape(rows // 8, 8, tile), axis=0)

    @pl.when(step == pl.num_programs(0) - 1)
    def _():
        sums_ref[...] = jnp.sum(acc[...], axis=0, keepdims=True)


def hidden_stage(inputs, attn_sum, d_activ, up_weight, up_bias, output_bias, gain, bias, block=256, tiles=4):
    rows, width = inputs.shape
    wide = up_weight.shape[1]
    vec = jnp.pad(jnp.stack([output_bias, gain, bias]), ((0, 5), (0, 0)))
    row = lambda cols: pl.BlockSpec((block, cols), lambda k: (k, 0))
    fixed = lambda shape: pl.BlockSpec(shape, lambda k: (0, 0))
    return pl.pallas_call(
        functools.partial(hidden_kernel, tiles),
        grid=(rows // block,),
        out_shape=(
            jax.ShapeDtypeStruct((rows, width), BF16),
            jax.ShapeDtypeStruct((rows, wide), BF16),
            jax.ShapeDtypeStruct((rows, wide), BF16),
            jax.ShapeDtypeStruct((1, wide), F32),
        ),
        in_specs=[
            row(width),
            row(width),
            row(wide),
            pl.BlockSpec(up_weight.shape, lambda k: (0, 0), pipeline_mode=pl.Buffered(1)),
            fixed((1, wide)),
            fixed((8, width)),
        ],
        out_specs=(row(width), row(wide), row(wide), fixed((1, wide))),
        scratch_shapes=[pltpu.VMEM((8, wide), F32)],
        compiler_params=pltpu.CompilerParams(vmem_limit_bytes=60 << 20),
        name="hidden",
    )(inputs, attn_sum, d_activ, up_weight, up_bias.reshape(1, wide), vec)


def hidden_back_kernel(
    chunks, dpre_ref, wu_hbm, n2_hbm, activ_hbm, cot_hbm, far_hbm, wd_hbm, dn_ref, own_out, other_out, down_out,
    mlp_out, weight_ref, n2_ref, activ_ref, cot_ref, far_ref, own_ref, other_ref, down_ref, mlp_ref, in_sem, out_sem,
    mlp_sem, activ_x, x_send, x_recv, part,
    from_core, summed, from_y, *sems,
):
    ts = TensorSum(chunks, part, dn_ref, from_core, summed, from_y, sems)
    side = lax.rem(lax.axis_index("dp"), 2)
    x_peer = (lax.axis_index("dp") + 1 - 2 * side, lax.axis_index("tensor"))
    half = activ_x.shape[1]
    mine = pl.ds(pl.multiple_of(side * half, half), half)
    theirs = pl.ds(pl.multiple_of((1 - side) * half, half), half)
    local = [
        pltpu.make_async_copy(source, target, in_sem.at[n])
        for n, (source, target) in enumerate(
            [
                (wu_hbm, weight_ref),
                (n2_hbm, n2_ref),
                (activ_hbm, activ_ref),
                (cot_hbm, cot_ref),
                (far_hbm, far_ref),
                (wd_hbm, weight_ref),
            ]
        )
    ]
    results = [
        pltpu.make_async_copy(source, target, out_sem.at[n])
        for n, (source, target) in enumerate(
            [(other_ref, other_out), (own_ref, own_out), (down_ref, down_out)]
        )
    ]
    local[0].start()
    greet([ts.core_peer, ts.y_peer, x_peer])
    to_x = remote(activ_hbm.at[:, theirs], activ_x, x_send, x_recv, x_peer)
    to_x.start()
    for copy in local[1:5]:
        copy.start()
    local[0].wait()

    @pl.loop(0, chunks)
    def _(k):
        at = ts.span(k)
        part[at, :] = contract(dpre_ref[at, :], weight_ref[...], 1, 1).astype(BF16)
        ts.first(k)

        @pl.when(k >= 1)
        def _():
            ts.second(k - 1)

    ts.second(chunks - 1)
    local[5].start()
    local[1].wait()
    grad_rows(n2_ref, dpre_ref, other_ref, 1 - side)
    results[0].start()
    grad_rows(n2_ref, dpre_ref, own_ref, side)
    results[1].start()
    levels, rows = down_ref.shape[0], down_ref.shape[1]
    local[2].wait()
    local[3].wait()

    @pl.loop(0, levels)
    def _(lev):
        cols = pl.ds(pl.multiple_of(lev * rows, rows), rows)
        down_ref[lev] = contract(cot_ref[:, cols], activ_ref[:, mine], 0, 0).astype(BF16)

    ready = chunks // 2

    @pl.loop(0, ready)
    def _(k):
        ts.third(k)

    local[5].wait()
    tiles = 4
    tile = mlp_ref.shape[2]

    def mlp_copy(j):
        cols = pl.ds(pl.multiple_of(j * tile, tile), tile)
        slot = lax.rem(j, 2)
        return pltpu.make_async_copy(mlp_ref.at[slot], mlp_out.at[:, cols], mlp_sem.at[slot])

    @pl.loop(0, tiles)
    def _(j):
        @pl.when(j >= 2)
        def _():
            mlp_copy(j - 2).wait()

        cols = pl.ds(pl.multiple_of(j * tile, tile), tile)
        mlp_ref[lax.rem(j, 2)] = jnp.dot(
            activ_ref[...], weight_ref[:, cols], preferred_element_type=F32
        ).astype(BF16)
        mlp_copy(j).start()

    local[4].wait()
    to_x.wait_recv()

    @pl.loop(0, levels)
    def _(lev):
        cols = pl.ds(pl.multiple_of(lev * rows, rows), rows)
        far = contract(far_ref[:, cols], activ_x[...], 0, 0)
        down_ref[lev] = (down_ref[lev].astype(F32) + far).astype(BF16)

    results[2].start()

    @pl.loop(ready, chunks)
    def _(k):
        ts.third(k)

    ts.finish(chunks)
    to_x.wait_send()
    for copy in results:
        copy.wait()
    for j in (tiles - 2, tiles - 1):
        mlp_copy(j).wait()


def hidden_back(
    d_pre, up_weight, normed2, activ, cotangent, far_cotangent, down_weight, count, chunks=4
):
    rows, width = d_pre.shape[0], up_weight.shape[0]
    hidden = up_weight.shape[1]
    levels = count // 2
    half = (levels, width // count, hidden)
    down = (levels, width // levels, hidden // 2)
    dma = pltpu.SemaphoreType.DMA
    hbm = pl.BlockSpec(memory_space=pl.ANY)
    return pl.pallas_call(
        functools.partial(hidden_back_kernel, chunks),
        out_shape=(
            jax.ShapeDtypeStruct((rows, width), BF16),
            jax.ShapeDtypeStruct(half, BF16),
            jax.ShapeDtypeStruct(half, BF16),
            jax.ShapeDtypeStruct(down, BF16),
            jax.ShapeDtypeStruct((rows, width), BF16),
        ),
        in_specs=[VMEM] + [hbm] * 6,
        out_specs=(VMEM,) + (hbm,) * 4,
        scratch_shapes=[
            pltpu.VMEM(up_weight.shape, BF16),
            pltpu.VMEM((rows, width), BF16),
            pltpu.VMEM((rows, hidden), BF16),
            pltpu.VMEM((rows, width), BF16),
            pltpu.VMEM((rows, width), BF16),
            pltpu.VMEM(half, BF16),
            pltpu.VMEM(half, BF16),
            pltpu.VMEM(down, BF16),
            pltpu.VMEM((2, rows, width // 4), BF16),
            dma((6,)),
            dma((3,)),
            dma((2,)),
            pltpu.VMEM((rows, hidden // 2), BF16),
            dma,
            dma,
        ]
        + sum_scratch(chunks, rows, width),
        compiler_params=pltpu.CompilerParams(
            collective_id=4, has_side_effects=True, vmem_limit_bytes=62 << 20
        ),
        name="hidden_back",
    )(d_pre, up_weight, normed2, activ, cotangent, far_cotangent, down_weight)


class Chain:
    def __init__(self, length, level, upper, lower, pair, bufs, sems, early=None):
        self.length, self.level = length, level
        self.peers = (upper, lower)
        self.pair = pair
        self.bufs = bufs
        self.sems = sems
        self.early = early
        self.skip = 0 if early is None else 1

    def copy(self, way, s):
        at = s - 1 - self.skip
        inward, outward = self.bufs[2 * way], self.bufs[2 * way + 1]
        send, recv = self.sems[2 * way], self.sems[2 * way + 1]
        return remote(outward.at[at], inward.at[at], send.at[at], recv.at[at], self.peers[way])

    def arrived(self, way, s):
        if s == 1 and self.early is not None:
            return self.early[way][...]
        return self.bufs[2 * way][s - 1 - self.skip]

    def rank(self, way):
        return self.level if way == 0 else self.length - 1 - self.level

    def start(self, s):
        for way in range(2):
            rank = self.rank(way)
            slot = rank + self.length - s
            slot = jnp.clip(slot if way == 0 else self.length - 1 - slot, 0, self.length - 1)
            outward = self.bufs[2 * way + 1]
            at = s - 1 - self.skip

            @pl.when(rank <= s - 1)
            def _(way=way, rank=rank, slot=slot, outward=outward, at=at):
                outward[at] = self.pair[slot]
                if s > 1:
                    @pl.when(rank >= 1)
                    def _():
                        outward[at] = (
                            self.pair[slot].astype(F32) + self.arrived(way, s - 1).astype(F32)
                        ).astype(BF16)

                self.copy(way, s).start()

    def arrive(self, s):
        for way in range(2):
            rank = self.rank(way)

            @pl.when((rank >= 1) & (rank <= s))
            def _(way=way):
                self.copy(way, s).wait_recv()

    def result(self, target):
        target[...] = self.pair[self.level].astype(F32)
        for way in range(2):
            @pl.when(self.rank(way) >= 1)
            def _(way=way):
                target[...] += self.arrived(way, self.length - 1).astype(F32)

    def drain(self, last=None):
        for s in range(1 + self.skip, (last or self.length - 1) + 1):
            for way in range(2):
                rank = self.rank(way)

                @pl.when(rank <= s - 1)
                def _(way=way, s=s):
                    self.copy(way, s).wait_send()


class FirstStep:
    def __init__(self, length, level, upper, lower, sources, targets, send, recv):
        self.length, self.level = length, level
        self.copies = [
            remote(sources[way], targets[way], send.at[way], recv.at[way], (upper, lower)[way])
            for way in range(2)
        ]

    def each(self, rank, act):
        for way in range(2):
            mine = self.level if way == 0 else self.length - 1 - self.level

            @pl.when(mine == rank)
            def _(way=way):
                act(self.copies[way])

    def start(self):
        self.each(0, lambda copy: copy.start())

    def wait(self):
        self.each(1, lambda copy: copy.wait_recv())
        self.each(0, lambda copy: copy.wait_send())


def chain_scratch(length, shape):
    return [pltpu.VMEM((length - 1,) + shape, BF16)] * 4 + [
        pltpu.SemaphoreType.DMA((length - 1,))
    ] * 4


def chain_peers():
    count = lax.axis_size("dp")
    block = lax.axis_index("dp")
    lane = lax.axis_index("tensor")
    level = block // 2
    upper = (jnp.where(level < count // 2 - 1, block + 2, block + 2 - count), lane)
    lower = (jnp.where(level > 0, block - 2, block - 2 + count), lane)
    return count // 2, level, upper, lower


def middle_kernel(
    chunk, vec_ref, dn_hbm, x_hbm, attn_hbm, cot_hbm, part_hbm, wo_hbm, ctx_hbm, down_hbm, own_hbm, other_hbm,
    dm_out, dctx_ref, mlp_out, out_own, out_other, sums_ref, edge_ref, far_up, far_down, dm_ref, x_ref, attn_ref,
    cot_ref, mlp_ref, row_sem, out_sem, wo_ref, ctx_ref, edge_own, edge_got, local_sem, x_send, x_recv, z_send, z_recv, acc,
):
    dp = lax.axis_index("dp")
    lane = lax.axis_index("tensor")
    side = lax.rem(dp, 2)
    x_peer = (dp + 1 - 2 * side, lane)
    length, level, upper, lower = chain_peers()
    edge = jnp.where(level < length // 2, length - 1, 0)
    local = [
        pltpu.make_async_copy(source, target, local_sem.at[n])
        for n, (source, target) in enumerate(
            [
                (wo_hbm, wo_ref),
                (ctx_hbm, ctx_ref),
                (own_hbm.at[edge], edge_own),
            ]
        )
    ]
    half = x_ref.shape[0] // 2
    rows_in = [
        [
            pltpu.make_async_copy(
                source.at[pl.ds(n * half, half)], target.at[pl.ds(n * half, half)], row_sem.at[n, k]
            )
            for k, (source, target) in enumerate(
                [
                    (x_hbm, x_ref),
                    (attn_hbm, attn_ref),
                    (dn_hbm, dm_ref),
                    (cot_hbm, cot_ref),
                    (part_hbm, mlp_ref),
                ]
            )
        ]
        for n in range(2)
    ]
    rows_out = [
        [
            pltpu.make_async_copy(
                source.at[pl.ds(n * half, half)], target.at[pl.ds(n * half, half)], out_sem.at[n, k]
            )
            for k, (source, target) in enumerate([(dm_ref, dm_out), (mlp_ref, mlp_out)])
        ]
        for n in range(2)
    ]
    for copy in rows_in[0] + rows_in[1]:
        copy.start()
    for copy in local:
        copy.start()
    greet([x_peer, upper, lower])
    to_x = remote(other_hbm.at[edge], edge_got, x_send, x_recv, x_peer)
    to_x.start()
    first_step = FirstStep(
        length, level, upper, lower, (down_hbm.at[length - 1], down_hbm.at[0]), (far_up, far_down), z_send,
        z_recv,
    )
    first_step.start()
    rows, width = x_ref.shape
    acc[...] = jnp.zeros_like(acc)
    share = 1.0 / lax.axis_size("tensor")

    def fold(values):
        return jnp.sum(values.reshape(chunk // 8, 8, width), axis=0)

    def norm_rows(k):
        at = pl.ds(pl.multiple_of(k * chunk, chunk), chunk)
        values = x_ref[at, :].astype(F32) + attn_ref[at, :].astype(F32) + vec_ref[0:1, :]
        base = share * (values + vec_ref[2:3, :])
        mlp_ref[at, :] = (mlp_ref[at, :].astype(F32) + base).astype(BF16)
        centred = values - jnp.mean(values, axis=-1, keepdims=True)
        scale = lax.rsqrt(jnp.mean(centred * centred, axis=-1, keepdims=True) + EPSILON)
        hat = centred * scale
        grad = dm_ref[at, :].astype(F32)
        acc[0] += fold(grad * hat)
        acc[1] += fold(grad)
        scaled = grad * vec_ref[1:2, :]
        first = jnp.mean(scaled, axis=-1, keepdims=True)
        second = jnp.mean(scaled * hat, axis=-1, keepdims=True)
        cot = cot_ref[at, :].astype(F32)
        d_middle = cot + scale * (scaled - first - hat * second)
        acc[2] += fold(d_middle)
        acc[3] += fold(cot)
        dm_ref[at, :] = d_middle.astype(BF16)

    each = rows // chunk // 2
    for n in range(2):
        for copy in rows_in[n]:
            copy.wait()

        @pl.loop(n * each, (n + 1) * each)
        def _(k):
            norm_rows(k)

        for copy in rows_out[n]:
            copy.start()
    for n in range(4):
        sums_ref[n : n + 1, :] = jnp.sum(acc[n], axis=0, keepdims=True)
    sums_ref[4:8, :] = jnp.zeros((4, width), F32)
    local[0].wait()

    @pl.loop(0, 4)
    def _(k):
        at = pl.ds(pl.multiple_of(k * (rows // 4), rows // 4), rows // 4)
        dctx_ref[at, :] = contract(dm_ref[at, :], wo_ref[...], 1, 1).astype(BF16)

    local[1].wait()
    grad_rows(dm_ref, ctx_ref, out_other, 1 - side)
    grad_rows(dm_ref, ctx_ref, out_own, side)
    local[2].wait()
    for copy in rows_out[0] + rows_out[1]:
        copy.wait()
    to_x.wait()
    edge_ref[...] = (edge_own[...].astype(F32) + edge_got[...].astype(F32)).astype(BF16)
    first_step.wait()


def middle_stage(
    d_normed2, inputs, attn_sum, cotangent, output_bias, gain, down_bias, part, output_weight, context, down,
    up_own, up_other, count, chunk=128,
):
    rows, width = inputs.shape
    heads = context.shape[1]
    vec = jnp.stack([output_bias, gain, down_bias])
    vec = jnp.pad(vec, ((0, 5), (0, 0)))
    half = jax.ShapeDtypeStruct((count // 2, width // count, heads), BF16)
    hbm = pl.BlockSpec(memory_space=pl.ANY)
    dma = pltpu.SemaphoreType.DMA
    low = lambda shape: jax.ShapeDtypeStruct(shape, BF16)
    edge = pltpu.VMEM(up_own.shape[1:], BF16)
    return pl.pallas_call(
        functools.partial(middle_kernel, chunk),
        out_shape=(
            low((rows, width)),
            low((rows, heads)),
            low((rows, width)),
            half,
            half,
            jax.ShapeDtypeStruct((8, width), F32),
            low(up_own.shape[1:]),
            low(down.shape[1:]),
            low(down.shape[1:]),
        ),
        in_specs=[VMEM] + [hbm] * 10,
        out_specs=(hbm, VMEM, hbm) + (VMEM,) * 4 + (hbm,) * 2,
        scratch_shapes=[pltpu.VMEM((rows, width), BF16)] * 5
        + [
            dma((2, 5)),
            dma((2, 2)),
            pltpu.VMEM(output_weight.shape, BF16),
            pltpu.VMEM(context.shape, BF16),
            edge,
            edge,
            dma((3,)),
            dma,
            dma,
            dma((2,)),
            dma((2,)),
            pltpu.VMEM((4, 8, width), F32),
        ],
        compiler_params=pltpu.CompilerParams(
            collective_id=7, has_side_effects=True, vmem_limit_bytes=60 << 20
        ),
        name="middle",
    )(
        vec, d_normed2, inputs, attn_sum, cotangent, part, output_weight, context, down, up_own, up_other,
    )


def query_back_kernel(
    chunks, steps, dq_ref, wq_ref, n1_ref, dkv_ref, wide_ref, wide_up, wide_down, proj_ref, proj_x, dn_ref,
    grad_ref, proj_grad, tot_ref, far_up, far_down, kv_local, part, from_core, summed, from_y, kv_core, kv_sum, kv_x,
    kv_pair, kv_z, kv_up, kv_y, kv_sems, own_ref, other_ref, got_ref, q_send, q_recv, proj_pair, *rest,
):
    chain_bufs, chain_sems, sems = rest[:4], rest[4:8], rest[8:14]
    wide_bufs, wide_sems = rest[14:18], rest[18:22]
    proj_bufs, proj_sems = rest[22:26], rest[26:]
    ts = TensorSum(chunks, part, dn_ref, from_core, summed, from_y, sems)
    block = lax.axis_index("dp")
    lane = lax.axis_index("tensor")
    place = lax.rem(block, SPAN)
    side = lax.rem(place, 2)
    level = place // 2
    levels = SPAN // 2
    x_peer = (block + 1 - 2 * side, lane)
    upper = (jnp.where(level < levels - 1, block + 2, block + 2 - SPAN), lane)
    lower = (jnp.where(level > 0, block - 2, block - 2 + SPAN), lane)
    length, chain_level, chain_upper, chain_lower = chain_peers()
    if length == levels:
        greet([ts.core_peer, ts.y_peer, x_peer, upper, lower])
    else:
        greet([ts.core_peer, ts.y_peer, x_peer, upper, lower, chain_upper, chain_lower])
    chain = Chain(length, chain_level, chain_upper, chain_lower, own_ref, chain_bufs, chain_sems)
    early = (wide_up, wide_down)
    wide = Chain(length, chain_level, chain_upper, chain_lower, wide_ref, wide_bufs, wide_sems, early)
    proj = Chain(length, chain_level, chain_upper, chain_lower, proj_pair, proj_bufs, proj_sems)
    core = lax.rem(lane, 2)
    seq_rows = tot_ref.shape[0]
    half = seq_rows // 2
    mine = pl.ds(pl.multiple_of(core * half, half), half)
    other = pl.ds(pl.multiple_of((1 - core) * half, half), half)

    def kv_copy(source, target, index, device):
        return remote(source, target, kv_sems.at[0, index], kv_sems.at[1, index], device)

    to_core = [
        kv_copy(
            dkv_ref.at[pl.ds(2 * lev, 2), other], kv_core.at[lev], 3 + levels + lev, ts.core_peer
        )
        for lev in range(levels)
    ]
    keep = [
        pltpu.make_async_copy(dkv_ref.at[pl.ds(2 * lev, 2), mine], kv_sum.at[lev], kv_local.at[lev])
        for lev in range(levels)
    ]
    for copy in to_core + keep:
        copy.start()
    proj_pair[...] = (proj_ref[...].astype(F32) + proj_x[...].astype(F32)).astype(BF16)
    proj.start(1)
    wide.start(2)
    grad_levels, rows = own_ref.shape[0], own_ref.shape[1]
    for lev in range(levels):
        to_core[lev].wait_recv()
        keep[lev].wait()
        kv_sum[lev] = (kv_sum[lev].astype(F32) + kv_core[lev].astype(F32)).astype(BF16)

    to_x = kv_copy(kv_sum.at[:, 1 - side], kv_x, 1, x_peer)
    to_x.start()

    @pl.loop(0, chunks)
    def _(k):
        at = ts.span(k)
        part[at, :] = contract(dq_ref[at, :], wq_ref[...], 1, 1).astype(BF16)
        ts.first(k)

        @pl.when(k >= 1)
        def _():
            ts.second(k - 1)

    ts.second(chunks - 1)

    def grad(target, which):
        grad_rows(n1_ref, dq_ref, target, which)

    grad(other_ref, 1 - side)
    q_to_x = remote(other_ref, got_ref, q_send, q_recv, x_peer)
    grad(own_ref, side)
    for s in range(1, length - 1):
        proj.arrive(s)
        proj.start(s + 1)
    to_x.wait_recv()
    q_to_x.start()

    @pl.loop(0, levels)
    def _(lev):
        kv_pair[lev] = (kv_sum[lev, side].astype(F32) + kv_x[lev].astype(F32)).astype(BF16)

    def down(s):
        slot = jnp.maximum(level - levels + s, 0)
        return kv_copy(kv_up.at[s - 1], kv_z.at[s - 1], 1 + s, lower), slot

    for s in range(1, levels):
        copy, slot = down(s)

        @pl.when(level >= levels - s)
        def _(copy=copy, slot=slot, s=s):
            kv_up[s - 1] = kv_pair[slot]
            if s > 1:
                @pl.when(level < levels - 1)
                def _():
                    kv_up[s - 1] = (
                        kv_pair[slot].astype(F32) + kv_z[s - 2].astype(F32)
                    ).astype(BF16)

            copy.start()

        @pl.when((level >= levels - 1 - s) & (level < levels - 1))
        def _(copy=copy):
            copy.wait_recv()

    kv_up[levels - 1] = kv_pair[level]

    @pl.when(level < levels - 1)
    def _():
        kv_up[levels - 1] = (
            kv_pair[level].astype(F32) + kv_z[levels - 2].astype(F32)
        ).astype(BF16)

    to_y = kv_copy(kv_up.at[levels - 1], kv_y, 1 + levels, ts.y_peer)
    to_y.start()
    for s in range(2, steps):
        wide.arrive(s)
        wide.start(s + 1)
    q_to_x.wait_recv()

    @pl.loop(0, grad_levels)
    def _(lev):
        own_ref[lev] = (own_ref[lev].astype(F32) + got_ref[lev].astype(F32)).astype(BF16)

    chain.start(1)
    to_y.wait_recv()
    tot_ref[mine] = (kv_up[levels - 1].astype(F32) + kv_y[...].astype(F32)).astype(BF16)
    back = kv_copy(tot_ref.at[mine], tot_ref.at[mine], 2 + levels, ts.core_peer)
    back.start()
    half_way = chunks // 2
    for s in range(1, length):
        if s == 2:
            @pl.loop(0, half_way)
            def _(k):
                ts.third(k)

        chain.arrive(s)
        if s + 1 < length:
            chain.start(s + 1)

    @pl.loop(half_way, chunks)
    def _(k):
        ts.third(k)

    chain.result(grad_ref)
    proj.arrive(length - 1)
    proj.result(proj_grad)
    wide.arrive(steps)
    far_up[...] = wide.arrived(0, steps)
    far_down[...] = wide.arrived(1, steps)
    chain.drain()
    proj.drain()
    wide.drain(steps)
    q_to_x.wait_send()
    back.wait()
    for copy in to_core:
        copy.wait_send()
    to_x.wait_send()
    to_y.wait_send()
    for s in range(1, levels):
        copy, _slot = down(s)

        @pl.when(level >= levels - s)
        def _(copy=copy):
            copy.wait_send()

    ts.finish(chunks)


def query_back(
    d_queries, query_weight, normed1, parts, wide, wide_up, wide_down, proj, proj_x, count, chunks=4
):
    rows, width = d_queries.shape[0], query_weight.shape[0]
    kv_width = parts.shape[2]
    steps = count // 2 - 2
    levels = SPAN // 2
    shape = (width // count, query_weight.shape[1])
    half = pltpu.VMEM((count // 2,) + shape, BF16)
    piece = (rows // 2, kv_width)
    return pl.pallas_call(
        functools.partial(query_back_kernel, chunks, steps),
        out_shape=(
            jax.ShapeDtypeStruct((rows, width), BF16),
            jax.ShapeDtypeStruct(shape, F32),
            jax.ShapeDtypeStruct(proj.shape[1:], F32),
            jax.ShapeDtypeStruct((rows, kv_width), BF16),
            jax.ShapeDtypeStruct(wide.shape[1:], BF16),
            jax.ShapeDtypeStruct(wide.shape[1:], BF16),
        ),
        in_specs=[VMEM] * 3 + [pl.BlockSpec(memory_space=pl.ANY)] + [VMEM] * 5,
        out_specs=(VMEM,) * 6,
        scratch_shapes=[
            pltpu.SemaphoreType.DMA((levels,)),
        ]
        + sum_scratch(chunks, rows, width)[:4]
        + [
            pltpu.VMEM((levels, 2) + piece, BF16),
            pltpu.VMEM((levels, 2) + piece, BF16),
            pltpu.VMEM((levels,) + piece, BF16),
            pltpu.VMEM((levels,) + piece, BF16),
            pltpu.VMEM((levels - 1,) + piece, BF16),
            pltpu.VMEM((levels,) + piece, BF16),
            pltpu.VMEM(piece, BF16),
            pltpu.SemaphoreType.DMA((2, 3 + 2 * levels)),
            half,
            half,
            half,
            pltpu.SemaphoreType.DMA,
            pltpu.SemaphoreType.DMA,
            pltpu.VMEM(proj.shape, BF16),
        ]
        + chain_scratch(count // 2, shape)
        + [pltpu.SemaphoreType.DMA((chunks,))] * 6
        + chain_scratch(steps, wide.shape[1:])
        + chain_scratch(count // 2, proj.shape[1:]),
        compiler_params=pltpu.CompilerParams(
            collective_id=5, has_side_effects=True, vmem_limit_bytes=63 << 20
        ),
        name="query_back",
    )(d_queries, query_weight, normed1, parts, wide, wide_up, wide_down, proj, proj_x)


def norm_back_kernel(
    dkv_ref, wkv_ref, dn_ref, x_ref, dm_ref, gain_ref, pass_in, grad_x, sums_ref, pass_out, acc, acc_kv
):
    k = pl.program_id(0)
    pass_out[...] = pass_in[...]

    @pl.when(k == 0)
    def _():
        acc[...] = jnp.zeros_like(acc)
        acc_kv[...] = jnp.zeros_like(acc_kv)

    chunk, width = x_ref.shape

    def fold(values):
        return jnp.sum(values.reshape(chunk // 8, 8, values.shape[1]), axis=0)

    values = x_ref[...].astype(F32)
    centred = values - jnp.mean(values, axis=-1, keepdims=True)
    scale = lax.rsqrt(jnp.mean(centred * centred, axis=-1, keepdims=True) + EPSILON)
    hat = centred * scale
    grad = dn_ref[...].astype(F32) + contract(dkv_ref[...], wkv_ref[...], 1, 1)
    acc[0] += fold(grad * hat)
    acc[1] += fold(grad)
    acc_kv[...] += fold(dkv_ref[...].astype(F32))
    scaled = grad * gain_ref[...]
    first = jnp.mean(scaled, axis=-1, keepdims=True)
    second = jnp.mean(scaled * hat, axis=-1, keepdims=True)
    grad_x[...] = dm_ref[...].astype(F32) + scale * (scaled - first - hat * second)

    @pl.when(k == pl.num_programs(0) - 1)
    def _():
        sums_ref[...] = jnp.zeros_like(sums_ref)
        sums_ref[0:1, :] = jnp.sum(acc[0], axis=0, keepdims=True)
        sums_ref[1:2, :] = jnp.sum(acc[1], axis=0, keepdims=True)
        sums_ref[2:3, 0 : acc_kv.shape[1]] = jnp.sum(acc_kv[...], axis=0, keepdims=True)


def norm_back(d_keyval, keyval_weight, d_normed1, inputs, d_middle, gain, passed, chunk=128):
    rows, width = inputs.shape
    kv_width = d_keyval.shape[1]
    row = lambda cols: pl.BlockSpec((chunk, cols), lambda k: (k, 0))
    fixed = lambda shape: pl.BlockSpec(shape, lambda k: (0, 0))
    return pl.pallas_call(
        norm_back_kernel,
        grid=(rows // chunk,),
        out_shape=(
            jax.ShapeDtypeStruct((rows, width), F32),
            jax.ShapeDtypeStruct((8, width), F32),
            jax.ShapeDtypeStruct(passed.shape, BF16),
        ),
        in_specs=[
            row(kv_width),
            fixed((width, kv_width)),
            row(width),
            row(width),
            row(width),
            fixed((1, width)),
            row(width),
        ],
        out_specs=(row(width), fixed((8, width)), row(width)),
        scratch_shapes=[pltpu.VMEM((2, 8, width), F32), pltpu.VMEM((8, kv_width), F32)],
        compiler_params=pltpu.CompilerParams(vmem_limit_bytes=62 << 20),
        name="norm_back",
    )(d_keyval, keyval_weight, d_normed1, inputs, d_middle, gain.reshape(1, width), passed)


def finish_kernel(
    dkv_ref, vec_in, far_up, far_down, down_ref, n1_hbm, wide_ref, grad_ref, vec_ref, up_ref, down_out, n1_ref,
    n1_sem, g_send, g_recv, ends_ref, local_sem, d_send, d_recv, down_low, down_got, up_out, up_in, up_send, up_recv, own_ref, other_ref, got_ref, x_send, x_recv, own_vec, low_vec, slots, send, recv, *chain_refs,
):
    block = lax.axis_index("dp")
    lane = lax.axis_index("tensor")
    count = lax.axis_size("dp")
    side = lax.rem(block, 2)
    pairs = count // 2
    others = [(lax.rem(block + 2 * k, count), lane) for k in range(1, pairs)]
    x_peer = (block + 1 - 2 * side, lane)
    length, level, upper, lower = chain_peers()
    local = [
        pltpu.make_async_copy(
            wide_ref.at[jnp.clip(level + k, 0, length - 1)], ends_ref.at[n], local_sem.at[n]
        )
        for n, k in enumerate((0, 1, -1))
    ]
    take = pltpu.make_async_copy(n1_hbm, n1_ref, n1_sem)
    take.start()
    for copy in local:
        copy.start()
    core = lax.rem(lane, 2)
    core_peer = (block, lane + 1 - 2 * core)
    half_kv = dkv_ref.shape[1] // 2
    mine = pl.ds(pl.multiple_of(core * half_kv, half_kv), half_kv)
    greet([core_peer, x_peer] + others)
    low_vec[0] = vec_in[...].astype(BF16)
    to_pair = remote(low_vec.at[0], slots.at[0], send.at[0], recv.at[0], x_peer)
    to_pair.start()

    def last(way):
        return remote(
            up_out.at[way], up_in.at[way], up_send.at[way], up_recv.at[way], (upper, lower)[way]
        )

    ranks = (level, length - 1 - level)
    for copy in local:
        copy.wait()
    for way, far in enumerate((far_up, far_down)):
        @pl.when(ranks[way] < length - 1)
        def _(way=way, far=far):
            up_out[way] = ends_ref[1 + way]

            @pl.when(ranks[way] >= 1)
            def _():
                up_out[way] = (ends_ref[1 + way].astype(F32) + far[...].astype(F32)).astype(BF16)

            last(way).start()

    take.wait()
    kv_half = dkv_ref.at[:, mine]
    grad_rows(n1_ref, kv_half, other_ref, 1 - side)
    to_x = remote(other_ref, got_ref, x_send, x_recv, x_peer)
    to_x.start()
    half_rows, half_cols = down_low.shape
    down_mine = pl.ds(pl.multiple_of(side * half_rows, half_rows), half_rows)
    down_theirs = pl.ds(pl.multiple_of((1 - side) * half_rows, half_rows), half_rows)
    down_low[...] = down_ref[down_theirs].astype(BF16)
    d_to_x = remote(down_low, down_got, d_send, d_recv, x_peer)
    to_pair.wait()
    own_vec[...] = vec_in[...] + slots[0].astype(F32)
    low_vec[1] = own_vec[...].astype(BF16)
    copies = []
    for k in range(1, pairs):
        copy = remote(low_vec.at[1], slots.at[k], send.at[k], recv.at[k], others[k - 1])
        copy.start()
        copies.append(copy)
    grad_rows(n1_ref, kv_half, own_ref, side)
    chain = Chain(length, level, upper, lower, own_ref, chain_refs[:4], chain_refs[4:8])
    to_x.wait_recv()
    own_ref[...] = (own_ref[...].astype(F32) + got_ref[...].astype(F32)).astype(BF16)
    chain.start(1)
    d_to_x.start()
    for s in range(1, length):
        chain.arrive(s)
        if s + 1 < length:
            chain.start(s + 1)
    chain.result(grad_ref.at[:, mine])
    to_core = remote(grad_ref.at[:, mine], grad_ref.at[:, mine], g_send, g_recv, core_peer)
    to_core.start()
    d_to_x.wait()
    first = pl.ds(pl.multiple_of(side * half_cols, half_cols), half_cols)
    second = pl.ds(pl.multiple_of((1 - side) * half_cols, half_cols), half_cols)
    down_out[:, first] = down_ref[down_mine]
    down_out[:, second] = down_got[...].astype(F32)
    total = own_vec[...]
    for k in range(1, pairs):
        copies[k - 1].wait()
        total = total + slots[k].astype(F32)
    vec_ref[...] = total
    up_ref[...] = ends_ref[0].astype(F32)
    for way in range(2):
        @pl.when(ranks[way] >= 1)
        def _(way=way):
            last(way).wait_recv()
            up_ref[...] += up_in[way].astype(F32)

        @pl.when(ranks[way] < length - 1)
        def _(way=way):
            last(way).wait_send()

    chain.drain()
    to_x.wait_send()
    to_core.wait()


def finish(normed1, d_keyval, rows_of_vectors, vectors, wide, far_up, far_down, down, count):
    width = normed1.shape[1]
    flat = jnp.concatenate(vectors)
    lines = -(-flat.shape[0] // width)
    flat = jnp.pad(flat, (0, lines * width - flat.shape[0])).reshape(lines, width)
    packed = jnp.concatenate(rows_of_vectors + [flat], axis=0)
    height = -(-packed.shape[0] // 8) * 8
    packed = jnp.pad(packed, ((0, height - packed.shape[0]), (0, 0)))
    shape = (width // count, d_keyval.shape[1])
    part = (shape[0], shape[1] // 2)
    half = pltpu.VMEM((count // 2,) + part, BF16)
    dma = pltpu.SemaphoreType.DMA
    two = pltpu.VMEM((2,) + far_up.shape, BF16)
    return pl.pallas_call(
        finish_kernel,
        out_shape=(
            jax.ShapeDtypeStruct(shape, F32),
            jax.ShapeDtypeStruct((height, width), F32),
            jax.ShapeDtypeStruct(far_up.shape, F32),
            jax.ShapeDtypeStruct((down.shape[0] // 2, 2 * down.shape[1]), F32),
        ),
        in_specs=[VMEM] * 5 + [pl.BlockSpec(memory_space=pl.ANY)] * 2,
        out_specs=(VMEM,) * 4,
        scratch_shapes=[
            pltpu.VMEM(normed1.shape, BF16),
            dma,
            dma,
            dma,
            pltpu.VMEM((3,) + far_up.shape, BF16),
            dma((3,)),
            dma,
            dma,
            pltpu.VMEM((down.shape[0] // 2, down.shape[1]), BF16),
            pltpu.VMEM((down.shape[0] // 2, down.shape[1]), BF16),
        ]
        + [two, two, dma((2,)), dma((2,)), half, half, half, dma, dma]
        + [
            pltpu.VMEM((height, width), F32),
            pltpu.VMEM((2, height, width), BF16),
            pltpu.VMEM((count // 2, height, width), BF16),
            dma((count // 2,)),
            dma((count // 2,)),
        ]
        + chain_scratch(count // 2, part),
        compiler_params=pltpu.CompilerParams(
            collective_id=2, has_side_effects=True, vmem_limit_bytes=62 << 20
        ),
        name="finish",
    )(d_keyval, packed, far_up, far_down, down, normed1, wide)


def front_kernel(
    block, chunks, q_ref, own_kv, cot_hbm, wo_ref, wd_hbm, kv_ref, ctx_ref, lse_ref, sum_ref, g_ref, far_ref,
    cot_ref, wd_ref, local_sem, x_send, x_recv, z_send, z_recv, s_send, s_recv, f_send, f_recv, acc, peak, total,
    part, from_core, summed, from_y, *sems,
):
    ts = TensorSum(chunks, part, sum_ref, from_core, summed, from_y, sems)
    dp = lax.axis_index("dp")
    lane = lax.axis_index("tensor")
    place = lax.rem(dp, SPAN)
    side = lax.rem(place, 2)
    level = place // 2
    levels = SPAN // 2
    core = lax.rem(lane, 2)
    y_lane = lax.rem(lane + 2, 4)
    core_peer, y_peer = ts.core_peer, ts.y_peer
    x_peer = (dp + 1 - 2 * side, lane)
    upper = (jnp.where(level < levels - 1, dp + 2, dp + 2 - SPAN), lane)
    lower = (jnp.where(level > 0, dp - 2, dp - 2 + SPAN), lane)
    seq_rows = own_kv.shape[0]
    piece = seq_rows // 4
    head = kv_ref.shape[2] // 2
    heads = q_ref.shape[1] // head
    parts = seq_rows // block

    def rows_of(which):
        return pl.ds(pl.multiple_of(which * piece, piece), piece)

    local = [
        pltpu.make_async_copy(own_kv, kv_ref.at[place], local_sem.at[0]),
        pltpu.make_async_copy(cot_hbm, cot_ref, local_sem.at[1]),
        pltpu.make_async_copy(wd_hbm, wd_ref, local_sem.at[2]),
    ]
    local[0].start()
    greet([core_peer, y_peer, x_peer, upper, lower])
    to_x = remote(own_kv.at[rows_of(lane)], kv_ref.at[place, rows_of(lane)], x_send, x_recv, x_peer)
    to_x.start()
    far_pieces = f_send.shape[1]
    far_step = cot_hbm.shape[0] // (2 * far_pieces)

    def far(kind, k):
        start = pl.multiple_of((core * far_pieces + k) * far_step, far_step)
        source = cot_hbm if kind == 0 else far_ref
        return remote(
            source.at[pl.ds(start, far_step)], far_ref.at[pl.ds(start, far_step)], f_send.at[kind, k],
            f_recv.at[kind, k], x_peer if kind == 0 else core_peer,
        )

    def share(s, kind):
        at = rows_of(y_lane if kind == 2 else lane)
        ref = kv_ref.at[pl.ds(2 * (level - s), 2), at]
        return remote(
            ref, ref, s_send.at[s, kind], s_recv.at[s, kind], y_peer if kind == 0 else core_peer
        )

    def share_pair(kind):
        ref = kv_ref.at[place + 1 - 2 * side, rows_of(y_lane if kind == 2 else lane)]
        return remote(
            ref, ref, s_send.at[0, kind], s_recv.at[0, kind], y_peer if kind == 0 else core_peer
        )

    def up(s):
        ref = kv_ref.at[pl.ds(2 * (level - s), 2), rows_of(lane)]
        return remote(ref, ref, z_send.at[s], z_recv.at[s], upper)

    def from_below(s):
        ref = kv_ref.at[pl.ds(2 * (level - 1 - s), 2), rows_of(lane)]
        return remote(ref, ref, z_send.at[s], z_recv.at[s], upper)

    def forward(s):
        from_below(s - 1).wait_recv()

        @pl.when((s < levels - 1) & (level < levels - 1))
        def _():
            up(s).start()

        share(s, 0).start()
        share(s, 1).start()

    def score(i, h, at_block, at_row, diagonal):
        keys = kv_ref[at_block, pl.ds(at_row, block), 0:head]
        query = q_ref[i * block : (i + 1) * block, h * head : (h + 1) * head]
        scores = contract(keys, query, 1, 1)
        if diagonal:
            key_at = lax.broadcasted_iota(jnp.int32, scores.shape, 0)
            query_at = lax.broadcasted_iota(jnp.int32, scores.shape, 1)
            scores = jnp.where(key_at <= query_at, scores, NEG_LARGE)
        return scores

    def soften(i, h, scores):
        old = peak[i, h]
        new = jnp.maximum(old, jnp.max(scores, axis=0, keepdims=True))
        probs = jnp.exp(scores - new)
        fade = jnp.exp(old - new)
        total[i, h] = total[i, h] * fade + jnp.sum(probs, axis=0, keepdims=True)
        peak[i, h] = new
        return probs.astype(BF16), fade

    def weigh(i, h, at_block, at_row, probs, fade):
        values = kv_ref[at_block, pl.ds(at_row, block), head : 2 * head]
        acc[i, h] = acc[i, h] * fade + contract(values, probs, 0, 0)

    def attend(i, pieces):
        items = [(h, piece) for piece in pieces for h in range(heads)]
        scores = score(i, items[0][0], *items[0][1])
        waiting = None
        for n, (h, (at_block, at_row, _diagonal)) in enumerate(items):
            following = None
            if n + 1 < len(items):
                following = score(i, items[n + 1][0], *items[n + 1][1])
            probs, fade = soften(i, h, scores)
            if waiting is not None:
                weigh(i, *waiting)
            waiting = (h, at_block, at_row, probs, fade)
            scores = following
        weigh(i, *waiting)

    def attend_level(i, s):
        @pl.loop(0, 2)
        def _(b):
            attend(i, [(2 * (level - s) + b, n * block, False) for n in range(parts)])

    peak[...] = jnp.full_like(peak, NEG_LARGE)
    total[...] = jnp.zeros_like(total)
    acc[...] = jnp.zeros_like(acc)
    local[0].wait()
    for copy in local[1:]:
        copy.start()
    for k in range(far_pieces):
        far(0, k).start()
    to_x.wait_recv()

    @pl.when(level < levels - 1)
    def _():
        up(0).start()

    share_pair(0).start()
    share_pair(1).start()
    for i in range(parts):
        attend(i, [(place, n * block, n == i) for n in range(i + 1)])

    @pl.when(level >= 1)
    def _():
        forward(1)

    share_pair(0).wait_recv()
    share_pair(2).start()
    share_pair(1).wait_recv()
    share_pair(2).wait_recv()

    @pl.when(side == 1)
    def _():
        for i in range(parts):
            attend(i, [(place - 1, n * block, False) for n in range(parts)])

    def complete(i):
        span = slice(i * block, (i + 1) * block)
        for h in range(heads):
            context = acc[i, h] / total[i, h]
            ctx_ref[span, h * head : (h + 1) * head] = context.T.astype(BF16)
            lse_ref[h : h + 1, span] = peak[i, h] + jnp.log(total[i, h])
        each = chunks // parts
        first = i * each

        @pl.loop(first, first + each)
        def _(k):
            at = ts.span(k)
            part[at, :] = jnp.dot(
                ctx_ref[at, :], wo_ref[...], preferred_element_type=F32
            ).astype(BF16)
            ts.first(k)

        @pl.loop(first, first + each)
        def _(k):
            ts.second(k)

    @pl.loop(1, level + 1)
    def _(s):
        @pl.when(s < level)
        def _():
            forward(s + 1)

        share(s, 0).wait_recv()
        share(s, 2).start()
        share(s, 1).wait_recv()
        share(s, 2).wait_recv()
        attend_level(0, s)

    complete(0)
    for i in range(1, parts):
        @pl.loop(1, level + 1)
        def _(s, i=i):
            attend_level(i, s)

        complete(i)

    for k in range(far_pieces):
        far(0, k).wait_recv()
        far(1, k).start()
    ready = chunks - chunks // parts

    @pl.loop(0, ready)
    def _(k):
        ts.third(k)

    for copy in local[1:]:
        copy.wait()
    tile = g_ref.shape[1] // 8

    @pl.loop(0, 8)
    def _(j):
        cols = pl.ds(pl.multiple_of(j * tile, tile), tile)
        g_ref[:, cols] = contract(cot_ref[...], wd_ref[cols, :], 1, 1).astype(BF16)

    @pl.loop(ready, chunks)
    def _(k):
        ts.third(k)

    to_x.wait_send()

    @pl.when(level < levels - 1)
    def _():
        up(0).wait_send()

    for kind in range(3):
        share_pair(kind).wait_send()

    @pl.loop(1, level + 1)
    def _(s):
        for kind in range(3):
            share(s, kind).wait_send()

        @pl.when((s < levels - 1) & (level < levels - 1))
        def _():
            up(s).wait_send()

    for k in range(far_pieces):
        far(0, k).wait_send()
        far(1, k).wait()
    ts.finish(chunks)


def front(queries, keyval, cotangent, output_weight, down_weight, block=512, chunks=8):
    rows, width = queries.shape
    wide = output_weight.shape[1]
    hidden = down_weight.shape[0]
    head = keyval.shape[1] // 2
    heads = width // head
    levels = SPAN // 2
    dma = pltpu.SemaphoreType.DMA
    hbm = pl.BlockSpec(memory_space=pl.ANY)
    stat = pltpu.VMEM((rows // block, heads, 1, block), F32)
    return pl.pallas_call(
        functools.partial(front_kernel, block, chunks),
        out_shape=(
            jax.ShapeDtypeStruct((SPAN,) + keyval.shape, BF16),
            jax.ShapeDtypeStruct((rows, width), BF16),
            jax.ShapeDtypeStruct((heads, rows), F32),
            jax.ShapeDtypeStruct((rows, wide), BF16),
            jax.ShapeDtypeStruct((rows, hidden), BF16),
            jax.ShapeDtypeStruct(cotangent.shape, BF16),
        ),
        in_specs=[VMEM, VMEM, hbm, VMEM, hbm],
        out_specs=(VMEM,) * 5 + (hbm,),
        scratch_shapes=[
            pltpu.VMEM(cotangent.shape, BF16),
            pltpu.VMEM(down_weight.shape, BF16),
            dma((3,)),
            dma,
            dma,
            dma((levels - 1,)),
            dma((levels - 1,)),
            dma((levels, 3)),
            dma((levels, 3)),
            dma((2, 4)),
            dma((2, 4)),
            pltpu.VMEM((rows // block, heads, head, block), F32),
            stat,
            stat,
        ]
        + sum_scratch(chunks, rows, wide),
        compiler_params=pltpu.CompilerParams(
            collective_id=1, has_side_effects=True, vmem_limit_bytes=60 << 20
        ),
        name="front",
    )(queries, keyval, cotangent, output_weight, down_weight)


def attend_back_kernel(
    block, chunks, q_ref, do_ref, ctx_ref, lse_ref, far_up, far_down, kv_hbm, pair_hbm, mlp_hbm, sent_ref,
    edge_ref, proj_ref, dq_ref, grad_ref, dkv_out, sum_out, got_ref, wide_up, wide_down, proj_got, kv_ref, pair_ref,
    mlp_ref, dkv_ref, out_ref, in_sem, dkv_sem, sum_sem, dq_acc, dkv_acc, delta, x_send, x_recv, z_send, z_recv,
    from_core, summed, from_y, *rest,
):
    sems, chain_refs = rest[:6], rest[6:]
    rows = q_ref.shape[0]
    head = kv_ref.shape[1] // 2
    heads = q_ref.shape[1] // head
    place = lax.rem(lax.axis_index("dp"), SPAN)
    side = lax.rem(lax.axis_index("dp"), 2)
    x_peer = (lax.axis_index("dp") + 1 - 2 * side, lax.axis_index("tensor"))
    ts = TensorSum(chunks, mlp_ref, out_ref, from_core, summed, from_y, sems)
    length, level, upper, lower = chain_peers()
    early = (far_up, far_down)
    chain = Chain(length, level, upper, lower, pair_ref, chain_refs[:4], chain_refs[4:], early)
    depth = 2 * rows
    local = [
        pltpu.make_async_copy(mlp_hbm, mlp_ref, in_sem.at[0]),
        pltpu.make_async_copy(pair_hbm, pair_ref, in_sem.at[1]),
    ] + [
        pltpu.make_async_copy(
            kv_hbm.at[pl.ds(n * depth, depth)], kv_ref.at[pl.ds(n * depth, depth)], in_sem.at[2 + n]
        )
        for n in range(SPAN // 2)
    ]
    dkv_copies = [
        pltpu.make_async_copy(
            dkv_ref.at[pl.ds(2 * n, 2)], dkv_out.at[pl.ds(2 * n, 2)], dkv_sem.at[n]
        )
        for n in range(SPAN // 2)
    ]
    sum_copy = pltpu.make_async_copy(out_ref, sum_out, sum_sem)
    for copy in local:
        copy.start()
    greet([ts.core_peer, ts.y_peer, x_peer, upper, lower])
    left = pl.ds(jnp.where(level < length // 2, 0, 1), length - 1)
    proj_to_x = remote(proj_ref, proj_got, x_send.at[1], x_recv.at[1], x_peer)
    proj_to_x.start()
    to_x = remote(sent_ref.at[left], got_ref.at[left], x_send.at[0], x_recv.at[0], x_peer)
    to_x.start()

    local[0].wait()

    @pl.loop(0, chunks)
    def _(k):
        ts.first(k)

    local[1].wait()
    chain.start(2)
    wide_step = FirstStep(
        length, level, upper, lower, (edge_ref, edge_ref), (wide_up, wide_down), z_send, z_recv
    )
    wide_step.start()
    levels = SPAN // 2
    parts = 2 * rows // block
    per_slot = -(-(length - 2) // (levels - 1))
    done = 1
    for target in range(levels):
        local[2 + target].wait()
        dkv_acc[...] = jnp.zeros_like(dkv_acc)
        for i in range(rows // block):
            span = slice(i * block, (i + 1) * block)
            if target == 0:
                for h in range(heads):
                    cols = slice(h * head, (h + 1) * head)
                    product = do_ref[span, cols].astype(F32) * ctx_ref[span, cols].astype(F32)
                    delta[h : h + 1, span] = jnp.sum(product.T, axis=0, keepdims=True)
                dq_acc[i] = jnp.zeros_like(dq_acc[i])

            def step(j, diagonal, span=span, i=i):
                at = pl.ds(pl.multiple_of(j * block, block), block)
                kv_at = pl.ds(pl.multiple_of((target * parts + j) * block, block), block)
                keys = kv_ref[kv_at, 0:head]
                values = kv_ref[kv_at, head : 2 * head]
                d_keys = jnp.zeros((block, head), F32)
                d_values = jnp.zeros((block, head), F32)

                def begin(h):
                    cols = slice(h * head, (h + 1) * head)
                    scores = contract(keys, q_ref[span, cols], 1, 1)
                    if diagonal:
                        key_at = lax.broadcasted_iota(jnp.int32, scores.shape, 0)
                        query_at = lax.broadcasted_iota(jnp.int32, scores.shape, 1)
                        scores = jnp.where(key_at <= query_at, scores, NEG_LARGE)
                    return scores, contract(values, do_ref[span, cols], 1, 1)

                begun = begin(0)
                for h in range(heads):
                    cols = slice(h * head, (h + 1) * head)
                    scores, d_probs = begun
                    if h + 1 < heads:
                        begun = begin(h + 1)
                    probs = jnp.exp(scores - lse_ref[h : h + 1, span])
                    d_scores = (probs * (d_probs - delta[h : h + 1, span])).astype(BF16)
                    d_values += contract(probs.astype(BF16), do_ref[span, cols], 1, 0)
                    d_keys += contract(d_scores, q_ref[span, cols], 1, 0)
                    dq_acc[i, h] += contract(keys, d_scores, 0, 0)
                dkv_acc[at, 0:head] += d_keys
                dkv_acc[at, head : 2 * head] += d_values

            full = (place * rows + i * block) // block - target * parts

            @pl.loop(0, jnp.clip(full, 0, parts))
            def _(j):
                step(j, False)

            @pl.when((full >= 0) & (full < parts))
            def _():
                step(full, True)

            if target == 0 and i == 0:
                @pl.loop(0, chunks)
                def _(k):
                    ts.second(k)

        for b in range(2):
            dkv_ref[2 * target + b] = dkv_acc[b * rows : (b + 1) * rows].astype(BF16)
        dkv_copies[target].start()
        if target < levels - 1:
            for _ in range(per_slot):
                if done < length - 1:
                    done += 1
                    chain.arrive(done)
                    if done < length - 1:
                        chain.start(done + 1)
                    else:
                        chain.result(grad_ref)
        if target == levels - 2:
            @pl.loop(0, chunks)
            def _(k):
                ts.third(k)

            ts.finish(chunks)
            sum_copy.start()

    for i in range(rows // block):
        span = slice(i * block, (i + 1) * block)
        for h in range(heads):
            dq_ref[span, h * head : (h + 1) * head] = (
                (dq_acc[i, h] * head**-0.5).T.astype(BF16)
            )
    chain.drain()
    wide_step.wait()
    for copy in dkv_copies + [sum_copy]:
        copy.wait()
    to_x.wait()
    proj_to_x.wait()


def attend_back(
    queries, keyval, d_context, context, lse, pair, far_up, far_down, mlp_part, sent, edge, proj, block=512, chunks=4
):
    rows, width = queries.shape
    head = keyval.shape[1] // 2
    heads = width // head
    hbm = pl.BlockSpec(memory_space=pl.ANY)
    dma = pltpu.SemaphoreType.DMA
    low = lambda shape: jax.ShapeDtypeStruct(shape, BF16)
    return pl.pallas_call(
        functools.partial(attend_back_kernel, block, chunks),
        out_shape=(
            low((rows, width)),
            jax.ShapeDtypeStruct(pair.shape[1:], F32),
            low((SPAN, rows, 2 * head)),
            low(mlp_part.shape),
            low(sent.shape),
            low(edge.shape),
            low(edge.shape),
            low(proj.shape),
        ),
        in_specs=[VMEM] * 6 + [hbm] * 6,
        out_specs=(VMEM,) * 2 + (hbm,) * 6,
        scratch_shapes=[
            pltpu.VMEM(keyval.shape, BF16),
            pltpu.VMEM(pair.shape, BF16),
            pltpu.VMEM(mlp_part.shape, BF16),
            pltpu.VMEM((SPAN, rows, 2 * head), BF16),
            pltpu.VMEM(mlp_part.shape, BF16),
            dma((2 + SPAN // 2,)),
            dma((SPAN // 2,)),
            dma,
            pltpu.VMEM((rows // block, heads, head, block), F32),
            pltpu.VMEM((2 * rows, 2 * head), F32),
            pltpu.VMEM((heads, rows), F32),
            dma((2,)),
            dma((2,)),
            dma((2,)),
            dma((2,)),
        ]
        + sum_scratch(chunks, *mlp_part.shape)[1:]
        + chain_scratch(pair.shape[0] - 1, pair.shape[1:]),
        compiler_params=pltpu.CompilerParams(
            collective_id=6, has_side_effects=True, vmem_limit_bytes=63 << 20
        ),
        name="attend_back",
    )(
        queries, d_context, context, lse, far_up, far_down, keyval, pair, mlp_part, sent, edge, proj
    )


def layer_norm(values, norm_gain, norm_bias):
    average = jnp.mean(values, axis=-1, keepdims=True)
    centred = values - average
    variance = jnp.mean(centred * centred, axis=-1, keepdims=True)
    return centred * lax.rsqrt(variance + EPSILON) * norm_gain + norm_bias


def per_device(
    inputs,
    first_gain,
    first_bias,
    query_weight,
    query_bias,
    keyval_weight,
    value_bias,
    output_weight,
    output_bias,
    second_gain,
    second_bias,
    up_weight,
    up_bias,
    down_weight,
    down_bias,
    cotangent,
):
    count = lax.axis_size("dp")
    head_size = value_bias.shape[0]
    score_scale = head_size ** (-0.5)
    x_full = inputs.astype(F32)
    normed1 = layer_norm(x_full, first_gain, first_bias).astype(BF16)
    query_pre = jnp.dot(normed1, query_weight, preferred_element_type=F32) + query_bias
    queries = (query_pre * score_scale).astype(BF16)
    kv_bias = jnp.concatenate([jnp.zeros_like(value_bias), value_bias])
    keyval = (jnp.dot(normed1, keyval_weight, preferred_element_type=F32) + kv_bias).astype(BF16)
    keyval_all, context_low, lse, attn_sum, d_activ, far_cotangent = front(
        queries, keyval, cotangent, output_weight, down_weight
    )
    keyval_all = keyval_all.reshape(-1, keyval.shape[1])
    normed2, activ, d_pre, d_up_bias = hidden_stage(
        inputs, attn_sum, d_activ, up_weight, up_bias, output_bias, second_gain, second_bias
    )
    d_up_bias = d_up_bias[0]
    d_normed2, up_own, up_other, pair_down, out_part = hidden_back(
        d_pre, up_weight, normed2, activ, cotangent, far_cotangent, down_weight, count
    )
    d_middle, d_context, out_part, proj_own, proj_other, row_sums, edge, far_up, far_down = middle_stage(
        d_normed2,
        inputs,
        attn_sum,
        cotangent,
        output_bias,
        second_gain,
        down_bias,
        out_part,
        output_weight,
        context_low,
        pair_down,
        up_own,
        up_other,
        count,
    )
    d_queries, half_down, d_kv_parts, layer_out, rest, wide_up, wide_down, proj_got = attend_back(
        queries,
        keyval_all,
        d_context,
        context_low,
        lse,
        pair_down,
        far_up,
        far_down,
        out_part,
        up_other,
        edge,
        proj_other,
    )
    length = count // 2
    at_edge = jnp.where(lax.axis_index("dp") // 2 < length // 2, length - 1, 0)
    pair_up = (up_own.astype(F32) + rest.astype(F32)).astype(BF16)
    pair_up = lax.dynamic_update_index_in_dim(pair_up, edge, at_edge, 0)
    d_query_bias = jnp.sum(d_queries.astype(F32), axis=0)
    d_normed1, sent_query, sent_proj, d_keyval, far_up, far_down = query_back(
        d_queries,
        query_weight,
        normed1,
        d_kv_parts,
        pair_up,
        wide_up,
        wide_down,
        proj_own,
        proj_got,
        count,
    )
    grad_inputs, first_sums, layer_out = norm_back(
        d_keyval, keyval_weight, d_normed1, inputs, d_middle, first_gain, layer_out
    )
    sent_kv, sums, sent_up, sent_down = finish(
        normed1,
        d_keyval,
        [first_sums[:3], row_sums[:4]],
        [d_up_bias, d_query_bias],
        pair_up,
        far_up,
        far_down,
        half_down,
        count,
    )
    local = query_weight.shape[1]
    hidden = d_up_bias.shape[0]
    flat = sums[7:].reshape(-1)
    return (
        layer_out,
        grad_inputs,
        sums[0],
        sums[1],
        sent_query,
        flat[hidden : hidden + local],
        sent_kv,
        sums[2, head_size : 2 * head_size],
        sent_proj.T,
        sums[5],
        sums[3],
        sums[4],
        sent_up,
        flat[:hidden],
        sent_down.T,
        sums[6],
    )


def solution(mesh):
    in_specs = (
        P("dp", None),
        P(),
        P(),
        P(None, "tensor"),
        P("tensor"),
        P(),
        P(),
        P("tensor", None),
        P(),
        P(),
        P(),
        P(None, "tensor"),
        P("tensor"),
        P("tensor", None),
        P(),
        P("dp", None),
    )
    out_specs = (
        P("dp", None),
        P("dp", None),
        P(),
        P(),
        P("dp", "tensor"),
        P("tensor"),
        P("dp", None),
        P(),
        P("tensor", "dp"),
        P(),
        P(),
        P(),
        P("dp", "tensor"),
        P("tensor"),
        P("tensor", "dp"),
        P(),
    )
    return jax.shard_map(
        per_device, mesh=mesh, in_specs=in_specs, out_specs=out_specs, check_vma=False
    )
```

```python
import functools

import jax
import jax.numpy as jnp
from jax import lax
from jax.experimental import pallas as pl
from jax.experimental.pallas import tpu as pltpu
from jax.sharding import PartitionSpec as P

SPAN = 8
EPSILON = 1e-05
NEG_LARGE = -1e30
MESH = pl.DeviceIdType.MESH
VMEM = pl.BlockSpec(memory_space=pltpu.VMEM)
F32 = jnp.float32
BF16 = jnp.bfloat16


def contract(left, right, left_dim, right_dim):
    return lax.dot_general(
        left, right, (((left_dim,), (right_dim,)), ((), ())), preferred_element_type=F32
    )


def remote(source, target, send_sem, recv_sem, device):
    return pltpu.make_async_remote_copy(
        src_ref=source,
        dst_ref=target,
        send_sem=send_sem,
        recv_sem=recv_sem,
        device_id=device,
        device_id_type=MESH,
    )


def greet(devices):
    barrier = pltpu.get_barrier_semaphore()
    for device in devices:
        pl.semaphore_signal(barrier, inc=1, device_id=device, device_id_type=MESH)
    pl.semaphore_wait(barrier, len(devices))


class TensorSum:
    def __init__(self, chunks, part, result, from_core, summed, from_y, sems):
        block = lax.axis_index("dp")
        lane = lax.axis_index("tensor")
        core = lax.rem(lane, 2)
        self.core_peer = (block, lane + 1 - 2 * core)
        self.y_peer = (block, lax.rem(lane + 2, 4))
        rows, width = part.shape
        half = width // 2
        self.step = rows // chunks
        self.mine = pl.ds(pl.multiple_of(core * half, half), half)
        self.other = pl.ds(pl.multiple_of((1 - core) * half, half), half)
        self.part, self.result = part, result
        self.from_core, self.summed, self.from_y = from_core, summed, from_y
        self.sems = sems

    def span(self, k):
        return pl.ds(pl.multiple_of(k * self.step, self.step), self.step)

    def to_core(self, k):
        at = self.span(k)
        return remote(
            self.part.at[at, self.other], self.from_core.at[at], self.sems[0].at[k],
            self.sems[1].at[k], self.core_peer,
        )

    def to_y(self, k):
        at = self.span(k)
        return remote(
            self.summed.at[at], self.from_y.at[at], self.sems[2].at[k], self.sems[3].at[k],
            self.y_peer,
        )

    def back(self, k):
        at = self.span(k)
        return remote(
            self.result.at[at, self.mine], self.result.at[at, self.mine], self.sems[4].at[k],
            self.sems[5].at[k], self.core_peer,
        )

    def first(self, k):
        self.to_core(k).start()

    def second(self, k):
        at = self.span(k)
        self.to_core(k).wait_recv()
        total = self.part[at, self.mine].astype(F32) + self.from_core[at].astype(F32)
        self.summed[at] = total.astype(BF16)
        self.to_y(k).start()

    def third(self, k):
        at = self.span(k)
        self.to_y(k).wait_recv()
        total = self.summed[at].astype(F32) + self.from_y[at].astype(F32)
        self.result[at, self.mine] = total.astype(BF16)
        self.back(k).start()

    def finish(self, chunks):
        @pl.loop(0, chunks)
        def _(k):
            self.back(k).wait_recv()
            self.back(k).wait_send()
            self.to_core(k).wait_send()
            self.to_y(k).wait_send()


def sum_scratch(chunks, rows, width):
    half = pltpu.VMEM((rows, width // 2), BF16)
    return [pltpu.VMEM((rows, width), BF16), half, half, half] + [
        pltpu.SemaphoreType.DMA((chunks,))
    ] * 6


def grad_rows(left_ref, right, target, which):
    levels, rows = target.shape[0], target.shape[1]

    @pl.loop(0, levels)
    def _(lev):
        if rows % 128 == 0:
            cols = pl.ds(pl.multiple_of((2 * lev + which) * rows, rows), rows)
            target[lev] = contract(left_ref[:, cols], right[...], 0, 0).astype(BF16)
        else:
            cols = pl.ds(pl.multiple_of(2 * lev * rows, 2 * rows), 2 * rows)
            both = contract(left_ref[:, cols], right[...], 0, 0)
            target[lev] = jnp.where(which == 0, both[:rows], both[rows:]).astype(BF16)


def hidden_kernel(tiles, x_ref, attn_ref, g_ref, wu_ref, bias_ref, vec_ref, n2_ref, act_ref, dpre_ref, sums_ref, acc):
    step = pl.program_id(0)

    @pl.when(step == 0)
    def _():
        acc[...] = jnp.zeros_like(acc)

    rows = x_ref.shape[0]
    values = x_ref[...].astype(F32) + attn_ref[...].astype(F32) + vec_ref[0:1, :]
    centred = values - jnp.mean(values, axis=-1, keepdims=True)
    scale = lax.rsqrt(jnp.mean(centred * centred, axis=-1, keepdims=True) + EPSILON)
    n2_ref[...] = (centred * scale * vec_ref[1:2, :] + vec_ref[2:3, :]).astype(BF16)
    tile = wu_ref.shape[1] // tiles
    root = 0.7978845608028654
    for j in range(tiles):
        cols = slice(j * tile, (j + 1) * tile)
        pre = jnp.dot(n2_ref[...], wu_ref[:, cols], preferred_element_type=F32) + bias_ref[0:1, cols]
        square = pre * pre
        bend = jnp.tanh(root * pre * (1.0 + 0.044715 * square))
        half = 0.5 * (1.0 + bend)
        act_ref[:, cols] = (pre * half).astype(BF16)
        slope = half + (0.5 * root) * pre * (1.0 - bend * bend) * (1.0 + (3 * 0.044715) * square)
        d_pre = (g_ref[:, cols].astype(F32) * slope).astype(BF16)
        dpre_ref[:, cols] = d_pre
        acc[:, cols] += jnp.sum(d_pre.astype(F32).reshape(rows // 8, 8, tile), axis=0)

    @pl.when(step == pl.num_programs(0) - 1)
    def _():
        sums_ref[...] = jnp.sum(acc[...], axis=0, keepdims=True)


def hidden_stage(inputs, attn_sum, d_activ, up_weight, up_bias, output_bias, gain, bias, block=256, tiles=4):
    rows, width = inputs.shape
    wide = up_weight.shape[1]
    vec = jnp.pad(jnp.stack([output_bias, gain, bias]), ((0, 5), (0, 0)))
    row = lambda cols: pl.BlockSpec((block, cols), lambda k: (k, 0))
    fixed = lambda shape: pl.BlockSpec(shape, lambda k: (0, 0))
    return pl.pallas_call(
        functools.partial(hidden_kernel, tiles),
        grid=(rows // block,),
        out_shape=(
            jax.ShapeDtypeStruct((rows, width), BF16),
            jax.ShapeDtypeStruct((rows, wide), BF16),
            jax.ShapeDtypeStruct((rows, wide), BF16),
            jax.ShapeDtypeStruct((1, wide), F32),
        ),
        in_specs=[
            row(width),
            row(width),
            row(wide),
            pl.BlockSpec(up_weight.shape, lambda k: (0, 0), pipeline_mode=pl.Buffered(1)),
            fixed((1, wide)),
            fixed((8, width)),
        ],
        out_specs=(row(width), row(wide), row(wide), fixed((1, wide))),
        scratch_shapes=[pltpu.VMEM((8, wide), F32)],
        compiler_params=pltpu.CompilerParams(vmem_limit_bytes=60 << 20),
        name="hidden",
    )(inputs, attn_sum, d_activ, up_weight, up_bias.reshape(1, wide), vec)


def hidden_back_kernel(
    chunks, dpre_ref, wu_hbm, n2_hbm, activ_hbm, cot_hbm, far_hbm, wd_hbm, dn_ref, own_out, other_out, down_out,
    mlp_out, weight_ref, n2_ref, activ_ref, cot_ref, far_ref, own_ref, other_ref, down_ref, mlp_ref, in_sem, out_sem,
    mlp_sem, activ_x, x_send, x_recv, part,
    from_core, summed, from_y, *sems,
):
    ts = TensorSum(chunks, part, dn_ref, from_core, summed, from_y, sems)
    side = lax.rem(lax.axis_index("dp"), 2)
    x_peer = (lax.axis_index("dp") + 1 - 2 * side, lax.axis_index("tensor"))
    half = activ_x.shape[1]
    mine = pl.ds(pl.multiple_of(side * half, half), half)
    theirs = pl.ds(pl.multiple_of((1 - side) * half, half), half)
    local = [
        pltpu.make_async_copy(source, target, in_sem.at[n])
        for n, (source, target) in enumerate(
            [
                (wu_hbm, weight_ref),
                (n2_hbm, n2_ref),
                (activ_hbm, activ_ref),
                (cot_hbm, cot_ref),
                (far_hbm, far_ref),
                (wd_hbm, weight_ref),
            ]
        )
    ]
    results = [
        pltpu.make_async_copy(source, target, out_sem.at[n])
        for n, (source, target) in enumerate(
            [(other_ref, other_out), (own_ref, own_out), (down_ref, down_out)]
        )
    ]
    local[0].start()
    greet([ts.core_peer, ts.y_peer, x_peer])
    to_x = remote(activ_hbm.at[:, theirs], activ_x, x_send, x_recv, x_peer)
    to_x.start()
    for copy in local[1:5]:
        copy.start()
    local[0].wait()

    @pl.loop(0, chunks)
    def _(k):
        at = ts.span(k)
        part[at, :] = contract(dpre_ref[at, :], weight_ref[...], 1, 1).astype(BF16)
        ts.first(k)

        @pl.when(k >= 1)
        def _():
            ts.second(k - 1)

    ts.second(chunks - 1)
    local[5].start()
    local[1].wait()
    grad_rows(n2_ref, dpre_ref, other_ref, 1 - side)
    results[0].start()
    grad_rows(n2_ref, dpre_ref, own_ref, side)
    results[1].start()
    levels, rows = down_ref.shape[0], down_ref.shape[1]
    local[2].wait()
    local[3].wait()

    @pl.loop(0, levels)
    def _(lev):
        cols = pl.ds(pl.multiple_of(lev * rows, rows), rows)
        down_ref[lev] = contract(cot_ref[:, cols], activ_ref[:, mine], 0, 0).astype(BF16)

    ready = chunks // 2

    @pl.loop(0, ready)
    def _(k):
        ts.third(k)

    local[5].wait()
    tiles = 4
    tile = mlp_ref.shape[2]

    def mlp_copy(j):
        cols = pl.ds(pl.multiple_of(j * tile, tile), tile)
        slot = lax.rem(j, 2)
        return pltpu.make_async_copy(mlp_ref.at[slot], mlp_out.at[:, cols], mlp_sem.at[slot])

    @pl.loop(0, tiles)
    def _(j):
        @pl.when(j >= 2)
        def _():
            mlp_copy(j - 2).wait()

        cols = pl.ds(pl.multiple_of(j * tile, tile), tile)
        mlp_ref[lax.rem(j, 2)] = jnp.dot(
            activ_ref[...], weight_ref[:, cols], preferred_element_type=F32
        ).astype(BF16)
        mlp_copy(j).start()

    local[4].wait()
    to_x.wait_recv()

    @pl.loop(0, levels)
    def _(lev):
        cols = pl.ds(pl.multiple_of(lev * rows, rows), rows)
        far = contract(far_ref[:, cols], activ_x[...], 0, 0)
        down_ref[lev] = (down_ref[lev].astype(F32) + far).astype(BF16)

    results[2].start()

    @pl.loop(ready, chunks)
    def _(k):
        ts.third(k)

    ts.finish(chunks)
    to_x.wait_send()
    for copy in results:
        copy.wait()
    for j in (tiles - 2, tiles - 1):
        mlp_copy(j).wait()


def hidden_back(
    d_pre, up_weight, normed2, activ, cotangent, far_cotangent, down_weight, count, chunks=4
):
    rows, width = d_pre.shape[0], up_weight.shape[0]
    hidden = up_weight.shape[1]
    levels = count // 2
    half = (levels, width // count, hidden)
    down = (levels, width // levels, hidden // 2)
    dma = pltpu.SemaphoreType.DMA
    hbm = pl.BlockSpec(memory_space=pl.ANY)
    return pl.pallas_call(
        functools.partial(hidden_back_kernel, chunks),
        out_shape=(
            jax.ShapeDtypeStruct((rows, width), BF16),
            jax.ShapeDtypeStruct(half, BF16),
            jax.ShapeDtypeStruct(half, BF16),
            jax.ShapeDtypeStruct(down, BF16),
            jax.ShapeDtypeStruct((rows, width), BF16),
        ),
        in_specs=[VMEM] + [hbm] * 6,
        out_specs=(VMEM,) + (hbm,) * 4,
        scratch_shapes=[
            pltpu.VMEM(up_weight.shape, BF16),
            pltpu.VMEM((rows, width), BF16),
            pltpu.VMEM((rows, hidden), BF16),
            pltpu.VMEM((rows, width), BF16),
            pltpu.VMEM((rows, width), BF16),
            pltpu.VMEM(half, BF16),
            pltpu.VMEM(half, BF16),
            pltpu.VMEM(down, BF16),
            pltpu.VMEM((2, rows, width // 4), BF16),
            dma((6,)),
            dma((3,)),
            dma((2,)),
            pltpu.VMEM((rows, hidden // 2), BF16),
            dma,
            dma,
        ]
        + sum_scratch(chunks, rows, width),
        compiler_params=pltpu.CompilerParams(
            collective_id=4, has_side_effects=True, vmem_limit_bytes=62 << 20
        ),
        name="hidden_back",
    )(d_pre, up_weight, normed2, activ, cotangent, far_cotangent, down_weight)


class Chain:
    def __init__(self, length, level, upper, lower, pair, bufs, sems, early=None):
        self.length, self.level = length, level
        self.peers = (upper, lower)
        self.pair = pair
        self.bufs = bufs
        self.sems = sems
        self.early = early
        self.skip = 0 if early is None else 1

    def copy(self, way, s):
        at = s - 1 - self.skip
        inward, outward = self.bufs[2 * way], self.bufs[2 * way + 1]
        send, recv = self.sems[2 * way], self.sems[2 * way + 1]
        return remote(outward.at[at], inward.at[at], send.at[at], recv.at[at], self.peers[way])

    def arrived(self, way, s):
        if s == 1 and self.early is not None:
            return self.early[way][...]
        return self.bufs[2 * way][s - 1 - self.skip]

    def rank(self, way):
        return self.level if way == 0 else self.length - 1 - self.level

    def start(self, s):
        for way in range(2):
            rank = self.rank(way)
            slot = rank + self.length - s
            slot = jnp.clip(slot if way == 0 else self.length - 1 - slot, 0, self.length - 1)
            outward = self.bufs[2 * way + 1]
            at = s - 1 - self.skip

            @pl.when(rank <= s - 1)
            def _(way=way, rank=rank, slot=slot, outward=outward, at=at):
                outward[at] = self.pair[slot]
                if s > 1:
                    @pl.when(rank >= 1)
                    def _():
                        outward[at] = (
                            self.pair[slot].astype(F32) + self.arrived(way, s - 1).astype(F32)
                        ).astype(BF16)

                self.copy(way, s).start()

    def arrive(self, s):
        for way in range(2):
            rank = self.rank(way)

            @pl.when((rank >= 1) & (rank <= s))
            def _(way=way):
                self.copy(way, s).wait_recv()

    def result(self, target):
        target[...] = self.pair[self.level].astype(F32)
        for way in range(2):
            @pl.when(self.rank(way) >= 1)
            def _(way=way):
                target[...] += self.arrived(way, self.length - 1).astype(F32)

    def drain(self, last=None):
        for s in range(1 + self.skip, (last or self.length - 1) + 1):
            for way in range(2):
                rank = self.rank(way)

                @pl.when(rank <= s - 1)
                def _(way=way, s=s):
                    self.copy(way, s).wait_send()


class FirstStep:
    def __init__(self, length, level, upper, lower, sources, targets, send, recv):
        self.length, self.level = length, level
        self.copies = [
            remote(sources[way], targets[way], send.at[way], recv.at[way], (upper, lower)[way])
            for way in range(2)
        ]

    def each(self, rank, act):
        for way in range(2):
            mine = self.level if way == 0 else self.length - 1 - self.level

            @pl.when(mine == rank)
            def _(way=way):
                act(self.copies[way])

    def start(self):
        self.each(0, lambda copy: copy.start())

    def wait(self):
        self.each(1, lambda copy: copy.wait_recv())
        self.each(0, lambda copy: copy.wait_send())


def chain_scratch(length, shape):
    return [pltpu.VMEM((length - 1,) + shape, BF16)] * 4 + [
        pltpu.SemaphoreType.DMA((length - 1,))
    ] * 4


def chain_peers():
    count = lax.axis_size("dp")
    block = lax.axis_index("dp")
    lane = lax.axis_index("tensor")
    level = block // 2
    upper = (jnp.where(level < count // 2 - 1, block + 2, block + 2 - count), lane)
    lower = (jnp.where(level > 0, block - 2, block - 2 + count), lane)
    return count // 2, level, upper, lower


def middle_kernel(
    chunk, vec_ref, dn_hbm, x_hbm, attn_hbm, cot_hbm, part_hbm, wo_hbm, ctx_hbm, down_hbm, own_hbm, other_hbm,
    dm_out, dctx_ref, mlp_out, out_own, out_other, sums_ref, edge_ref, far_up, far_down, dm_ref, x_ref, attn_ref,
    cot_ref, mlp_ref, row_sem, out_sem, wo_ref, ctx_ref, edge_own, edge_got, local_sem, x_send, x_recv, z_send, z_recv, acc,
):
    dp = lax.axis_index("dp")
    lane = lax.axis_index("tensor")
    side = lax.rem(dp, 2)
    x_peer = (dp + 1 - 2 * side, lane)
    length, level, upper, lower = chain_peers()
    edge = jnp.where(level < length // 2, length - 1, 0)
    local = [
        pltpu.make_async_copy(source, target, local_sem.at[n])
        for n, (source, target) in enumerate(
            [
                (wo_hbm, wo_ref),
                (ctx_hbm, ctx_ref),
                (own_hbm.at[edge], edge_own),
            ]
        )
    ]
    half = x_ref.shape[0] // 2
    rows_in = [
        [
            pltpu.make_async_copy(
                source.at[pl.ds(n * half, half)], target.at[pl.ds(n * half, half)], row_sem.at[n, k]
            )
            for k, (source, target) in enumerate(
                [
                    (x_hbm, x_ref),
                    (attn_hbm, attn_ref),
                    (dn_hbm, dm_ref),
                    (cot_hbm, cot_ref),
                    (part_hbm, mlp_ref),
                ]
            )
        ]
        for n in range(2)
    ]
    rows_out = [
        [
            pltpu.make_async_copy(
                source.at[pl.ds(n * half, half)], target.at[pl.ds(n * half, half)], out_sem.at[n, k]
            )
            for k, (source, target) in enumerate([(dm_ref, dm_out), (mlp_ref, mlp_out)])
        ]
        for n in range(2)
    ]
    for copy in rows_in[0] + rows_in[1]:
        copy.start()
    for copy in local:
        copy.start()
    greet([x_peer, upper, lower])
    to_x = remote(other_hbm.at[edge], edge_got, x_send, x_recv, x_peer)
    to_x.start()
    first_step = FirstStep(
        length, level, upper, lower, (down_hbm.at[length - 1], down_hbm.at[0]), (far_up, far_down), z_send,
        z_recv,
    )
    first_step.start()
    rows, width = x_ref.shape
    acc[...] = jnp.zeros_like(acc)
    share = 1.0 / lax.axis_size("tensor")

    def fold(values):
        return jnp.sum(values.reshape(chunk // 8, 8, width), axis=0)

    def norm_rows(k):
        at = pl.ds(pl.multiple_of(k * chunk, chunk), chunk)
        values = x_ref[at, :].astype(F32) + attn_ref[at, :].astype(F32) + vec_ref[0:1, :]
        base = share * (values + vec_ref[2:3, :])
        mlp_ref[at, :] = (mlp_ref[at, :].astype(F32) + base).astype(BF16)
        centred = values - jnp.mean(values, axis=-1, keepdims=True)
        scale = lax.rsqrt(jnp.mean(centred * centred, axis=-1, keepdims=True) + EPSILON)
        hat = centred * scale
        grad = dm_ref[at, :].astype(F32)
        acc[0] += fold(grad * hat)
        acc[1] += fold(grad)
        scaled = grad * vec_ref[1:2, :]
        first = jnp.mean(scaled, axis=-1, keepdims=True)
        second = jnp.mean(scaled * hat, axis=-1, keepdims=True)
        cot = cot_ref[at, :].astype(F32)
        d_middle = cot + scale * (scaled - first - hat * second)
        acc[2] += fold(d_middle)
        acc[3] += fold(cot)
        dm_ref[at, :] = d_middle.astype(BF16)

    each = rows // chunk // 2
    for n in range(2):
        for copy in rows_in[n]:
            copy.wait()

        @pl.loop(n * each, (n + 1) * each)
        def _(k):
            norm_rows(k)

        for copy in rows_out[n]:
            copy.start()
    for n in range(4):
        sums_ref[n : n + 1, :] = jnp.sum(acc[n], axis=0, keepdims=True)
    sums_ref[4:8, :] = jnp.zeros((4, width), F32)
    local[0].wait()

    @pl.loop(0, 4)
    def _(k):
        at = pl.ds(pl.multiple_of(k * (rows // 4), rows // 4), rows // 4)
        dctx_ref[at, :] = contract(dm_ref[at, :], wo_ref[...], 1, 1).astype(BF16)

    local[1].wait()
    grad_rows(dm_ref, ctx_ref, out_other, 1 - side)
    grad_rows(dm_ref, ctx_ref, out_own, side)
    local[2].wait()
    for copy in rows_out[0] + rows_out[1]:
        copy.wait()
    to_x.wait()
    edge_ref[...] = (edge_own[...].astype(F32) + edge_got[...].astype(F32)).astype(BF16)
    first_step.wait()


def middle_stage(
    d_normed2, inputs, attn_sum, cotangent, output_bias, gain, down_bias, part, output_weight, context, down,
    up_own, up_other, count, chunk=128,
):
    rows, width = inputs.shape
    heads = context.shape[1]
    vec = jnp.stack([output_bias, gain, down_bias])
    vec = jnp.pad(vec, ((0, 5), (0, 0)))
    half = jax.ShapeDtypeStruct((count // 2, width // count, heads), BF16)
    hbm = pl.BlockSpec(memory_space=pl.ANY)
    dma = pltpu.SemaphoreType.DMA
    low = lambda shape: jax.ShapeDtypeStruct(shape, BF16)
    edge = pltpu.VMEM(up_own.shape[1:], BF16)
    return pl.pallas_call(
        functools.partial(middle_kernel, chunk),
        out_shape=(
            low((rows, width)),
            low((rows, heads)),
            low((rows, width)),
            half,
            half,
            jax.ShapeDtypeStruct((8, width), F32),
            low(up_own.shape[1:]),
            low(down.shape[1:]),
            low(down.shape[1:]),
        ),
        in_specs=[VMEM] + [hbm] * 10,
        out_specs=(hbm, VMEM, hbm) + (VMEM,) * 4 + (hbm,) * 2,
        scratch_shapes=[pltpu.VMEM((rows, width), BF16)] * 5
        + [
            dma((2, 5)),
            dma((2, 2)),
            pltpu.VMEM(output_weight.shape, BF16),
            pltpu.VMEM(context.shape, BF16),
            edge,
            edge,
            dma((3,)),
            dma,
            dma,
            dma((2,)),
            dma((2,)),
            pltpu.VMEM((4, 8, width), F32),
        ],
        compiler_params=pltpu.CompilerParams(
            collective_id=7, has_side_effects=True, vmem_limit_bytes=60 << 20
        ),
        name="middle",
    )(
        vec, d_normed2, inputs, attn_sum, cotangent, part, output_weight, context, down, up_own, up_other,
    )


def query_back_kernel(
    chunks, steps, dq_ref, wq_ref, n1_ref, dkv_ref, wide_ref, wide_up, wide_down, proj_ref, proj_x, dn_ref,
    grad_ref, proj_grad, tot_ref, far_up, far_down, kv_local, part, from_core, summed, from_y, kv_core, kv_sum, kv_x,
    kv_pair, kv_z, kv_up, kv_y, kv_sems, own_ref, other_ref, got_ref, q_send, q_recv, proj_pair, *rest,
):
    chain_bufs, chain_sems, sems = rest[:4], rest[4:8], rest[8:14]
    wide_bufs, wide_sems = rest[14:18], rest[18:22]
    proj_bufs, proj_sems = rest[22:26], rest[26:]
    ts = TensorSum(chunks, part, dn_ref, from_core, summed, from_y, sems)
    block = lax.axis_index("dp")
    lane = lax.axis_index("tensor")
    place = lax.rem(block, SPAN)
    side = lax.rem(place, 2)
    level = place // 2
    levels = SPAN // 2
    x_peer = (block + 1 - 2 * side, lane)
    upper = (jnp.where(level < levels - 1, block + 2, block + 2 - SPAN), lane)
    lower = (jnp.where(level > 0, block - 2, block - 2 + SPAN), lane)
    length, chain_level, chain_upper, chain_lower = chain_peers()
    if length == levels:
        greet([ts.core_peer, ts.y_peer, x_peer, upper, lower])
    else:
        greet([ts.core_peer, ts.y_peer, x_peer, upper, lower, chain_upper, chain_lower])
    chain = Chain(length, chain_level, chain_upper, chain_lower, own_ref, chain_bufs, chain_sems)
    early = (wide_up, wide_down)
    wide = Chain(length, chain_level, chain_upper, chain_lower, wide_ref, wide_bufs, wide_sems, early)
    proj = Chain(length, chain_level, chain_upper, chain_lower, proj_pair, proj_bufs, proj_sems)
    core = lax.rem(lane, 2)
    seq_rows = tot_ref.shape[0]
    half = seq_rows // 2
    mine = pl.ds(pl.multiple_of(core * half, half), half)
    other = pl.ds(pl.multiple_of((1 - core) * half, half), half)

    def kv_copy(source, target, index, device):
        return remote(source, target, kv_sems.at[0, index], kv_sems.at[1, index], device)

    to_core = [
        kv_copy(
            dkv_ref.at[pl.ds(2 * lev, 2), other], kv_core.at[lev], 3 + levels + lev, ts.core_peer
        )
        for lev in range(levels)
    ]
    keep = [
        pltpu.make_async_copy(dkv_ref.at[pl.ds(2 * lev, 2), mine], kv_sum.at[lev], kv_local.at[lev])
        for lev in range(levels)
    ]
    for copy in to_core + keep:
        copy.start()
    proj_pair[...] = (proj_ref[...].astype(F32) + proj_x[...].astype(F32)).astype(BF16)
    proj.start(1)
    wide.start(2)
    grad_levels, rows = own_ref.shape[0], own_ref.shape[1]
    for lev in range(levels):
        to_core[lev].wait_recv()
        keep[lev].wait()
        kv_sum[lev] = (kv_sum[lev].astype(F32) + kv_core[lev].astype(F32)).astype(BF16)

    to_x = kv_copy(kv_sum.at[:, 1 - side], kv_x, 1, x_peer)
    to_x.start()

    @pl.loop(0, chunks)
    def _(k):
        at = ts.span(k)
        part[at, :] = contract(dq_ref[at, :], wq_ref[...], 1, 1).astype(BF16)
        ts.first(k)

        @pl.when(k >= 1)
        def _():
            ts.second(k - 1)

    ts.second(chunks - 1)

    def grad(target, which):
        grad_rows(n1_ref, dq_ref, target, which)

    grad(other_ref, 1 - side)
    q_to_x = remote(other_ref, got_ref, q_send, q_recv, x_peer)
    grad(own_ref, side)
    for s in range(1, length - 1):
        proj.arrive(s)
        proj.start(s + 1)
    to_x.wait_recv()
    q_to_x.start()

    @pl.loop(0, levels)
    def _(lev):
        kv_pair[lev] = (kv_sum[lev, side].astype(F32) + kv_x[lev].astype(F32)).astype(BF16)

    def down(s):
        slot = jnp.maximum(level - levels + s, 0)
        return kv_copy(kv_up.at[s - 1], kv_z.at[s - 1], 1 + s, lower), slot

    for s in range(1, levels):
        copy, slot = down(s)

        @pl.when(level >= levels - s)
        def _(copy=copy, slot=slot, s=s):
            kv_up[s - 1] = kv_pair[slot]
            if s > 1:
                @pl.when(level < levels - 1)
                def _():
                    kv_up[s - 1] = (
                        kv_pair[slot].astype(F32) + kv_z[s - 2].astype(F32)
                    ).astype(BF16)

            copy.start()

        @pl.when((level >= levels - 1 - s) & (level < levels - 1))
        def _(copy=copy):
            copy.wait_recv()

    kv_up[levels - 1] = kv_pair[level]

    @pl.when(level < levels - 1)
    def _():
        kv_up[levels - 1] = (
            kv_pair[level].astype(F32) + kv_z[levels - 2].astype(F32)
        ).astype(BF16)

    to_y = kv_copy(kv_up.at[levels - 1], kv_y, 1 + levels, ts.y_peer)
    to_y.start()
    for s in range(2, steps):
        wide.arrive(s)
        wide.start(s + 1)
    q_to_x.wait_recv()

    @pl.loop(0, grad_levels)
    def _(lev):
        own_ref[lev] = (own_ref[lev].astype(F32) + got_ref[lev].astype(F32)).astype(BF16)

    chain.start(1)
    to_y.wait_recv()
    tot_ref[mine] = (kv_up[levels - 1].astype(F32) + kv_y[...].astype(F32)).astype(BF16)
    back = kv_copy(tot_ref.at[mine], tot_ref.at[mine], 2 + levels, ts.core_peer)
    back.start()
    half_way = chunks // 2
    for s in range(1, length):
        if s == 2:
            @pl.loop(0, half_way)
            def _(k):
                ts.third(k)

        chain.arrive(s)
        if s + 1 < length:
            chain.start(s + 1)

    @pl.loop(half_way, chunks)
    def _(k):
        ts.third(k)

    chain.result(grad_ref)
    proj.arrive(length - 1)
    proj.result(proj_grad)
    wide.arrive(steps)
    far_up[...] = wide.arrived(0, steps)
    far_down[...] = wide.arrived(1, steps)
    chain.drain()
    proj.drain()
    wide.drain(steps)
    q_to_x.wait_send()
    back.wait()
    for copy in to_core:
        copy.wait_send()
    to_x.wait_send()
    to_y.wait_send()
    for s in range(1, levels):
        copy, _slot = down(s)

        @pl.when(level >= levels - s)
        def _(copy=copy):
            copy.wait_send()

    ts.finish(chunks)


def query_back(
    d_queries, query_weight, normed1, parts, wide, wide_up, wide_down, proj, proj_x, count, chunks=4
):
    rows, width = d_queries.shape[0], query_weight.shape[0]
    kv_width = parts.shape[2]
    steps = count // 2 - 2
    levels = SPAN // 2
    shape = (width // count, query_weight.shape[1])
    half = pltpu.VMEM((count // 2,) + shape, BF16)
    piece = (rows // 2, kv_width)
    return pl.pallas_call(
        functools.partial(query_back_kernel, chunks, steps),
        out_shape=(
            jax.ShapeDtypeStruct((rows, width), BF16),
            jax.ShapeDtypeStruct(shape, F32),
            jax.ShapeDtypeStruct(proj.shape[1:], F32),
            jax.ShapeDtypeStruct((rows, kv_width), BF16),
            jax.ShapeDtypeStruct(wide.shape[1:], BF16),
            jax.ShapeDtypeStruct(wide.shape[1:], BF16),
        ),
        in_specs=[VMEM] * 3 + [pl.BlockSpec(memory_space=pl.ANY)] + [VMEM] * 5,
        out_specs=(VMEM,) * 6,
        scratch_shapes=[
            pltpu.SemaphoreType.DMA((levels,)),
        ]
        + sum_scratch(chunks, rows, width)[:4]
        + [
            pltpu.VMEM((levels, 2) + piece, BF16),
            pltpu.VMEM((levels, 2) + piece, BF16),
            pltpu.VMEM((levels,) + piece, BF16),
            pltpu.VMEM((levels,) + piece, BF16),
            pltpu.VMEM((levels - 1,) + piece, BF16),
            pltpu.VMEM((levels,) + piece, BF16),
            pltpu.VMEM(piece, BF16),
            pltpu.SemaphoreType.DMA((2, 3 + 2 * levels)),
            half,
            half,
            half,
            pltpu.SemaphoreType.DMA,
            pltpu.SemaphoreType.DMA,
            pltpu.VMEM(proj.shape, BF16),
        ]
        + chain_scratch(count // 2, shape)
        + [pltpu.SemaphoreType.DMA((chunks,))] * 6
        + chain_scratch(steps, wide.shape[1:])
        + chain_scratch(count // 2, proj.shape[1:]),
        compiler_params=pltpu.CompilerParams(
            collective_id=5, has_side_effects=True, vmem_limit_bytes=63 << 20
        ),
        name="query_back",
    )(d_queries, query_weight, normed1, parts, wide, wide_up, wide_down, proj, proj_x)


def pair_kernel(own_ref, rest_ref, edge_ref, out_ref):
    length = pl.num_programs(0)
    lev = pl.program_id(0)
    at_edge = jnp.where(lax.axis_index("dp") // 2 < length // 2, length - 1, 0)

    @pl.when(lev == at_edge)
    def _():
        out_ref[0] = edge_ref[...]

    @pl.when(lev != at_edge)
    def _():
        out_ref[0] = (own_ref[0].astype(F32) + rest_ref[0].astype(F32)).astype(BF16)


def pair_sum(own, rest, edge):
    level = pl.BlockSpec((1,) + own.shape[1:], lambda k: (k, 0, 0))
    return pl.pallas_call(
        pair_kernel,
        grid=(own.shape[0],),
        out_shape=jax.ShapeDtypeStruct(own.shape, BF16),
        in_specs=[level, level, pl.BlockSpec(edge.shape, lambda k: (0, 0))],
        out_specs=level,
        compiler_params=pltpu.CompilerParams(vmem_limit_bytes=62 << 20),
        name="pair_sum",
    )(own, rest, edge)


def norm_back_kernel(
    dkv_ref, wkv_ref, dn_ref, x_ref, dm_ref, gain_ref, pass_in, grad_x, sums_ref, pass_out, acc, acc_kv
):
    k = pl.program_id(0)
    pass_out[...] = pass_in[...]

    @pl.when(k == 0)
    def _():
        acc[...] = jnp.zeros_like(acc)
        acc_kv[...] = jnp.zeros_like(acc_kv)

    chunk, width = x_ref.shape

    def fold(values):
        return jnp.sum(values.reshape(chunk // 8, 8, values.shape[1]), axis=0)

    values = x_ref[...].astype(F32)
    centred = values - jnp.mean(values, axis=-1, keepdims=True)
    scale = lax.rsqrt(jnp.mean(centred * centred, axis=-1, keepdims=True) + EPSILON)
    hat = centred * scale
    grad = dn_ref[...].astype(F32) + contract(dkv_ref[...], wkv_ref[...], 1, 1)
    acc[0] += fold(grad * hat)
    acc[1] += fold(grad)
    acc_kv[...] += fold(dkv_ref[...].astype(F32))
    scaled = grad * gain_ref[...]
    first = jnp.mean(scaled, axis=-1, keepdims=True)
    second = jnp.mean(scaled * hat, axis=-1, keepdims=True)
    grad_x[...] = dm_ref[...].astype(F32) + scale * (scaled - first - hat * second)

    @pl.when(k == pl.num_programs(0) - 1)
    def _():
        sums_ref[...] = jnp.zeros_like(sums_ref)
        sums_ref[0:1, :] = jnp.sum(acc[0], axis=0, keepdims=True)
        sums_ref[1:2, :] = jnp.sum(acc[1], axis=0, keepdims=True)
        sums_ref[2:3, 0 : acc_kv.shape[1]] = jnp.sum(acc_kv[...], axis=0, keepdims=True)


def norm_back(d_keyval, keyval_weight, d_normed1, inputs, d_middle, gain, passed, chunk=256):
    rows, width = inputs.shape
    kv_width = d_keyval.shape[1]
    row = lambda cols: pl.BlockSpec((chunk, cols), lambda k: (k, 0))
    fixed = lambda shape: pl.BlockSpec(shape, lambda k: (0, 0))
    return pl.pallas_call(
        norm_back_kernel,
        grid=(rows // chunk,),
        out_shape=(
            jax.ShapeDtypeStruct((rows, width), F32),
            jax.ShapeDtypeStruct((8, width), F32),
            jax.ShapeDtypeStruct(passed.shape, BF16),
        ),
        in_specs=[
            row(kv_width),
            fixed((width, kv_width)),
            row(width),
            row(width),
            row(width),
            fixed((1, width)),
            row(width),
        ],
        out_specs=(row(width), fixed((8, width)), row(width)),
        scratch_shapes=[pltpu.VMEM((2, 8, width), F32), pltpu.VMEM((8, kv_width), F32)],
        compiler_params=pltpu.CompilerParams(vmem_limit_bytes=62 << 20),
        name="norm_back",
    )(d_keyval, keyval_weight, d_normed1, inputs, d_middle, gain.reshape(1, width), passed)


def finish_kernel(
    dkv_ref, vec_in, far_up, far_down, down_ref, n1_hbm, wide_ref, grad_ref, vec_ref, up_ref, down_out, n1_ref,
    n1_sem, g_send, g_recv, ends_ref, local_sem, d_send, d_recv, down_low, down_got, up_out, up_in, up_send, up_recv, own_ref, other_ref, got_ref, x_send, x_recv, own_vec, low_vec, slots, send, recv, *chain_refs,
):
    block = lax.axis_index("dp")
    lane = lax.axis_index("tensor")
    count = lax.axis_size("dp")
    side = lax.rem(block, 2)
    pairs = count // 2
    others = [(lax.rem(block + 2 * k, count), lane) for k in range(1, pairs)]
    x_peer = (block + 1 - 2 * side, lane)
    length, level, upper, lower = chain_peers()
    local = [
        pltpu.make_async_copy(
            wide_ref.at[jnp.clip(level + k, 0, length - 1)], ends_ref.at[n], local_sem.at[n]
        )
        for n, k in enumerate((0, 1, -1))
    ]
    take = pltpu.make_async_copy(n1_hbm, n1_ref, n1_sem)
    take.start()
    for copy in local:
        copy.start()
    core = lax.rem(lane, 2)
    core_peer = (block, lane + 1 - 2 * core)
    half_kv = dkv_ref.shape[1] // 2
    mine = pl.ds(pl.multiple_of(core * half_kv, half_kv), half_kv)
    greet([core_peer, x_peer] + others)
    low_vec[0] = vec_in[...].astype(BF16)
    to_pair = remote(low_vec.at[0], slots.at[0], send.at[0], recv.at[0], x_peer)
    to_pair.start()

    def last(way):
        return remote(
            up_out.at[way], up_in.at[way], up_send.at[way], up_recv.at[way], (upper, lower)[way]
        )

    ranks = (level, length - 1 - level)
    for copy in local:
        copy.wait()
    for way, far in enumerate((far_up, far_down)):
        @pl.when(ranks[way] < length - 1)
        def _(way=way, far=far):
            up_out[way] = ends_ref[1 + way]

            @pl.when(ranks[way] >= 1)
            def _():
                up_out[way] = (ends_ref[1 + way].astype(F32) + far[...].astype(F32)).astype(BF16)

            last(way).start()

    take.wait()
    kv_half = dkv_ref.at[:, mine]
    grad_rows(n1_ref, kv_half, other_ref, 1 - side)
    to_x = remote(other_ref, got_ref, x_send, x_recv, x_peer)
    to_x.start()
    half_rows, half_cols = down_low.shape
    down_mine = pl.ds(pl.multiple_of(side * half_rows, half_rows), half_rows)
    down_theirs = pl.ds(pl.multiple_of((1 - side) * half_rows, half_rows), half_rows)
    down_low[...] = down_ref[down_theirs].astype(BF16)
    d_to_x = remote(down_low, down_got, d_send, d_recv, x_peer)
    to_pair.wait()
    own_vec[...] = vec_in[...] + slots[0].astype(F32)
    low_vec[1] = own_vec[...].astype(BF16)
    copies = []
    for k in range(1, pairs):
        copy = remote(low_vec.at[1], slots.at[k], send.at[k], recv.at[k], others[k - 1])
        copy.start()
        copies.append(copy)
    grad_rows(n1_ref, kv_half, own_ref, side)
    chain = Chain(length, level, upper, lower, own_ref, chain_refs[:4], chain_refs[4:8])
    to_x.wait_recv()
    own_ref[...] = (own_ref[...].astype(F32) + got_ref[...].astype(F32)).astype(BF16)
    chain.start(1)
    d_to_x.start()
    for s in range(1, length):
        chain.arrive(s)
        if s + 1 < length:
            chain.start(s + 1)
    chain.result(grad_ref.at[:, mine])
    to_core = remote(grad_ref.at[:, mine], grad_ref.at[:, mine], g_send, g_recv, core_peer)
    to_core.start()
    d_to_x.wait()
    first = pl.ds(pl.multiple_of(side * half_cols, half_cols), half_cols)
    second = pl.ds(pl.multiple_of((1 - side) * half_cols, half_cols), half_cols)
    down_out[:, first] = down_ref[down_mine]
    down_out[:, second] = down_got[...].astype(F32)
    total = own_vec[...]
    for k in range(1, pairs):
        copies[k - 1].wait()
        total = total + slots[k].astype(F32)
    vec_ref[...] = total
    up_ref[...] = ends_ref[0].astype(F32)
    for way in range(2):
        @pl.when(ranks[way] >= 1)
        def _(way=way):
            last(way).wait_recv()
            up_ref[...] += up_in[way].astype(F32)

        @pl.when(ranks[way] < length - 1)
        def _(way=way):
            last(way).wait_send()

    chain.drain()
    to_x.wait_send()
    to_core.wait()


def finish(normed1, d_keyval, rows_of_vectors, vectors, wide, far_up, far_down, down, count):
    width = normed1.shape[1]
    flat = jnp.concatenate(vectors)
    lines = -(-flat.shape[0] // width)
    flat = jnp.pad(flat, (0, lines * width - flat.shape[0])).reshape(lines, width)
    packed = jnp.concatenate(rows_of_vectors + [flat], axis=0)
    height = -(-packed.shape[0] // 8) * 8
    packed = jnp.pad(packed, ((0, height - packed.shape[0]), (0, 0)))
    shape = (width // count, d_keyval.shape[1])
    part = (shape[0], shape[1] // 2)
    half = pltpu.VMEM((count // 2,) + part, BF16)
    dma = pltpu.SemaphoreType.DMA
    two = pltpu.VMEM((2,) + far_up.shape, BF16)
    return pl.pallas_call(
        finish_kernel,
        out_shape=(
            jax.ShapeDtypeStruct(shape, F32),
            jax.ShapeDtypeStruct((height, width), F32),
            jax.ShapeDtypeStruct(far_up.shape, F32),
            jax.ShapeDtypeStruct((down.shape[0] // 2, 2 * down.shape[1]), F32),
        ),
        in_specs=[VMEM] * 5 + [pl.BlockSpec(memory_space=pl.ANY)] * 2,
        out_specs=(VMEM,) * 4,
        scratch_shapes=[
            pltpu.VMEM(normed1.shape, BF16),
            dma,
            dma,
            dma,
            pltpu.VMEM((3,) + far_up.shape, BF16),
            dma((3,)),
            dma,
            dma,
            pltpu.VMEM((down.shape[0] // 2, down.shape[1]), BF16),
            pltpu.VMEM((down.shape[0] // 2, down.shape[1]), BF16),
        ]
        + [two, two, dma((2,)), dma((2,)), half, half, half, dma, dma]
        + [
            pltpu.VMEM((height, width), F32),
            pltpu.VMEM((2, height, width), BF16),
            pltpu.VMEM((count // 2, height, width), BF16),
            dma((count // 2,)),
            dma((count // 2,)),
        ]
        + chain_scratch(count // 2, part),
        compiler_params=pltpu.CompilerParams(
            collective_id=2, has_side_effects=True, vmem_limit_bytes=62 << 20
        ),
        name="finish",
    )(d_keyval, packed, far_up, far_down, down, normed1, wide)


def front_kernel(
    block, chunks, q_ref, own_kv, cot_hbm, wo_ref, wd_hbm, kv_ref, ctx_ref, lse_ref, sum_ref, g_ref, far_ref,
    cot_ref, wd_ref, local_sem, x_send, x_recv, z_send, z_recv, s_send, s_recv, f_send, f_recv, acc, peak, total,
    part, from_core, summed, from_y, *sems,
):
    ts = TensorSum(chunks, part, sum_ref, from_core, summed, from_y, sems)
    dp = lax.axis_index("dp")
    lane = lax.axis_index("tensor")
    place = lax.rem(dp, SPAN)
    side = lax.rem(place, 2)
    level = place // 2
    levels = SPAN // 2
    core = lax.rem(lane, 2)
    y_lane = lax.rem(lane + 2, 4)
    core_peer, y_peer = ts.core_peer, ts.y_peer
    x_peer = (dp + 1 - 2 * side, lane)
    upper = (jnp.where(level < levels - 1, dp + 2, dp + 2 - SPAN), lane)
    lower = (jnp.where(level > 0, dp - 2, dp - 2 + SPAN), lane)
    seq_rows = own_kv.shape[0]
    piece = seq_rows // 4
    head = kv_ref.shape[2] // 2
    heads = q_ref.shape[1] // head
    parts = seq_rows // block

    def rows_of(which):
        return pl.ds(pl.multiple_of(which * piece, piece), piece)

    local = [
        pltpu.make_async_copy(own_kv, kv_ref.at[place], local_sem.at[0]),
        pltpu.make_async_copy(cot_hbm, cot_ref, local_sem.at[1]),
        pltpu.make_async_copy(wd_hbm, wd_ref, local_sem.at[2]),
    ]
    local[0].start()
    greet([core_peer, y_peer, x_peer, upper, lower])
    to_x = remote(own_kv.at[rows_of(lane)], kv_ref.at[place, rows_of(lane)], x_send, x_recv, x_peer)
    to_x.start()
    far_pieces = f_send.shape[1]
    far_step = cot_hbm.shape[0] // (2 * far_pieces)

    def far(kind, k):
        start = pl.multiple_of((core * far_pieces + k) * far_step, far_step)
        source = cot_hbm if kind == 0 else far_ref
        return remote(
            source.at[pl.ds(start, far_step)], far_ref.at[pl.ds(start, far_step)], f_send.at[kind, k],
            f_recv.at[kind, k], x_peer if kind == 0 else core_peer,
        )

    def share(s, kind):
        at = rows_of(y_lane if kind == 2 else lane)
        ref = kv_ref.at[pl.ds(2 * (level - s), 2), at]
        return remote(
            ref, ref, s_send.at[s, kind], s_recv.at[s, kind], y_peer if kind == 0 else core_peer
        )

    def share_pair(kind):
        ref = kv_ref.at[place + 1 - 2 * side, rows_of(y_lane if kind == 2 else lane)]
        return remote(
            ref, ref, s_send.at[0, kind], s_recv.at[0, kind], y_peer if kind == 0 else core_peer
        )

    def up(s):
        ref = kv_ref.at[pl.ds(2 * (level - s), 2), rows_of(lane)]
        return remote(ref, ref, z_send.at[s], z_recv.at[s], upper)

    def from_below(s):
        ref = kv_ref.at[pl.ds(2 * (level - 1 - s), 2), rows_of(lane)]
        return remote(ref, ref, z_send.at[s], z_recv.at[s], upper)

    def forward(s):
        from_below(s - 1).wait_recv()

        @pl.when((s < levels - 1) & (level < levels - 1))
        def _():
            up(s).start()

        share(s, 0).start()
        share(s, 1).start()

    def score(i, h, at_block, at_row, diagonal):
        keys = kv_ref[at_block, pl.ds(at_row, block), 0:head]
        query = q_ref[i * block : (i + 1) * block, h * head : (h + 1) * head]
        scores = contract(keys, query, 1, 1)
        if diagonal:
            key_at = lax.broadcasted_iota(jnp.int32, scores.shape, 0)
            query_at = lax.broadcasted_iota(jnp.int32, scores.shape, 1)
            scores = jnp.where(key_at <= query_at, scores, NEG_LARGE)
        return scores

    def soften(i, h, scores):
        old = peak[i, h]
        new = jnp.maximum(old, jnp.max(scores, axis=0, keepdims=True))
        probs = jnp.exp(scores - new)
        fade = jnp.exp(old - new)
        total[i, h] = total[i, h] * fade + jnp.sum(probs, axis=0, keepdims=True)
        peak[i, h] = new
        return probs.astype(BF16), fade

    def weigh(i, h, at_block, at_row, probs, fade):
        values = kv_ref[at_block, pl.ds(at_row, block), head : 2 * head]
        acc[i, h] = acc[i, h] * fade + contract(values, probs, 0, 0)

    def attend(i, pieces):
        items = [(h, piece) for piece in pieces for h in range(heads)]
        scores = score(i, items[0][0], *items[0][1])
        waiting = None
        for n, (h, (at_block, at_row, _diagonal)) in enumerate(items):
            following = None
            if n + 1 < len(items):
                following = score(i, items[n + 1][0], *items[n + 1][1])
            probs, fade = soften(i, h, scores)
            if waiting is not None:
                weigh(i, *waiting)
            waiting = (h, at_block, at_row, probs, fade)
            scores = following
        weigh(i, *waiting)

    def attend_level(i, s):
        @pl.loop(0, 2)
        def _(b):
            attend(i, [(2 * (level - s) + b, n * block, False) for n in range(parts)])

    peak[...] = jnp.full_like(peak, NEG_LARGE)
    total[...] = jnp.zeros_like(total)
    acc[...] = jnp.zeros_like(acc)
    local[0].wait()
    for copy in local[1:]:
        copy.start()
    for k in range(far_pieces):
        far(0, k).start()
    to_x.wait_recv()

    @pl.when(level < levels - 1)
    def _():
        up(0).start()

    share_pair(0).start()
    share_pair(1).start()
    for i in range(parts):
        attend(i, [(place, n * block, n == i) for n in range(i + 1)])

    @pl.when(level >= 1)
    def _():
        forward(1)

    share_pair(0).wait_recv()
    share_pair(2).start()
    share_pair(1).wait_recv()
    share_pair(2).wait_recv()

    @pl.when(side == 1)
    def _():
        for i in range(parts):
            attend(i, [(place - 1, n * block, False) for n in range(parts)])

    def complete(i):
        span = slice(i * block, (i + 1) * block)
        for h in range(heads):
            context = acc[i, h] / total[i, h]
            ctx_ref[span, h * head : (h + 1) * head] = context.T.astype(BF16)
            lse_ref[h : h + 1, span] = peak[i, h] + jnp.log(total[i, h])
        each = chunks // parts
        first = i * each

        @pl.loop(first, first + each)
        def _(k):
            at = ts.span(k)
            part[at, :] = jnp.dot(
                ctx_ref[at, :], wo_ref[...], preferred_element_type=F32
            ).astype(BF16)
            ts.first(k)

        @pl.loop(first, first + each)
        def _(k):
            ts.second(k)

    @pl.loop(1, level + 1)
    def _(s):
        @pl.when(s < level)
        def _():
            forward(s + 1)

        share(s, 0).wait_recv()
        share(s, 2).start()
        share(s, 1).wait_recv()
        share(s, 2).wait_recv()
        attend_level(0, s)

    complete(0)
    for i in range(1, parts):
        @pl.loop(1, level + 1)
        def _(s, i=i):
            attend_level(i, s)

        complete(i)

    for k in range(far_pieces):
        far(0, k).wait_recv()
        far(1, k).start()
    ready = chunks - chunks // parts

    @pl.loop(0, ready)
    def _(k):
        ts.third(k)

    for copy in local[1:]:
        copy.wait()
    tile = g_ref.shape[1] // 8

    @pl.loop(0, 8)
    def _(j):
        cols = pl.ds(pl.multiple_of(j * tile, tile), tile)
        g_ref[:, cols] = contract(cot_ref[...], wd_ref[cols, :], 1, 1).astype(BF16)

    @pl.loop(ready, chunks)
    def _(k):
        ts.third(k)

    to_x.wait_send()

    @pl.when(level < levels - 1)
    def _():
        up(0).wait_send()

    for kind in range(3):
        share_pair(kind).wait_send()

    @pl.loop(1, level + 1)
    def _(s):
        for kind in range(3):
            share(s, kind).wait_send()

        @pl.when((s < levels - 1) & (level < levels - 1))
        def _():
            up(s).wait_send()

    for k in range(far_pieces):
        far(0, k).wait_send()
        far(1, k).wait()
    ts.finish(chunks)


def front(queries, keyval, cotangent, output_weight, down_weight, block=512, chunks=8):
    rows, width = queries.shape
    wide = output_weight.shape[1]
    hidden = down_weight.shape[0]
    head = keyval.shape[1] // 2
    heads = width // head
    levels = SPAN // 2
    dma = pltpu.SemaphoreType.DMA
    hbm = pl.BlockSpec(memory_space=pl.ANY)
    stat = pltpu.VMEM((rows // block, heads, 1, block), F32)
    return pl.pallas_call(
        functools.partial(front_kernel, block, chunks),
        out_shape=(
            jax.ShapeDtypeStruct((SPAN,) + keyval.shape, BF16),
            jax.ShapeDtypeStruct((rows, width), BF16),
            jax.ShapeDtypeStruct((heads, rows), F32),
            jax.ShapeDtypeStruct((rows, wide), BF16),
            jax.ShapeDtypeStruct((rows, hidden), BF16),
            jax.ShapeDtypeStruct(cotangent.shape, BF16),
        ),
        in_specs=[VMEM, VMEM, hbm, VMEM, hbm],
        out_specs=(VMEM,) * 5 + (hbm,),
        scratch_shapes=[
            pltpu.VMEM(cotangent.shape, BF16),
            pltpu.VMEM(down_weight.shape, BF16),
            dma((3,)),
            dma,
            dma,
            dma((levels - 1,)),
            dma((levels - 1,)),
            dma((levels, 3)),
            dma((levels, 3)),
            dma((2, 4)),
            dma((2, 4)),
            pltpu.VMEM((rows // block, heads, head, block), F32),
            stat,
            stat,
        ]
        + sum_scratch(chunks, rows, wide),
        compiler_params=pltpu.CompilerParams(
            collective_id=1, has_side_effects=True, vmem_limit_bytes=60 << 20
        ),
        name="front",
    )(queries, keyval, cotangent, output_weight, down_weight)


def attend_back_kernel(
    block, chunks, q_ref, do_ref, ctx_ref, lse_ref, far_up, far_down, kv_hbm, pair_hbm, mlp_hbm, sent_ref,
    edge_ref, proj_ref, dq_ref, grad_ref, dkv_out, sum_out, got_ref, wide_up, wide_down, proj_got, kv_ref, pair_ref,
    mlp_ref, dkv_ref, out_ref, in_sem, dkv_sem, sum_sem, dq_acc, dkv_acc, delta, x_send, x_recv, z_send, z_recv,
    from_core, summed, from_y, *rest,
):
    sems, chain_refs = rest[:6], rest[6:]
    rows = q_ref.shape[0]
    head = kv_ref.shape[1] // 2
    heads = q_ref.shape[1] // head
    place = lax.rem(lax.axis_index("dp"), SPAN)
    side = lax.rem(lax.axis_index("dp"), 2)
    x_peer = (lax.axis_index("dp") + 1 - 2 * side, lax.axis_index("tensor"))
    ts = TensorSum(chunks, mlp_ref, out_ref, from_core, summed, from_y, sems)
    length, level, upper, lower = chain_peers()
    early = (far_up, far_down)
    chain = Chain(length, level, upper, lower, pair_ref, chain_refs[:4], chain_refs[4:], early)
    depth = 2 * rows
    local = [
        pltpu.make_async_copy(mlp_hbm, mlp_ref, in_sem.at[0]),
        pltpu.make_async_copy(pair_hbm, pair_ref, in_sem.at[1]),
    ] + [
        pltpu.make_async_copy(
            kv_hbm.at[pl.ds(n * depth, depth)], kv_ref.at[pl.ds(n * depth, depth)], in_sem.at[2 + n]
        )
        for n in range(SPAN // 2)
    ]
    dkv_copies = [
        pltpu.make_async_copy(
            dkv_ref.at[pl.ds(2 * n, 2)], dkv_out.at[pl.ds(2 * n, 2)], dkv_sem.at[n]
        )
        for n in range(SPAN // 2)
    ]
    sum_copy = pltpu.make_async_copy(out_ref, sum_out, sum_sem)
    for copy in local:
        copy.start()
    greet([ts.core_peer, ts.y_peer, x_peer, upper, lower])
    left = pl.ds(jnp.where(level < length // 2, 0, 1), length - 1)
    proj_to_x = remote(proj_ref, proj_got, x_send.at[1], x_recv.at[1], x_peer)
    proj_to_x.start()
    to_x = remote(sent_ref.at[left], got_ref.at[left], x_send.at[0], x_recv.at[0], x_peer)
    to_x.start()

    local[0].wait()

    @pl.loop(0, chunks)
    def _(k):
        ts.first(k)

    local[1].wait()
    chain.start(2)
    wide_step = FirstStep(
        length, level, upper, lower, (edge_ref, edge_ref), (wide_up, wide_down), z_send, z_recv
    )
    wide_step.start()
    levels = SPAN // 2
    parts = 2 * rows // block
    per_slot = -(-(length - 2) // (levels - 1))
    done = 1
    for target in range(levels):
        local[2 + target].wait()
        dkv_acc[...] = jnp.zeros_like(dkv_acc)
        for i in range(rows // block):
            span = slice(i * block, (i + 1) * block)
            if target == 0:
                for h in range(heads):
                    cols = slice(h * head, (h + 1) * head)
                    product = do_ref[span, cols].astype(F32) * ctx_ref[span, cols].astype(F32)
                    delta[h : h + 1, span] = jnp.sum(product.T, axis=0, keepdims=True)
                dq_acc[i] = jnp.zeros_like(dq_acc[i])

            def step(j, diagonal, span=span, i=i):
                at = pl.ds(pl.multiple_of(j * block, block), block)
                kv_at = pl.ds(pl.multiple_of((target * parts + j) * block, block), block)
                keys = kv_ref[kv_at, 0:head]
                values = kv_ref[kv_at, head : 2 * head]
                d_keys = jnp.zeros((block, head), F32)
                d_values = jnp.zeros((block, head), F32)

                def begin(h):
                    cols = slice(h * head, (h + 1) * head)
                    scores = contract(keys, q_ref[span, cols], 1, 1)
                    if diagonal:
                        key_at = lax.broadcasted_iota(jnp.int32, scores.shape, 0)
                        query_at = lax.broadcasted_iota(jnp.int32, scores.shape, 1)
                        scores = jnp.where(key_at <= query_at, scores, NEG_LARGE)
                    return scores, contract(values, do_ref[span, cols], 1, 1)

                begun = begin(0)
                for h in range(heads):
                    cols = slice(h * head, (h + 1) * head)
                    scores, d_probs = begun
                    if h + 1 < heads:
                        begun = begin(h + 1)
                    probs = jnp.exp(scores - lse_ref[h : h + 1, span])
                    d_scores = (probs * (d_probs - delta[h : h + 1, span])).astype(BF16)
                    d_values += contract(probs.astype(BF16), do_ref[span, cols], 1, 0)
                    d_keys += contract(d_scores, q_ref[span, cols], 1, 0)
                    dq_acc[i, h] += contract(keys, d_scores, 0, 0)
                dkv_acc[at, 0:head] += d_keys
                dkv_acc[at, head : 2 * head] += d_values

            full = (place * rows + i * block) // block - target * parts

            @pl.loop(0, jnp.clip(full, 0, parts))
            def _(j):
                step(j, False)

            @pl.when((full >= 0) & (full < parts))
            def _():
                step(full, True)

            if target == 0 and i == 0:
                @pl.loop(0, chunks)
                def _(k):
                    ts.second(k)

        for b in range(2):
            dkv_ref[2 * target + b] = dkv_acc[b * rows : (b + 1) * rows].astype(BF16)
        dkv_copies[target].start()
        if target < levels - 1:
            for _ in range(per_slot):
                if done < length - 1:
                    done += 1
                    chain.arrive(done)
                    if done < length - 1:
                        chain.start(done + 1)
                    else:
                        chain.result(grad_ref)
        if target == levels - 2:
            @pl.loop(0, chunks)
            def _(k):
                ts.third(k)

            ts.finish(chunks)
            sum_copy.start()

    for i in range(rows // block):
        span = slice(i * block, (i + 1) * block)
        for h in range(heads):
            dq_ref[span, h * head : (h + 1) * head] = (
                (dq_acc[i, h] * head**-0.5).T.astype(BF16)
            )
    chain.drain()
    wide_step.wait()
    for copy in dkv_copies + [sum_copy]:
        copy.wait()
    to_x.wait()
    proj_to_x.wait()


def attend_back(
    queries, keyval, d_context, context, lse, pair, far_up, far_down, mlp_part, sent, edge, proj, block=512, chunks=4
):
    rows, width = queries.shape
    head = keyval.shape[1] // 2
    heads = width // head
    hbm = pl.BlockSpec(memory_space=pl.ANY)
    dma = pltpu.SemaphoreType.DMA
    low = lambda shape: jax.ShapeDtypeStruct(shape, BF16)
    return pl.pallas_call(
        functools.partial(attend_back_kernel, block, chunks),
        out_shape=(
            low((rows, width)),
            jax.ShapeDtypeStruct(pair.shape[1:], F32),
            low((SPAN, rows, 2 * head)),
            low(mlp_part.shape),
            low(sent.shape),
            low(edge.shape),
            low(edge.shape),
            low(proj.shape),
        ),
        in_specs=[VMEM] * 6 + [hbm] * 6,
        out_specs=(VMEM,) * 2 + (hbm,) * 6,
        scratch_shapes=[
            pltpu.VMEM(keyval.shape, BF16),
            pltpu.VMEM(pair.shape, BF16),
            pltpu.VMEM(mlp_part.shape, BF16),
            pltpu.VMEM((SPAN, rows, 2 * head), BF16),
            pltpu.VMEM(mlp_part.shape, BF16),
            dma((2 + SPAN // 2,)),
            dma((SPAN // 2,)),
            dma,
            pltpu.VMEM((rows // block, heads, head, block), F32),
            pltpu.VMEM((2 * rows, 2 * head), F32),
            pltpu.VMEM((heads, rows), F32),
            dma((2,)),
            dma((2,)),
            dma((2,)),
            dma((2,)),
        ]
        + sum_scratch(chunks, *mlp_part.shape)[1:]
        + chain_scratch(pair.shape[0] - 1, pair.shape[1:]),
        compiler_params=pltpu.CompilerParams(
            collective_id=6, has_side_effects=True, vmem_limit_bytes=63 << 20
        ),
        name="attend_back",
    )(
        queries, d_context, context, lse, far_up, far_down, keyval, pair, mlp_part, sent, edge, proj
    )


def layer_norm(values, norm_gain, norm_bias):
    average = jnp.mean(values, axis=-1, keepdims=True)
    centred = values - average
    variance = jnp.mean(centred * centred, axis=-1, keepdims=True)
    return centred * lax.rsqrt(variance + EPSILON) * norm_gain + norm_bias


def per_device(
    inputs,
    first_gain,
    first_bias,
    query_weight,
    query_bias,
    keyval_weight,
    value_bias,
    output_weight,
    output_bias,
    second_gain,
    second_bias,
    up_weight,
    up_bias,
    down_weight,
    down_bias,
    cotangent,
):
    count = lax.axis_size("dp")
    head_size = value_bias.shape[0]
    score_scale = head_size ** (-0.5)
    x_full = inputs.astype(F32)
    normed1 = layer_norm(x_full, first_gain, first_bias).astype(BF16)
    query_pre = jnp.dot(normed1, query_weight, preferred_element_type=F32) + query_bias
    queries = (query_pre * score_scale).astype(BF16)
    kv_bias = jnp.concatenate([jnp.zeros_like(value_bias), value_bias])
    keyval = (jnp.dot(normed1, keyval_weight, preferred_element_type=F32) + kv_bias).astype(BF16)
    keyval_all, context_low, lse, attn_sum, d_activ, far_cotangent = front(
        queries, keyval, cotangent, output_weight, down_weight
    )
    keyval_all = keyval_all.reshape(-1, keyval.shape[1])
    normed2, activ, d_pre, d_up_bias = hidden_stage(
        inputs, attn_sum, d_activ, up_weight, up_bias, output_bias, second_gain, second_bias
    )
    d_up_bias = d_up_bias[0]
    d_normed2, up_own, up_other, pair_down, out_part = hidden_back(
        d_pre, up_weight, normed2, activ, cotangent, far_cotangent, down_weight, count
    )
    d_middle, d_context, out_part, proj_own, proj_other, row_sums, edge, far_up, far_down = middle_stage(
        d_normed2,
        inputs,
        attn_sum,
        cotangent,
        output_bias,
        second_gain,
        down_bias,
        out_part,
        output_weight,
        context_low,
        pair_down,
        up_own,
        up_other,
        count,
    )
    d_queries, half_down, d_kv_parts, layer_out, rest, wide_up, wide_down, proj_got = attend_back(
        queries,
        keyval_all,
        d_context,
        context_low,
        lse,
        pair_down,
        far_up,
        far_down,
        out_part,
        up_other,
        edge,
        proj_other,
    )
    pair_up = pair_sum(up_own, rest, edge)
    d_query_bias = jnp.sum(d_queries.astype(F32), axis=0)
    d_normed1, sent_query, sent_proj, d_keyval, far_up, far_down = query_back(
        d_queries,
        query_weight,
        normed1,
        d_kv_parts,
        pair_up,
        wide_up,
        wide_down,
        proj_own,
        proj_got,
        count,
    )
    grad_inputs, first_sums, layer_out = norm_back(
        d_keyval, keyval_weight, d_normed1, inputs, d_middle, first_gain, layer_out
    )
    sent_kv, sums, sent_up, sent_down = finish(
        normed1,
        d_keyval,
        [first_sums[:3], row_sums[:4]],
        [d_up_bias, d_query_bias],
        pair_up,
        far_up,
        far_down,
        half_down,
        count,
    )
    local = query_weight.shape[1]
    hidden = d_up_bias.shape[0]
    flat = sums[7:].reshape(-1)
    return (
        layer_out,
        grad_inputs,
        sums[0],
        sums[1],
        sent_query,
        flat[hidden : hidden + local],
        sent_kv,
        sums[2, head_size : 2 * head_size],
        sent_proj.T,
        sums[5],
        sums[3],
        sums[4],
        sent_up,
        flat[:hidden],
        sent_down.T,
        sums[6],
    )


def solution(mesh):
    in_specs = (
        P("dp", None),
        P(),
        P(),
        P(None, "tensor"),
        P("tensor"),
        P(),
        P(),
        P("tensor", None),
        P(),
        P(),
        P(),
        P(None, "tensor"),
        P("tensor"),
        P("tensor", None),
        P(),
        P("dp", None),
    )
    out_specs = (
        P("dp", None),
        P("dp", None),
        P(),
        P(),
        P("dp", "tensor"),
        P("tensor"),
        P("dp", None),
        P(),
        P("tensor", "dp"),
        P(),
        P(),
        P(),
        P("dp", "tensor"),
        P("tensor"),
        P("tensor", "dp"),
        P(),
    )
    return jax.shard_map(
        per_device, mesh=mesh, in_specs=in_specs, out_specs=out_specs, check_vma=False
    )
```
